512 devices in a mesh: rows: 32 (over z_lo, y), cols: 16 (over x, z_hi, core).
Axes of the slice: x: 4, y: 8, z: 8 (z_hi: 2, z_lo: 4; z = z_hi * 4 + z_lo), core: 2. Of those that a mesh axis runs over, the one named last changes fastest.
Arguments:
- series: float32 [2097152], P(('rows', 'cols')), may hold values from -6 to 6
- tile_list: int32 [3, 2048], P(None, 'rows'), may hold values from 0 to 4094, as said below
Outputs:
- profile: float32 [2097152], P(('rows', 'cols'))
The draws below stay inside these ranges and needn't reach their ends.
Inputs may be any that keep to these rules, and one draw needn't show every extreme that they name: The columns of tile_list lying on one index of rows list 64 distinct tiles (row block, offset) of that row group: the row block lies in the group, the offset is below 8, and row block plus offset is at most 4094. Every group but the last lists a tile whose column block lies in the next group; the last group lists the tile of row block 4094 and offset 0. The third row is an index of cols; in each group no index owns more than 8 tiles and one owns exactly 8.
All inputs are finite; a program needn't handle non-finite values.
Results may differ from the reference program's by a relative error of at most 0.0001.
Values sent between devices are 32-bit elements; how exact they have to be, the bound alone decides.
A program may use at most 64 MiB of HBM per device.

```python
import math
import jax
import jax.numpy as jnp
from jax import lax

M = 256
B = 512
BPR = 128
DB = 8
CAP = 8
TPR = 64
TILES = 2048
NB = 4096
SAMPLES = 2097152
EXCL = 64
N_ROWS = 32
N_COLS = 16


def draw_tile_list(key, part):
    key_rank, key_force, key_owner, key_place = jax.random.split(key, 4)
    total = BPR * DB
    cand = jnp.arange(total, dtype=jnp.int32)
    local_block = cand // DB
    offset = cand % DB
    groups = jnp.arange(N_ROWS, dtype=jnp.int32)[:, None]
    valid = groups * BPR + local_block[None, :] + offset[None, :] <= NB - 2
    ranks = jax.vmap(lambda k: jax.random.permutation(k, total))(jax.random.split(key_rank, N_ROWS)).astype(jnp.int32)
    force_off = jax.random.randint(key_force, (N_ROWS, 1), 1, DB).astype(jnp.int32)
    forced = (local_block[None, :] == BPR - 1) & (offset[None, :] == force_off) & valid
    forced_last = (groups == N_ROWS - 1) & (local_block[None, :] == BPR - 2) & (offset[None, :] == 0)
    forced = forced | forced_last
    score = ranks + jnp.where(valid, 0, 2 * total) - jnp.where(forced, 2 * total, 0)
    chosen = jnp.argsort(score, axis=1, stable=True)[:, :TPR].astype(jnp.int32)
    sel_block = groups * BPR + chosen // DB
    sel_off = chosen % DB
    position = jnp.arange(TPR, dtype=jnp.int32)
    slot = jnp.where(position < CAP, 0, 1 + (position - CAP) % (N_COLS - 1))
    placed = jax.vmap(lambda k: jax.random.permutation(k, TPR))(jax.random.split(key_place, N_ROWS)).astype(jnp.int32)
    slot_of_tile = slot[placed]
    owner_perm = jax.vmap(lambda k: jax.random.permutation(k, N_COLS))(jax.random.split(key_owner, N_ROWS)).astype(jnp.int32)
    owners = jnp.take_along_axis(owner_perm, slot_of_tile, axis=1)
    stacked = jnp.stack([sel_block, sel_off, owners], axis=0)
    return stacked.reshape(3, N_ROWS * TPR).astype(jnp.int32)


def shard_levels(stream_key, extent, cuts, smallest, high):
    def one(dim, shards_of):
        heights = jax.random.uniform(jax.random.fold_in(jax.random.fold_in(stream_key, 6), dim), (shards_of,), jnp.float32, smallest / len(cuts), high / len(cuts))
        return jnp.repeat(jnp.exp(heights), extent[dim] // shards_of).reshape((-1,) + (1,) * (len(extent) - dim - 1))

    level = one(*cuts[0])
    for cut in cuts[1:]:
        level = level * one(*cut)
    return level


def noise(key, dims, scale, reach, cuts=(), held_as=jnp.bfloat16):
    factor_of = shard_levels(key, dims, cuts, -0.22, 0.18) if cuts else 1.0
    array = jax.random.normal(key, dims, jnp.float32) * scale * factor_of
    return jnp.minimum(jnp.maximum(array, -reach), reach).astype(held_as)


def setup_inputs(seed: int = 0) -> dict:
    streams_of = jax.random.split(jax.random.key(seed), 3)
    series = noise(streams_of[0], (SAMPLES,), 1.0, 6.0, ((0, 512),), jnp.float32)
    tile_list = draw_tile_list(jax.random.fold_in(streams_of[2], 71), 0)
    return dict(series=series, tile_list=tile_list)


def hankel(values, rows, width):
    length = values.shape[0]
    flat = jnp.concatenate([jnp.tile(values, rows), jnp.zeros((rows,), values.dtype)])
    return flat.reshape(rows, length + 1)[:, :width]

def normalize(values):
    windows = hankel(values, B, M)
    centre = windows - lax.optimization_barrier(jnp.mean(windows, axis=1, keepdims=True))
    spread = lax.optimization_barrier(jnp.mean(centre * centre, axis=1))
    factor = lax.rsqrt(spread + 1e-05) / math.sqrt(M)
    return centre * factor[:, None]

def tile_maxima(left_data, right_data, offset):
    left_z = normalize(left_data)
    right_z = normalize(right_data)
    corr = lax.dot_general(left_z, right_z, (((1,), (1,)), ((), ())), precision=lax.Precision.HIGHEST, preferred_element_type=jnp.float32)
    row_pos = lax.broadcasted_iota(jnp.int32, (B, B), 0)
    col_pos = lax.broadcasted_iota(jnp.int32, (B, B), 1)
    keep = offset * B + col_pos - row_pos >= EXCL
    corr = jnp.where(keep, corr, jnp.float32(-1.0))
    return (lax.optimization_barrier(jnp.max(corr, axis=1)), lax.optimization_barrier(jnp.max(corr, axis=0)))

def raise_block(profile, start, values):
    current = lax.dynamic_slice_in_dim(profile, start, B)
    return lax.dynamic_update_slice_in_dim(profile, jnp.maximum(current, values), start, 0)

def reference(series, tile_list):
    profile = jnp.full((SAMPLES,), -1.0, jnp.float32)

    def step(index, profile):
        row_block = tile_list[0, index].astype(jnp.int32)
        offset = tile_list[1, index].astype(jnp.int32)
        row_start = (row_block * B).astype(jnp.int32)
        col_start = ((row_block + offset) * B).astype(jnp.int32)
        left_data = lax.dynamic_slice_in_dim(series, row_start, B + M)
        right_data = lax.dynamic_slice_in_dim(series, col_start, B + M)
        row_max, col_max = tile_maxima(left_data, right_data, offset)
        profile = raise_block(profile, row_start, row_max)
        return raise_block(profile, col_start, col_max)
    return lax.fori_loop(0, TILES, step, profile)
```

```python
import math

import jax
import jax.numpy as jnp
from jax import lax
from jax.experimental import pallas as pl
from jax.experimental.pallas import tpu as pltpu
from jax.sharding import PartitionSpec as P

M = 256
B = 512
BPR = 128
EXCL = 64
SPILL = 8
SEG = B + M


def passed_along(block, axis, distance):
    devices = range(lax.axis_size(axis))
    route = [(i - distance, i) for i in devices if i - distance in devices]
    return lax.ppermute(block, axis, route)


def windows(row):
    wide = jnp.broadcast_to(row, (B, SEG))
    rolled = pltpu.roll(wide, 0, 1, stride=1, stride_axis=0)
    w = rolled[:, B:SEG]
    centre = w - jnp.mean(w, axis=1, keepdims=True)
    spread = jnp.mean(centre * centre, axis=1, keepdims=True)
    factor = lax.rsqrt(spread + 1e-05) / math.sqrt(M)
    return centre * factor


def tile_kernel(n_tiles, idx_ref, blocks_ref, out_ref):
    out_ref[...] = jnp.full(out_ref.shape, -1.0, jnp.float32)
    q = lax.broadcasted_iota(jnp.int32, (B, B), 0)
    s = lax.broadcasted_iota(jnp.int32, (B, B), 1)

    def body(t, carry):
        i = idx_ref[0, t]
        d = idx_ref[1, t]
        j = i + d
        zl = windows(blocks_ref[pl.ds(i, 1), :])
        zr = windows(blocks_ref[pl.ds(j, 1), :])
        corr = lax.dot_general(
            zl,
            zr,
            (((1,), (1,)), ((), ())),
            precision=lax.Precision.HIGHEST,
            preferred_element_type=jnp.float32,
        )
        corr = jnp.where(d * B + s - q >= EXCL, corr, jnp.float32(-1.0))
        col_max = jnp.max(corr, axis=0, keepdims=True)
        row_max_c = jnp.max(corr, axis=1, keepdims=True)
        row_max = jnp.sum(jnp.where(q == s, row_max_c, 0.0), axis=0, keepdims=True)
        out_ref[pl.ds(i, 1), :] = jnp.maximum(out_ref[pl.ds(i, 1), :], row_max)
        out_ref[pl.ds(j, 1), :] = jnp.maximum(out_ref[pl.ds(j, 1), :], col_max)
        return carry

    lax.fori_loop(0, n_tiles, body, 0)


def tile_maxima(idx, blocks):
    n_tiles = idx.shape[1]
    n_blocks = blocks.shape[0]
    return pl.pallas_call(
        lambda *refs: tile_kernel(n_tiles, *refs),
        out_shape=jax.ShapeDtypeStruct((n_blocks, B), jnp.float32),
        in_specs=[
            pl.BlockSpec(memory_space=pltpu.SMEM),
            pl.BlockSpec(memory_space=pltpu.VMEM),
        ],
        out_specs=pl.BlockSpec(memory_space=pltpu.VMEM),
        cost_estimate=pl.CostEstimate(
            flops=n_tiles * 2 * B * B * M * 6,
            bytes_accessed=n_blocks * (SEG + B) * 4,
            transcendentals=n_tiles * 2 * B,
        ),
    )(idx, blocks)


def on_device(series, tile_list):
    piece = series.shape[0]
    col_count = lax.axis_size("cols")
    group = lax.axis_index("rows")
    col_id = lax.axis_index("cols")
    segment = lax.all_gather(series, "cols", axis=0, tiled=True)
    head = passed_along(segment[: SPILL * B], "rows", -1)
    signal = jnp.concatenate([segment, head, jnp.zeros((B,), jnp.float32)])
    n_blocks = BPR + SPILL
    by_block = signal.reshape(n_blocks + 1, B)
    blocks = jnp.concatenate([by_block[:n_blocks], by_block[1:, :M]], axis=1)[:, ::-1]

    per_dev = tile_list.shape[1] // col_count
    mine = lax.dynamic_slice_in_dim(
        tile_list[:2].reshape(2, per_dev, col_count), col_id, 1, axis=2
    )[:, :, 0]
    idx = jnp.stack([mine[0] - group * BPR, mine[1]])

    partial = tile_maxima(idx, blocks)
    own = partial[:BPR]
    spill = partial[BPR:]
    arrived = passed_along(spill, "rows", 1)
    arrived = jnp.where(group > 0, arrived, jnp.float32(-1.0))
    own = jnp.concatenate([jnp.maximum(own[:SPILL], arrived), own[SPILL:]])
    chunks = own.reshape(col_count, BPR // col_count, B)
    got = lax.all_to_all(chunks, "cols", 0, 0, tiled=True)
    result = jnp.max(got.reshape(col_count, BPR // col_count, B), axis=0)
    return result.reshape(piece)


def solution(mesh):
    in_specs = (P(("rows", "cols")), P(None, "rows"))
    out_specs = P(("rows", "cols"))
    return jax.shard_map(
        on_device, mesh=mesh, in_specs=in_specs, out_specs=out_specs, check_vma=False
    )
```

```python
import math

import jax
import jax.numpy as jnp
from jax import lax
from jax.experimental import pallas as pl
from jax.experimental.pallas import tpu as pltpu
from jax.sharding import PartitionSpec as P

M = 256
B = 512
BPR = 128
EXCL = 64
SPILL = 8
SEG = B + M
MESH = pl.DeviceIdType.MESH


def passed_along(block, axis, distance):
    devices = range(lax.axis_size(axis))
    route = [(i - distance, i) for i in devices if i - distance in devices]
    return lax.ppermute(block, axis, route)


def windows(row):
    wide = jnp.broadcast_to(row, (B, SEG))
    rolled = pltpu.roll(wide, 0, 1, stride=1, stride_axis=0)
    w = rolled[:, B:SEG]
    centre = w - jnp.mean(w, axis=1, keepdims=True)
    spread = jnp.mean(centre * centre, axis=1, keepdims=True)
    factor = lax.rsqrt(spread + 1e-05) / math.sqrt(M)
    return centre * factor


def tile_kernel(n_tiles, idx_ref, blocks_ref, out_ref):
    out_ref[...] = jnp.full(out_ref.shape, -1.0, jnp.float32)
    q = lax.broadcasted_iota(jnp.int32, (B, B), 0)
    s = lax.broadcasted_iota(jnp.int32, (B, B), 1)

    def body(t, carry):
        i = idx_ref[0, t]
        d = idx_ref[1, t]
        j = i + d
        zl = windows(blocks_ref[pl.ds(i, 1), :])
        zr = windows(blocks_ref[pl.ds(j, 1), :])
        corr = lax.dot_general(
            zl,
            zr,
            (((1,), (1,)), ((), ())),
            precision=lax.Precision.HIGHEST,
            preferred_element_type=jnp.float32,
        )
        corr = jnp.where(d * B + s - q >= EXCL, corr, jnp.float32(-1.0))
        col_max = jnp.max(corr, axis=0, keepdims=True)
        row_max_c = jnp.max(corr, axis=1, keepdims=True)
        row_max = jnp.sum(jnp.where(q == s, row_max_c, 0.0), axis=0, keepdims=True)
        out_ref[pl.ds(i, 1), :] = jnp.maximum(out_ref[pl.ds(i, 1), :], row_max)
        out_ref[pl.ds(j, 1), :] = jnp.maximum(out_ref[pl.ds(j, 1), :], col_max)
        return carry

    lax.fori_loop(0, n_tiles, body, 0)


def tile_maxima(idx, blocks):
    n_tiles = idx.shape[1]
    n_blocks = blocks.shape[0]
    return pl.pallas_call(
        lambda *refs: tile_kernel(n_tiles, *refs),
        out_shape=jax.ShapeDtypeStruct((n_blocks, B), jnp.float32),
        in_specs=[
            pl.BlockSpec(memory_space=pltpu.SMEM),
            pl.BlockSpec(memory_space=pltpu.VMEM),
        ],
        out_specs=pl.BlockSpec(memory_space=pltpu.VMEM),
        cost_estimate=pl.CostEstimate(
            flops=n_tiles * 2 * B * B * M * 6,
            bytes_accessed=n_blocks * (SEG + B) * 4,
            transcendentals=n_tiles * 2 * B,
        ),
    )(idx, blocks)


def greet_partners(n_rows, n_cols):
    g = lax.axis_index("rows")
    c = lax.axis_index("cols")
    barrier = pltpu.get_barrier_semaphore()
    for p in range(n_cols):
        @pl.when(p != c)
        def _():
            pl.semaphore_signal(barrier, 1, device_id=(g, p), device_id_type=MESH)

    @pl.when(g + 1 < n_rows)
    def _():
        pl.semaphore_signal(barrier, 1, device_id=(g + 1, 0), device_id_type=MESH)

    first = jnp.logical_and(c == 0, g > 0)

    @pl.when(first)
    def _():
        for p in range(n_cols):
            pl.semaphore_signal(barrier, 1, device_id=(g - 1, p), device_id_type=MESH)

    count = (n_cols - 1) + (g + 1 < n_rows).astype(jnp.int32) + n_cols * first.astype(jnp.int32)
    pl.semaphore_wait(barrier, count)
    return g, c, first


def gather_kernel(n_rows, n_cols, piece_ref, out_ref, held, send_sems, recv_sems):
    g, c, first = greet_partners(n_rows, n_cols)

    def to_peer(p):
        return pltpu.make_async_remote_copy(
            src_ref=piece_ref,
            dst_ref=held.at[c],
            send_sem=send_sems.at[p],
            recv_sem=recv_sems.at[c],
            device_id=(g, p),
            device_id_type=MESH,
        )

    def from_peer(p):
        return pltpu.make_async_remote_copy(
            src_ref=piece_ref,
            dst_ref=held.at[p],
            send_sem=send_sems.at[p],
            recv_sem=recv_sems.at[p],
            device_id=(g, p),
            device_id_type=MESH,
        )

    def head_to(p):
        return pltpu.make_async_remote_copy(
            src_ref=piece_ref,
            dst_ref=held.at[n_cols],
            send_sem=send_sems.at[n_cols + p],
            recv_sem=recv_sems.at[n_cols],
            device_id=(g - 1, p),
            device_id_type=MESH,
        )

    @pl.when(first)
    def _():
        for p in range(n_cols):
            head_to(p).start()

    for p in range(n_cols):
        @pl.when(p != c)
        def _():
            to_peer(p).start()

    held[pl.ds(c, 1)] = piece_ref[...][None]

    @pl.when(g + 1 == n_rows)
    def _():
        held[n_cols] = jnp.zeros(piece_ref.shape, jnp.float32)

    for p in range(n_cols):
        @pl.when(p != c)
        def _():
            from_peer(p).wait_recv()
            to_peer(p).wait_send()

    @pl.when(g + 1 < n_rows)
    def _():
        head_to(0).wait_recv()

    @pl.when(first)
    def _():
        for p in range(n_cols):
            head_to(p).wait_send()

    out_ref[...] = held[...]


def gather_group(piece, n_rows, n_cols):
    shape = (n_cols + 1,) + piece.shape
    return pl.pallas_call(
        lambda *refs: gather_kernel(n_rows, n_cols, *refs),
        out_shape=jax.ShapeDtypeStruct(shape, jnp.float32),
        in_specs=[pl.BlockSpec(memory_space=pltpu.VMEM)],
        out_specs=pl.BlockSpec(memory_space=pltpu.VMEM),
        scratch_shapes=[
            pltpu.VMEM(shape, jnp.float32),
            pltpu.SemaphoreType.DMA((2 * n_cols,)),
            pltpu.SemaphoreType.DMA((n_cols + 1,)),
        ],
        compiler_params=pltpu.CompilerParams(collective_id=0, has_side_effects=True),
    )(piece)


def on_device(series, tile_list):
    piece = series.shape[0]
    col_count = lax.axis_size("cols")
    group = lax.axis_index("rows")
    col_id = lax.axis_index("cols")
    n_rows = lax.axis_size("rows")
    held = gather_group(series.reshape(SPILL, B), n_rows, col_count)
    signal = jnp.concatenate([held.reshape(-1), jnp.zeros((B,), jnp.float32)])
    n_blocks = BPR + SPILL
    by_block = signal.reshape(n_blocks + 1, B)
    blocks = jnp.concatenate([by_block[:n_blocks], by_block[1:, :M]], axis=1)[:, ::-1]

    per_dev = tile_list.shape[1] // col_count
    mine = lax.dynamic_slice_in_dim(
        tile_list[:2].reshape(2, per_dev, col_count), col_id, 1, axis=2
    )[:, :, 0]
    idx = jnp.stack([mine[0] - group * BPR, mine[1]])

    partial = tile_maxima(idx, blocks)
    own = partial[:BPR]
    spill = partial[BPR:]
    arrived = passed_along(spill, "rows", 1)
    arrived = jnp.where(group > 0, arrived, jnp.float32(-1.0))
    own = jnp.concatenate([jnp.maximum(own[:SPILL], arrived), own[SPILL:]])
    chunks = own.reshape(col_count, BPR // col_count, B)
    got = lax.all_to_all(chunks, "cols", 0, 0, tiled=True)
    result = jnp.max(got.reshape(col_count, BPR // col_count, B), axis=0)
    return result.reshape(piece)


def solution(mesh):
    in_specs = (P(("rows", "cols")), P(None, "rows"))
    out_specs = P(("rows", "cols"))
    return jax.shard_map(
        on_device, mesh=mesh, in_specs=in_specs, out_specs=out_specs, check_vma=False
    )
```

```python
import math

import jax
import jax.numpy as jnp
from jax import lax
from jax.experimental import pallas as pl
from jax.experimental.pallas import tpu as pltpu
from jax.sharding import PartitionSpec as P

M = 256
B = 512
BPR = 128
EXCL = 64
SPILL = 8
SEG = B + M
MESH = pl.DeviceIdType.MESH


def passed_along(block, axis, distance):
    devices = range(lax.axis_size(axis))
    route = [(i - distance, i) for i in devices if i - distance in devices]
    return lax.ppermute(block, axis, route)


def windows(row):
    wide = jnp.broadcast_to(row, (B, SEG))
    rolled = pltpu.roll(wide, 0, 1, stride=1, stride_axis=0)
    w = rolled[:, B:SEG]
    centre = w - jnp.mean(w, axis=1, keepdims=True)
    spread = jnp.mean(centre * centre, axis=1, keepdims=True)
    factor = lax.rsqrt(spread + 1e-05) / math.sqrt(M)
    return centre * factor


def split_dot(a, b):
    a_hi = a.astype(jnp.bfloat16)
    b_hi = b.astype(jnp.bfloat16)
    a_lo = (a - a_hi.astype(jnp.float32)).astype(jnp.bfloat16)
    b_lo = (b - b_hi.astype(jnp.float32)).astype(jnp.bfloat16)
    dims = (((1,), (1,)), ((), ()))

    def dot(x, y):
        return lax.dot_general(x, y, dims, preferred_element_type=jnp.float32)

    return dot(a_hi, b_hi) + (dot(a_hi, b_lo) + dot(a_lo, b_hi))


def tile_kernel(n_tiles, idx_ref, blocks_ref, out_ref):
    out_ref[...] = jnp.full(out_ref.shape, -1.0, jnp.float32)
    q = lax.broadcasted_iota(jnp.int32, (B, B), 0)
    s = lax.broadcasted_iota(jnp.int32, (B, B), 1)

    def body(t, carry):
        i = idx_ref[0, t]
        d = idx_ref[1, t]
        j = i + d
        zl = windows(blocks_ref[pl.ds(i, 1), :])
        zr = windows(blocks_ref[pl.ds(j, 1), :])
        corr = split_dot(zl, zr)
        corr = jnp.where(d * B + s - q >= EXCL, corr, jnp.float32(-1.0))
        col_max = jnp.max(corr, axis=0, keepdims=True)
        row_max_c = jnp.max(corr, axis=1, keepdims=True)
        row_max = jnp.sum(jnp.where(q == s, row_max_c, 0.0), axis=0, keepdims=True)
        out_ref[pl.ds(i, 1), :] = jnp.maximum(out_ref[pl.ds(i, 1), :], row_max)
        out_ref[pl.ds(j, 1), :] = jnp.maximum(out_ref[pl.ds(j, 1), :], col_max)
        return carry

    lax.fori_loop(0, n_tiles, body, 0)


def tile_maxima(idx, blocks):
    n_tiles = idx.shape[1]
    n_blocks = blocks.shape[0]
    return pl.pallas_call(
        lambda *refs: tile_kernel(n_tiles, *refs),
        out_shape=jax.ShapeDtypeStruct((n_blocks, B), jnp.float32),
        in_specs=[
            pl.BlockSpec(memory_space=pltpu.SMEM),
            pl.BlockSpec(memory_space=pltpu.VMEM),
        ],
        out_specs=pl.BlockSpec(memory_space=pltpu.VMEM),
        cost_estimate=pl.CostEstimate(
            flops=n_tiles * 2 * B * B * M * 3,
            bytes_accessed=n_blocks * (SEG + B) * 4,
            transcendentals=n_tiles * 2 * B,
        ),
    )(idx, blocks)


def greet_partners(n_rows, n_cols):
    g = lax.axis_index("rows")
    c = lax.axis_index("cols")
    barrier = pltpu.get_barrier_semaphore()
    for p in range(n_cols):
        @pl.when(p != c)
        def _():
            pl.semaphore_signal(barrier, 1, device_id=(g, p), device_id_type=MESH)

    @pl.when(g + 1 < n_rows)
    def _():
        pl.semaphore_signal(barrier, 1, device_id=(g + 1, 0), device_id_type=MESH)

    first = jnp.logical_and(c == 0, g > 0)

    @pl.when(first)
    def _():
        for p in range(n_cols):
            pl.semaphore_signal(barrier, 1, device_id=(g - 1, p), device_id_type=MESH)

    count = (n_cols - 1) + (g + 1 < n_rows).astype(jnp.int32) + n_cols * first.astype(jnp.int32)
    pl.semaphore_wait(barrier, count)
    return g, c, first


def gather_kernel(n_rows, n_cols, piece_ref, out_ref, held, send_sems, recv_sems):
    g, c, first = greet_partners(n_rows, n_cols)

    def to_peer(p):
        return pltpu.make_async_remote_copy(
            src_ref=piece_ref,
            dst_ref=held.at[c],
            send_sem=send_sems.at[p],
            recv_sem=recv_sems.at[c],
            device_id=(g, p),
            device_id_type=MESH,
        )

    def from_peer(p):
        return pltpu.make_async_remote_copy(
            src_ref=piece_ref,
            dst_ref=held.at[p],
            send_sem=send_sems.at[p],
            recv_sem=recv_sems.at[p],
            device_id=(g, p),
            device_id_type=MESH,
        )

    def head_to(p):
        return pltpu.make_async_remote_copy(
            src_ref=piece_ref,
            dst_ref=held.at[n_cols],
            send_sem=send_sems.at[n_cols + p],
            recv_sem=recv_sems.at[n_cols],
            device_id=(g - 1, p),
            device_id_type=MESH,
        )

    @pl.when(first)
    def _():
        for p in range(n_cols):
            head_to(p).start()

    for p in range(n_cols):
        @pl.when(p != c)
        def _():
            to_peer(p).start()

    held[pl.ds(c, 1)] = piece_ref[...][None]

    @pl.when(g + 1 == n_rows)
    def _():
        held[n_cols] = jnp.zeros(piece_ref.shape, jnp.float32)

    for p in range(n_cols):
        @pl.when(p != c)
        def _():
            from_peer(p).wait_recv()
            to_peer(p).wait_send()

    @pl.when(g + 1 < n_rows)
    def _():
        head_to(0).wait_recv()

    @pl.when(first)
    def _():
        for p in range(n_cols):
            head_to(p).wait_send()

    out_ref[...] = held[...]


def gather_group(piece, n_rows, n_cols):
    shape = (n_cols + 1,) + piece.shape
    return pl.pallas_call(
        lambda *refs: gather_kernel(n_rows, n_cols, *refs),
        out_shape=jax.ShapeDtypeStruct(shape, jnp.float32),
        in_specs=[pl.BlockSpec(memory_space=pltpu.VMEM)],
        out_specs=pl.BlockSpec(memory_space=pltpu.VMEM),
        scratch_shapes=[
            pltpu.VMEM(shape, jnp.float32),
            pltpu.SemaphoreType.DMA((2 * n_cols,)),
            pltpu.SemaphoreType.DMA((n_cols + 1,)),
        ],
        compiler_params=pltpu.CompilerParams(collective_id=0, has_side_effects=True),
    )(piece)


def on_device(series, tile_list):
    piece = series.shape[0]
    col_count = lax.axis_size("cols")
    group = lax.axis_index("rows")
    col_id = lax.axis_index("cols")
    n_rows = lax.axis_size("rows")
    held = gather_group(series.reshape(SPILL, B), n_rows, col_count)
    signal = jnp.concatenate([held.reshape(-1), jnp.zeros((B,), jnp.float32)])
    n_blocks = BPR + SPILL
    by_block = signal.reshape(n_blocks + 1, B)
    blocks = jnp.concatenate([by_block[:n_blocks], by_block[1:, :M]], axis=1)[:, ::-1]

    per_dev = tile_list.shape[1] // col_count
    mine = lax.dynamic_slice_in_dim(
        tile_list[:2].reshape(2, per_dev, col_count), col_id, 1, axis=2
    )[:, :, 0]
    idx = jnp.stack([mine[0] - group * BPR, mine[1]])

    partial = tile_maxima(idx, blocks)
    own = partial[:BPR]
    spill = partial[BPR:]
    arrived = passed_along(spill, "rows", 1)
    arrived = jnp.where(group > 0, arrived, jnp.float32(-1.0))
    own = jnp.concatenate([jnp.maximum(own[:SPILL], arrived), own[SPILL:]])
    chunks = own.reshape(col_count, BPR // col_count, B)
    got = lax.all_to_all(chunks, "cols", 0, 0, tiled=True)
    result = jnp.max(got.reshape(col_count, BPR // col_count, B), axis=0)
    return result.reshape(piece)


def solution(mesh):
    in_specs = (P(("rows", "cols")), P(None, "rows"))
    out_specs = P(("rows", "cols"))
    return jax.shard_map(
        on_device, mesh=mesh, in_specs=in_specs, out_specs=out_specs, check_vma=False
    )
```

```python
import math

import jax
import jax.numpy as jnp
from jax import lax
from jax.experimental import pallas as pl
from jax.experimental.pallas import tpu as pltpu
from jax.sharding import PartitionSpec as P

M = 256
B = 512
BPR = 128
EXCL = 64
SPILL = 8
SEG = B + M
MESH = pl.DeviceIdType.MESH


def passed_along(block, axis, distance):
    devices = range(lax.axis_size(axis))
    route = [(i - distance, i) for i in devices if i - distance in devices]
    return lax.ppermute(block, axis, route)


def windows(row):
    wide = jnp.broadcast_to(row, (B, SEG))
    rolled = pltpu.roll(wide, 0, 1, stride=1, stride_axis=0)
    w = rolled[:, B:SEG]
    centre = w - jnp.mean(w, axis=1, keepdims=True)
    spread = jnp.mean(centre * centre, axis=1, keepdims=True)
    factor = lax.rsqrt(spread + 1e-05) / math.sqrt(M)
    return centre * factor


def split_dot(a, b):
    a_hi = a.astype(jnp.bfloat16)
    b_hi = b.astype(jnp.bfloat16)
    a_lo = (a - a_hi.astype(jnp.float32)).astype(jnp.bfloat16)
    b_lo = (b - b_hi.astype(jnp.float32)).astype(jnp.bfloat16)
    dims = (((1,), (1,)), ((), ()))

    def dot(x, y):
        return lax.dot_general(x, y, dims, preferred_element_type=jnp.float32)

    return dot(a_hi, b_hi) + (dot(a_hi, b_lo) + dot(a_lo, b_hi))


def tile_kernel(n_tiles, idx_ref, blocks_ref, out_ref):
    out_ref[...] = jnp.full(out_ref.shape, -1.0, jnp.float32)
    q = lax.broadcasted_iota(jnp.int32, (B, B), 0)
    s = lax.broadcasted_iota(jnp.int32, (B, B), 1)

    def body(t, carry):
        i = idx_ref[0, t]
        d = idx_ref[1, t]
        j = i + d
        zl = windows(blocks_ref[pl.ds(i, 1), :])
        zr = windows(blocks_ref[pl.ds(j, 1), :])
        corr = split_dot(zl, zr)
        corr = jnp.where(d * B + s - q >= EXCL, corr, jnp.float32(-1.0))
        col_max = jnp.max(corr, axis=0, keepdims=True)
        row_max_c = jnp.max(corr, axis=1, keepdims=True)
        row_max = jnp.sum(jnp.where(q == s, row_max_c, 0.0), axis=0, keepdims=True)
        out_ref[pl.ds(i, 1), :] = jnp.maximum(out_ref[pl.ds(i, 1), :], row_max)
        out_ref[pl.ds(j, 1), :] = jnp.maximum(out_ref[pl.ds(j, 1), :], col_max)
        return carry

    lax.fori_loop(0, n_tiles, body, 0)


def tile_maxima(idx, blocks):
    n_tiles = idx.shape[1]
    n_blocks = blocks.shape[0]
    return pl.pallas_call(
        lambda *refs: tile_kernel(n_tiles, *refs),
        out_shape=jax.ShapeDtypeStruct((n_blocks, B), jnp.float32),
        in_specs=[
            pl.BlockSpec(memory_space=pltpu.SMEM),
            pl.BlockSpec(memory_space=pltpu.VMEM),
        ],
        out_specs=pl.BlockSpec(memory_space=pltpu.VMEM),
        cost_estimate=pl.CostEstimate(
            flops=n_tiles * 2 * B * B * M * 3,
            bytes_accessed=n_blocks * (SEG + B) * 4,
            transcendentals=n_tiles * 2 * B,
        ),
    )(idx, blocks)


def greet_partners(n_rows, n_cols):
    g = lax.axis_index("rows")
    c = lax.axis_index("cols")
    barrier = pltpu.get_barrier_semaphore()
    half = (c // 2) % 2
    peers = [p for p in range(n_cols)]
    for p in peers:
        @pl.when(jnp.logical_and(p != c, jnp.logical_or((p // 2) % 2 == half, p == c ^ 2)))
        def _():
            pl.semaphore_signal(barrier, 1, device_id=(g, p), device_id_type=MESH)

    collector = jnp.logical_or(c == 0, c == 2)
    up = jnp.logical_and(collector, g + 1 < n_rows)

    @pl.when(up)
    def _():
        pl.semaphore_signal(barrier, 1, device_id=(g + 1, 0), device_id_type=MESH)

    down = jnp.logical_and(c == 0, g > 0)

    @pl.when(down)
    def _():
        pl.semaphore_signal(barrier, 1, device_id=(g - 1, 0), device_id_type=MESH)
        pl.semaphore_signal(barrier, 1, device_id=(g - 1, 2), device_id_type=MESH)

    count = n_cols // 2 + up.astype(jnp.int32) + 2 * down.astype(jnp.int32)
    pl.semaphore_wait(barrier, count)
    return g, c, half, collector, up, down


def half_peers(n_cols, c, half):
    return [
        (p, jnp.logical_and(p != c, (p // 2) % 2 == half)) for p in range(n_cols)
    ]


def gather_kernel(n_rows, n_cols, piece_ref, out_ref, held, send_sems, recv_sems):
    g, c, half, collector, up, down = greet_partners(n_rows, n_cols)
    mate = c ^ 2
    head = n_cols

    def remote(src, slot, sem, device):
        return pltpu.make_async_remote_copy(
            src_ref=src,
            dst_ref=held.at[slot],
            send_sem=send_sems.at[sem],
            recv_sem=recv_sems.at[slot],
            device_id=device,
            device_id_type=MESH,
        )

    to_mate = remote(piece_ref, c, 0, (g, mate))
    to_mate.start()

    @pl.when(down)
    def _():
        remote(piece_ref, head, 1, (g - 1, 0)).start()
        remote(piece_ref, head, 2, (g - 1, 2)).start()

    @pl.when(g + 1 == n_rows)
    def _():
        held[head] = jnp.zeros(piece_ref.shape, jnp.float32)

    remote(piece_ref, mate, 0, (g, mate)).wait_recv()

    @pl.when(up)
    def _():
        remote(piece_ref, head, 1, (g + 1, 0)).wait_recv()

    peers = half_peers(n_cols, c, half)
    for p, live in peers:
        @pl.when(live)
        def _():
            remote(piece_ref, c, 3 + 3 * p, (g, p)).start()
            remote(held.at[mate], mate, 4 + 3 * p, (g, p)).start()

        @pl.when(jnp.logical_and(live, up))
        def _():
            remote(held.at[head], head, 5 + 3 * p, (g, p)).start()

    held[pl.ds(c, 1)] = piece_ref[...][None]

    for p, live in peers:
        @pl.when(live)
        def _():
            remote(piece_ref, p, 3 + 3 * p, (g, p)).wait_recv()
            remote(piece_ref, p ^ 2, 3 + 3 * p, (g, p)).wait_recv()

    not_collector = jnp.logical_and(jnp.logical_not(collector), g + 1 < n_rows)

    @pl.when(not_collector)
    def _():
        remote(piece_ref, head, 1, (g, 0)).wait_recv()

    to_mate.wait_send()

    @pl.when(down)
    def _():
        remote(piece_ref, head, 1, (g - 1, 0)).wait_send()
        remote(piece_ref, head, 2, (g - 1, 2)).wait_send()

    for p, live in peers:
        @pl.when(live)
        def _():
            remote(piece_ref, c, 3 + 3 * p, (g, p)).wait_send()
            remote(piece_ref, c, 4 + 3 * p, (g, p)).wait_send()

        @pl.when(jnp.logical_and(live, up))
        def _():
            remote(piece_ref, c, 5 + 3 * p, (g, p)).wait_send()

    out_ref[...] = held[...]


def gather_group(piece, n_rows, n_cols):
    shape = (n_cols + 1,) + piece.shape
    return pl.pallas_call(
        lambda *refs: gather_kernel(n_rows, n_cols, *refs),
        out_shape=jax.ShapeDtypeStruct(shape, jnp.float32),
        in_specs=[pl.BlockSpec(memory_space=pltpu.VMEM)],
        out_specs=pl.BlockSpec(memory_space=pltpu.VMEM),
        scratch_shapes=[
            pltpu.VMEM(shape, jnp.float32),
            pltpu.SemaphoreType.DMA((3 + 3 * n_cols,)),
            pltpu.SemaphoreType.DMA((n_cols + 1,)),
        ],
        compiler_params=pltpu.CompilerParams(collective_id=0, has_side_effects=True),
    )(piece)


def reduce_kernel(n_rows, n_cols, part_ref, out_ref, got, mine, spills, send_sems, recv_sems):
    got[...] = jnp.full(got.shape, -1.0, jnp.float32)
    spills[...] = jnp.full(spills.shape, -1.0, jnp.float32)
    g, c, half, collector, up, down = greet_partners(n_rows, n_cols)
    mate = c ^ 2
    spill = n_cols
    hub = 2 * half
    peers = half_peers(n_cols, c, half)

    def remote(src, dst, send, recv, device):
        return pltpu.make_async_remote_copy(
            src_ref=src,
            dst_ref=dst,
            send_sem=send_sems.at[send],
            recv_sem=recv_sems.at[recv],
            device_id=device,
            device_id_type=MESH,
        )

    def to_peer(p, k):
        return remote(part_ref.at[p ^ (2 * k)], got.at[c, k], 3 * p + k, 2 * c + k, (g, p))

    def from_peer(p, k):
        return remote(part_ref.at[p], got.at[p, k], 3 * p + k, 2 * p + k, (g, p))

    def spill_to_hub():
        return remote(part_ref.at[spill], got.at[c, 2], 3 * n_cols, 2 * n_cols + 1 + c, (g, hub))

    def spill_from(p):
        return remote(part_ref.at[spill], got.at[p, 2], 3 * n_cols, 2 * n_cols + 1 + p, (g, p))

    for p, live in peers:
        @pl.when(live)
        def _():
            to_peer(p, 0).start()
            to_peer(p, 1).start()

    @pl.when(jnp.logical_not(collector))
    def _():
        spill_to_hub().start()

    for p, live in peers:
        @pl.when(live)
        def _():
            from_peer(p, 0).wait_recv()
            from_peer(p, 1).wait_recv()

    acc = jnp.maximum(part_ref[pl.ds(c, 1)][0], jnp.max(got[:, 0], axis=0))
    mine[0] = jnp.maximum(part_ref[pl.ds(mate, 1)][0], jnp.max(got[:, 1], axis=0))

    to_mate = remote(mine.at[0], mine.at[1], 3 * n_cols + 1, 3 * n_cols + 1, (g, mate))
    to_mate.start()

    @pl.when(collector)
    def _():
        for p, live in peers:
            @pl.when(live)
            def _():
                spill_from(p).wait_recv()

    mine[2] = jnp.maximum(part_ref[spill], jnp.max(got[:, 2], axis=0))

    def spill_up():
        return remote(mine.at[2], spills.at[half], 3 * n_cols + 2, 3 * n_cols + 2 + half, (g + 1, 0))

    @pl.when(up)
    def _():
        spill_up().start()

    to_mate.wait_recv()

    @pl.when(down)
    def _():
        remote(mine.at[2], spills.at[0], 3 * n_cols + 2, 3 * n_cols + 2, (g - 1, 0)).wait_recv()
        remote(mine.at[2], spills.at[1], 3 * n_cols + 2, 3 * n_cols + 3, (g - 1, 2)).wait_recv()

    acc = jnp.maximum(acc, mine[1])
    out_ref[...] = jnp.maximum(acc, jnp.maximum(spills[0], spills[1]))

    for p, live in peers:
        @pl.when(live)
        def _():
            to_peer(p, 0).wait_send()
            to_peer(p, 1).wait_send()

    @pl.when(jnp.logical_not(collector))
    def _():
        spill_to_hub().wait_send()

    to_mate.wait_send()

    @pl.when(up)
    def _():
        spill_up().wait_send()


def reduce_group(partial, n_rows, n_cols):
    chunk = partial.shape[1:]
    return pl.pallas_call(
        lambda *refs: reduce_kernel(n_rows, n_cols, *refs),
        out_shape=jax.ShapeDtypeStruct(chunk, jnp.float32),
        in_specs=[pl.BlockSpec(memory_space=pltpu.VMEM)],
        out_specs=pl.BlockSpec(memory_space=pltpu.VMEM),
        scratch_shapes=[
            pltpu.VMEM((n_cols, 3) + chunk, jnp.float32),
            pltpu.VMEM((3,) + chunk, jnp.float32),
            pltpu.VMEM((2,) + chunk, jnp.float32),
            pltpu.SemaphoreType.DMA((3 * n_cols + 3,)),
            pltpu.SemaphoreType.DMA((3 * n_cols + 4,)),
        ],
        compiler_params=pltpu.CompilerParams(collective_id=1, has_side_effects=True),
    )(partial)


def on_device(series, tile_list):
    piece = series.shape[0]
    col_count = lax.axis_size("cols")
    group = lax.axis_index("rows")
    col_id = lax.axis_index("cols")
    n_rows = lax.axis_size("rows")
    held = gather_group(series.reshape(SPILL, B), n_rows, col_count)
    signal = jnp.concatenate([held.reshape(-1), jnp.zeros((B,), jnp.float32)])
    n_blocks = BPR + SPILL
    by_block = signal.reshape(n_blocks + 1, B)
    blocks = jnp.concatenate([by_block[:n_blocks], by_block[1:, :M]], axis=1)[:, ::-1]

    per_dev = tile_list.shape[1] // col_count
    mine = lax.dynamic_slice_in_dim(
        tile_list[:2].reshape(2, per_dev, col_count), col_id, 1, axis=2
    )[:, :, 0]
    idx = jnp.stack([mine[0] - group * BPR, mine[1]])

    partial = tile_maxima(idx, blocks)
    result = reduce_group(partial.reshape(col_count + 1, SPILL, B), n_rows, col_count)
    return result.reshape(piece)


def solution(mesh):
    in_specs = (P(("rows", "cols")), P(None, "rows"))
    out_specs = P(("rows", "cols"))
    return jax.shard_map(
        on_device, mesh=mesh, in_specs=in_specs, out_specs=out_specs, check_vma=False
    )
```

```python
import math

import jax
import jax.numpy as jnp
from jax import lax
from jax.experimental import pallas as pl
from jax.experimental.pallas import tpu as pltpu
from jax.sharding import PartitionSpec as P

M = 256
B = 512
BPR = 128
EXCL = 64
SPILL = 8
SEG = B + M
MESH = pl.DeviceIdType.MESH


def passed_along(block, axis, distance):
    devices = range(lax.axis_size(axis))
    route = [(i - distance, i) for i in devices if i - distance in devices]
    return lax.ppermute(block, axis, route)


def windows(held, b):
    seg = jnp.concatenate([held[pl.ds(b, 1), :], held[pl.ds(b + 1, 1), :][:, :M]], axis=1)
    wide = jnp.broadcast_to(seg, (B, SEG))
    rolled = pltpu.roll(wide, 1, 1, stride=1, stride_axis=0)
    w = rolled[:, B:SEG]
    centre = w - jnp.mean(w, axis=1, keepdims=True)
    spread = jnp.mean(centre * centre, axis=1, keepdims=True)
    factor = lax.rsqrt(spread + 1e-05) / math.sqrt(M)
    return centre * factor


def split_dot(a, b):
    a_hi = a.astype(jnp.bfloat16)
    b_hi = b.astype(jnp.bfloat16)
    a_lo = (a - a_hi.astype(jnp.float32)).astype(jnp.bfloat16)
    b_lo = (b - b_hi.astype(jnp.float32)).astype(jnp.bfloat16)
    dims = (((1,), (1,)), ((), ()))

    def dot(x, y):
        return lax.dot_general(x, y, dims, preferred_element_type=jnp.float32)

    return dot(a_hi, b_hi) + (dot(a_hi, b_lo) + dot(a_lo, b_hi))


def greet_partners(n_rows, n_cols):
    g = lax.axis_index("rows")
    c = lax.axis_index("cols")
    barrier = pltpu.get_barrier_semaphore()
    half = (c // 2) % 2
    peers = [p for p in range(n_cols)]
    for p in peers:
        @pl.when(jnp.logical_and(p != c, jnp.logical_or((p // 2) % 2 == half, p == c ^ 2)))
        def _():
            pl.semaphore_signal(barrier, 1, device_id=(g, p), device_id_type=MESH)

    collector = jnp.logical_or(c == 0, c == 2)
    up = jnp.logical_and(collector, g + 1 < n_rows)

    @pl.when(up)
    def _():
        pl.semaphore_signal(barrier, 1, device_id=(g + 1, 0), device_id_type=MESH)

    down = jnp.logical_and(c == 0, g > 0)

    @pl.when(down)
    def _():
        pl.semaphore_signal(barrier, 1, device_id=(g - 1, 0), device_id_type=MESH)
        pl.semaphore_signal(barrier, 1, device_id=(g - 1, 2), device_id_type=MESH)

    count = n_cols // 2 + up.astype(jnp.int32) + 2 * down.astype(jnp.int32)
    pl.semaphore_wait(barrier, count)
    return g, c, half, collector, up, down


def half_peers(n_cols, c, half):
    return [
        (p, jnp.logical_and(p != c, (p // 2) % 2 == half)) for p in range(n_cols)
    ]


def fused_kernel(n_rows, n_cols, n_tiles, idx_ref, piece_ref, out_ref,
                 held, partial, got, mine, spills, g_send, g_recv, r_send, r_recv):
    got[...] = jnp.full(got.shape, -1.0, jnp.float32)
    spills[...] = jnp.full(spills.shape, -1.0, jnp.float32)
    partial[...] = jnp.full(partial.shape, -1.0, jnp.float32)
    g, c, half, collector, up, down = greet_partners(n_rows, n_cols)
    mate = c ^ 2
    head = n_cols
    rows = SPILL
    peers = half_peers(n_cols, c, half)

    def slab(ref, k):
        if isinstance(k, int):
            return ref.at[pl.ds(k * rows, rows)]
        return ref.at[pl.ds(pl.multiple_of(k * rows, rows), rows)]

    def remote(src, slot, sem, device):
        return pltpu.make_async_remote_copy(
            src_ref=src,
            dst_ref=slab(held, slot),
            send_sem=g_send.at[sem],
            recv_sem=g_recv.at[slot],
            device_id=device,
            device_id_type=MESH,
        )

    to_mate = remote(piece_ref, c, 0, (g, mate))
    to_mate.start()

    @pl.when(down)
    def _():
        remote(piece_ref, head, 1, (g - 1, 0)).start()
        remote(piece_ref, head, 2, (g - 1, 2)).start()

    @pl.when(g + 1 == n_rows)
    def _():
        held[pl.ds(head * rows, rows), :] = jnp.zeros(piece_ref.shape, jnp.float32)

    remote(piece_ref, mate, 0, (g, mate)).wait_recv()

    @pl.when(up)
    def _():
        remote(piece_ref, head, 1, (g + 1, 0)).wait_recv()

    for p, live in peers:
        @pl.when(live)
        def _():
            remote(piece_ref, c, 3 + 3 * p, (g, p)).start()
            remote(slab(held, mate), mate, 4 + 3 * p, (g, p)).start()

        @pl.when(jnp.logical_and(live, up))
        def _():
            remote(slab(held, head), head, 5 + 3 * p, (g, p)).start()

    held[pl.ds(pl.multiple_of(c * rows, rows), rows), :] = piece_ref[...]

    for p, live in peers:
        @pl.when(live)
        def _():
            remote(piece_ref, p, 3 + 3 * p, (g, p)).wait_recv()
            remote(piece_ref, p ^ 2, 3 + 3 * p, (g, p)).wait_recv()

    @pl.when(jnp.logical_and(jnp.logical_not(collector), g + 1 < n_rows))
    def _():
        remote(piece_ref, head, 1, (g, 0)).wait_recv()

    r_i = lax.broadcasted_iota(jnp.int32, (B, B), 0)
    r_j = lax.broadcasted_iota(jnp.int32, (B, B), 1)
    flip = r_i + r_j == B - 1

    def body(t, carry):
        i = idx_ref[0, t]
        d = idx_ref[1, t]
        j = i + d
        zl = windows(held, i)
        zr = windows(held, j)
        corr = split_dot(zl, zr)
        corr = jnp.where(d * B + r_i - r_j >= EXCL, corr, jnp.float32(-1.0))
        row_c = jnp.max(corr, axis=1, keepdims=True)
        row_max = jnp.sum(jnp.where(flip, row_c, 0.0), axis=0, keepdims=True)
        col_r = jnp.max(corr, axis=0, keepdims=True)
        col_c = jnp.sum(jnp.where(flip, col_r, 0.0), axis=1, keepdims=True)
        col_max = jnp.sum(jnp.where(r_i == r_j, col_c, 0.0), axis=0, keepdims=True)
        blk = lax.broadcasted_iota(jnp.int32, partial.shape, 0)
        upd = jnp.maximum(
            jnp.where(blk == i, row_max, jnp.float32(-1.0)),
            jnp.where(blk == j, col_max, jnp.float32(-1.0)),
        )
        partial[...] = jnp.maximum(partial[...], upd)
        return carry

    lax.fori_loop(0, n_tiles, body, 0)

    spill = n_cols

    def rremote(src, dst, send, recv, device):
        return pltpu.make_async_remote_copy(
            src_ref=src,
            dst_ref=dst,
            send_sem=r_send.at[send],
            recv_sem=r_recv.at[recv],
            device_id=device,
            device_id_type=MESH,
        )

    hub = 2 * half

    def to_peer(p, k):
        return rremote(slab(partial, p ^ (2 * k)), got.at[c, k], 3 * p + k, 2 * c + k, (g, p))

    def from_peer(p, k):
        return rremote(slab(partial, p), got.at[p, k], 3 * p + k, 2 * p + k, (g, p))

    def spill_to_hub():
        return rremote(slab(partial, spill), got.at[c, 2], 3 * n_cols, 2 * n_cols + 1 + c, (g, hub))

    def spill_from(p):
        return rremote(slab(partial, spill), got.at[p, 2], 3 * n_cols, 2 * n_cols + 1 + p, (g, p))

    for p, live in peers:
        @pl.when(live)
        def _():
            to_peer(p, 0).start()
            to_peer(p, 1).start()

    @pl.when(jnp.logical_not(collector))
    def _():
        spill_to_hub().start()

    for p, live in peers:
        @pl.when(live)
        def _():
            from_peer(p, 0).wait_recv()
            from_peer(p, 1).wait_recv()

    own = partial[pl.ds(pl.multiple_of(c * rows, rows), rows), :]
    mate_part = partial[pl.ds(pl.multiple_of(mate * rows, rows), rows), :]
    acc = jnp.maximum(own, jnp.max(got[:, 0], axis=0))
    mine[0] = jnp.maximum(mate_part, jnp.max(got[:, 1], axis=0))

    to_mate_r = rremote(mine.at[0], mine.at[1], 3 * n_cols + 1, 3 * n_cols + 1, (g, mate))
    to_mate_r.start()

    @pl.when(collector)
    def _():
        for p, live in peers:
            @pl.when(live)
            def _():
                spill_from(p).wait_recv()

    mine[2] = jnp.maximum(partial[pl.ds(spill * rows, rows), :], jnp.max(got[:, 2], axis=0))

    def spill_up():
        return rremote(mine.at[2], spills.at[half], 3 * n_cols + 2, 3 * n_cols + 2 + half, (g + 1, 0))

    @pl.when(up)
    def _():
        spill_up().start()

    to_mate_r.wait_recv()

    @pl.when(down)
    def _():
        rremote(mine.at[2], spills.at[0], 3 * n_cols + 2, 3 * n_cols + 2, (g - 1, 0)).wait_recv()
        rremote(mine.at[2], spills.at[1], 3 * n_cols + 2, 3 * n_cols + 3, (g - 1, 2)).wait_recv()

    acc = jnp.maximum(acc, mine[1])
    out_ref[...] = jnp.maximum(acc, jnp.maximum(spills[0], spills[1]))

    to_mate.wait_send()

    @pl.when(down)
    def _():
        remote(piece_ref, head, 1, (g - 1, 0)).wait_send()
        remote(piece_ref, head, 2, (g - 1, 2)).wait_send()

    for p, live in peers:
        @pl.when(live)
        def _():
            remote(piece_ref, c, 3 + 3 * p, (g, p)).wait_send()
            remote(piece_ref, c, 4 + 3 * p, (g, p)).wait_send()
            to_peer(p, 0).wait_send()
            to_peer(p, 1).wait_send()

        @pl.when(jnp.logical_and(live, up))
        def _():
            remote(piece_ref, c, 5 + 3 * p, (g, p)).wait_send()

    @pl.when(jnp.logical_not(collector))
    def _():
        spill_to_hub().wait_send()

    to_mate_r.wait_send()

    @pl.when(up)
    def _():
        spill_up().wait_send()


def fused_call(idx, piece, n_rows, n_cols):
    n_tiles = idx.shape[1]
    slots = n_cols + 1
    chunk = piece.shape
    return pl.pallas_call(
        lambda *refs: fused_kernel(n_rows, n_cols, n_tiles, *refs),
        out_shape=jax.ShapeDtypeStruct(chunk, jnp.float32),
        in_specs=[
            pl.BlockSpec(memory_space=pltpu.SMEM),
            pl.BlockSpec(memory_space=pltpu.VMEM),
        ],
        out_specs=pl.BlockSpec(memory_space=pltpu.VMEM),
        scratch_shapes=[
            pltpu.VMEM((slots * chunk[0], B), jnp.float32),
            pltpu.VMEM((slots * chunk[0], B), jnp.float32),
            pltpu.VMEM((n_cols, 3) + chunk, jnp.float32),
            pltpu.VMEM((3,) + chunk, jnp.float32),
            pltpu.VMEM((2,) + chunk, jnp.float32),
            pltpu.SemaphoreType.DMA((3 + 3 * n_cols,)),
            pltpu.SemaphoreType.DMA((slots,)),
            pltpu.SemaphoreType.DMA((3 * n_cols + 3,)),
            pltpu.SemaphoreType.DMA((3 * n_cols + 4,)),
        ],
        cost_estimate=pl.CostEstimate(
            flops=n_tiles * 2 * B * B * M * 3,
            bytes_accessed=slots * chunk[0] * B * 4,
            transcendentals=n_tiles * 2 * B,
        ),
        compiler_params=pltpu.CompilerParams(collective_id=0, has_side_effects=True),
    )(idx, piece)


def on_device(series, tile_list):
    piece = series.shape[0]
    col_count = lax.axis_size("cols")
    n_rows = lax.axis_size("rows")
    group = lax.axis_index("rows")
    col_id = lax.axis_index("cols")
    per_dev = tile_list.shape[1] // col_count
    mine = lax.dynamic_slice_in_dim(
        tile_list[:2].reshape(2, per_dev, col_count), col_id, 1, axis=2
    )[:, :, 0]
    idx = jnp.stack([mine[0] - group * BPR, mine[1]])
    result = fused_call(idx, series.reshape(SPILL, B), n_rows, col_count)
    return result.reshape(piece)


def solution(mesh):
    in_specs = (P(("rows", "cols")), P(None, "rows"))
    out_specs = P(("rows", "cols"))
    return jax.shard_map(
        on_device, mesh=mesh, in_specs=in_specs, out_specs=out_specs, check_vma=False
    )
```

```python
import math

import jax
import jax.numpy as jnp
from jax import lax
from jax.experimental import pallas as pl
from jax.experimental.pallas import tpu as pltpu
from jax.sharding import PartitionSpec as P

M = 256
B = 512
BPR = 128
EXCL = 64
SPILL = 8
SEG = B + M
MESH = pl.DeviceIdType.MESH


def passed_along(block, axis, distance):
    devices = range(lax.axis_size(axis))
    route = [(i - distance, i) for i in devices if i - distance in devices]
    return lax.ppermute(block, axis, route)


def windows(held, b):
    seg = jnp.concatenate([held[pl.ds(b, 1), :], held[pl.ds(b + 1, 1), :][:, :M]], axis=1)
    parts = []
    for m in range(B // 128):
        lo = 3 * 128 - 128 * m
        sub = jnp.broadcast_to(seg[:, lo:lo + 3 * 128], (128, 3 * 128))
        parts.append(pltpu.roll(sub, 1, 1, stride=1, stride_axis=0)[:, 128:])
    w = jnp.concatenate(parts, axis=0)
    centre = w - jnp.mean(w, axis=1, keepdims=True)
    spread = jnp.mean(centre * centre, axis=1, keepdims=True)
    factor = lax.rsqrt(spread + 1e-05) / math.sqrt(M)
    return centre * factor


def split_dot(a, b):
    a_hi = a.astype(jnp.bfloat16)
    b_hi = b.astype(jnp.bfloat16)
    a_lo = (a - a_hi.astype(jnp.float32)).astype(jnp.bfloat16)
    b_lo = (b - b_hi.astype(jnp.float32)).astype(jnp.bfloat16)
    dims = (((1,), (1,)), ((), ()))

    def dot(x, y):
        return lax.dot_general(x, y, dims, preferred_element_type=jnp.float32)

    return dot(a_hi, b_hi) + (dot(a_hi, b_lo) + dot(a_lo, b_hi))


def greet_partners(n_rows, n_cols):
    g = lax.axis_index("rows")
    c = lax.axis_index("cols")
    barrier = pltpu.get_barrier_semaphore()
    half = (c // 2) % 2
    peers = [p for p in range(n_cols)]
    for p in peers:
        @pl.when(jnp.logical_and(p != c, jnp.logical_or((p // 2) % 2 == half, p == c ^ 2)))
        def _():
            pl.semaphore_signal(barrier, 1, device_id=(g, p), device_id_type=MESH)

    collector = jnp.logical_or(c == 0, c == 2)
    up = jnp.logical_and(collector, g + 1 < n_rows)

    @pl.when(up)
    def _():
        pl.semaphore_signal(barrier, 1, device_id=(g + 1, 0), device_id_type=MESH)

    down = jnp.logical_and(c == 0, g > 0)

    @pl.when(down)
    def _():
        pl.semaphore_signal(barrier, 1, device_id=(g - 1, 0), device_id_type=MESH)
        pl.semaphore_signal(barrier, 1, device_id=(g - 1, 2), device_id_type=MESH)

    count = n_cols // 2 + up.astype(jnp.int32) + 2 * down.astype(jnp.int32)
    pl.semaphore_wait(barrier, count)
    return g, c, half, collector, up, down


def half_peers(n_cols, c, half):
    return [
        (p, jnp.logical_and(p != c, (p // 2) % 2 == half)) for p in range(n_cols)
    ]


def fused_kernel(n_rows, n_cols, n_tiles, tiles_ref, piece_ref, out_ref,
                 held, partial, got, mine, spills, g_send, g_recv, r_send, r_recv):
    got[...] = jnp.full(got.shape, -1.0, jnp.float32)
    spills[...] = jnp.full(spills.shape, -1.0, jnp.float32)
    partial[...] = jnp.full(partial.shape, -1.0, jnp.float32)
    g, c, half, collector, up, down = greet_partners(n_rows, n_cols)
    mate = c ^ 2
    head = n_cols
    rows = SPILL
    peers = half_peers(n_cols, c, half)

    def slab(ref, k):
        if isinstance(k, int):
            return ref.at[pl.ds(k * rows, rows)]
        return ref.at[pl.ds(pl.multiple_of(k * rows, rows), rows)]

    def remote(src, slot, sem, device):
        return pltpu.make_async_remote_copy(
            src_ref=src,
            dst_ref=slab(held, slot),
            send_sem=g_send.at[sem],
            recv_sem=g_recv.at[slot],
            device_id=device,
            device_id_type=MESH,
        )

    to_mate = remote(piece_ref, c, 0, (g, mate))
    to_mate.start()

    @pl.when(down)
    def _():
        remote(piece_ref, head, 1, (g - 1, 0)).start()
        remote(piece_ref, head, 2, (g - 1, 2)).start()

    @pl.when(g + 1 == n_rows)
    def _():
        held[pl.ds(head * rows, rows), :] = jnp.zeros(piece_ref.shape, jnp.float32)

    remote(piece_ref, mate, 0, (g, mate)).wait_recv()

    @pl.when(up)
    def _():
        remote(piece_ref, head, 1, (g + 1, 0)).wait_recv()

    for p, live in peers:
        @pl.when(live)
        def _():
            remote(piece_ref, c, 3 + 3 * p, (g, p)).start()
            remote(slab(held, mate), mate, 4 + 3 * p, (g, p)).start()

        @pl.when(jnp.logical_and(live, up))
        def _():
            remote(slab(held, head), head, 5 + 3 * p, (g, p)).start()

    held[pl.ds(pl.multiple_of(c * rows, rows), rows), :] = piece_ref[...]

    for p, live in peers:
        @pl.when(live)
        def _():
            remote(piece_ref, p, 3 + 3 * p, (g, p)).wait_recv()
            remote(piece_ref, p ^ 2, 3 + 3 * p, (g, p)).wait_recv()

    @pl.when(jnp.logical_and(jnp.logical_not(collector), g + 1 < n_rows))
    def _():
        remote(piece_ref, head, 1, (g, 0)).wait_recv()

    r_i = lax.broadcasted_iota(jnp.int32, (B, B), 0)
    r_j = lax.broadcasted_iota(jnp.int32, (B, B), 1)
    flip = r_i + r_j == B - 1

    def body(t, carry):
        col = c + n_cols * t
        i = jnp.clip(tiles_ref[0, col] - g * BPR, 0, BPR - 1)
        d = jnp.clip(tiles_ref[1, col], 0, SPILL - 1)
        j = i + d
        zl = windows(held, i)
        zr = windows(held, j)
        corr = split_dot(zl, zr)
        corr = jnp.where(d * B + r_i - r_j >= EXCL, corr, jnp.float32(-1.0))
        row_c = jnp.max(corr, axis=1, keepdims=True)
        row_max = jnp.sum(jnp.where(flip, row_c, 0.0), axis=0, keepdims=True)
        col_r = jnp.max(corr, axis=0, keepdims=True)
        col_c = jnp.sum(jnp.where(flip, col_r, 0.0), axis=1, keepdims=True)
        col_max = jnp.sum(jnp.where(r_i == r_j, col_c, 0.0), axis=0, keepdims=True)
        blk = lax.broadcasted_iota(jnp.int32, partial.shape, 0)
        upd = jnp.maximum(
            jnp.where(blk == i, row_max, jnp.float32(-1.0)),
            jnp.where(blk == j, col_max, jnp.float32(-1.0)),
        )
        partial[...] = jnp.maximum(partial[...], upd)
        return carry

    lax.fori_loop(0, n_tiles, body, 0)

    spill = n_cols

    def rremote(src, dst, send, recv, device):
        return pltpu.make_async_remote_copy(
            src_ref=src,
            dst_ref=dst,
            send_sem=r_send.at[send],
            recv_sem=r_recv.at[recv],
            device_id=device,
            device_id_type=MESH,
        )

    hub = 2 * half

    def to_peer(p, k):
        return rremote(slab(partial, p ^ (2 * k)), got.at[c, k], 3 * p + k, 2 * c + k, (g, p))

    def from_peer(p, k):
        return rremote(slab(partial, p), got.at[p, k], 3 * p + k, 2 * p + k, (g, p))

    def spill_to_hub():
        return rremote(slab(partial, spill), got.at[c, 2], 3 * n_cols, 2 * n_cols + 1 + c, (g, hub))

    def spill_from(p):
        return rremote(slab(partial, spill), got.at[p, 2], 3 * n_cols, 2 * n_cols + 1 + p, (g, p))

    for p, live in peers:
        @pl.when(live)
        def _():
            to_peer(p, 0).start()
            to_peer(p, 1).start()

    @pl.when(jnp.logical_not(collector))
    def _():
        spill_to_hub().start()

    for p, live in peers:
        @pl.when(live)
        def _():
            from_peer(p, 0).wait_recv()
            from_peer(p, 1).wait_recv()

    own = partial[pl.ds(pl.multiple_of(c * rows, rows), rows), :]
    mate_part = partial[pl.ds(pl.multiple_of(mate * rows, rows), rows), :]
    acc = jnp.maximum(own, jnp.max(got[:, 0], axis=0))
    mine[0] = jnp.maximum(mate_part, jnp.max(got[:, 1], axis=0))

    to_mate_r = rremote(mine.at[0], mine.at[1], 3 * n_cols + 1, 3 * n_cols + 1, (g, mate))
    to_mate_r.start()

    @pl.when(collector)
    def _():
        for p, live in peers:
            @pl.when(live)
            def _():
                spill_from(p).wait_recv()

    mine[2] = jnp.maximum(partial[pl.ds(spill * rows, rows), :], jnp.max(got[:, 2], axis=0))

    def spill_up():
        return rremote(mine.at[2], spills.at[half], 3 * n_cols + 2, 3 * n_cols + 2 + half, (g + 1, 0))

    @pl.when(up)
    def _():
        spill_up().start()

    to_mate_r.wait_recv()

    @pl.when(down)
    def _():
        rremote(mine.at[2], spills.at[0], 3 * n_cols + 2, 3 * n_cols + 2, (g - 1, 0)).wait_recv()
        rremote(mine.at[2], spills.at[1], 3 * n_cols + 2, 3 * n_cols + 3, (g - 1, 2)).wait_recv()

    acc = jnp.maximum(acc, mine[1])
    acc = jnp.maximum(acc, jnp.maximum(spills[0], spills[1]))
    lanes = 128
    per_row = B // lanes
    for k in range(rows):
        for v in range(per_row):
            out_ref[pl.ds(k * per_row + v, 1), :] = acc[k:k + 1, v * lanes:(v + 1) * lanes]

    to_mate.wait_send()

    @pl.when(down)
    def _():
        remote(piece_ref, head, 1, (g - 1, 0)).wait_send()
        remote(piece_ref, head, 2, (g - 1, 2)).wait_send()

    for p, live in peers:
        @pl.when(live)
        def _():
            remote(piece_ref, c, 3 + 3 * p, (g, p)).wait_send()
            remote(piece_ref, c, 4 + 3 * p, (g, p)).wait_send()
            to_peer(p, 0).wait_send()
            to_peer(p, 1).wait_send()

        @pl.when(jnp.logical_and(live, up))
        def _():
            remote(piece_ref, c, 5 + 3 * p, (g, p)).wait_send()

    @pl.when(jnp.logical_not(collector))
    def _():
        spill_to_hub().wait_send()

    to_mate_r.wait_send()

    @pl.when(up)
    def _():
        spill_up().wait_send()


def fused_call(tiles, piece, n_rows, n_cols):
    n_tiles = tiles.shape[1] // n_cols
    slots = n_cols + 1
    chunk = piece.shape
    return pl.pallas_call(
        lambda *refs: fused_kernel(n_rows, n_cols, n_tiles, *refs),
        out_shape=jax.ShapeDtypeStruct((chunk[0] * chunk[1] // 128, 128), jnp.float32),
        in_specs=[
            pl.BlockSpec(memory_space=pltpu.SMEM),
            pl.BlockSpec(memory_space=pltpu.VMEM),
        ],
        out_specs=pl.BlockSpec(memory_space=pltpu.VMEM),
        scratch_shapes=[
            pltpu.VMEM((slots * chunk[0], B), jnp.float32),
            pltpu.VMEM((slots * chunk[0], B), jnp.float32),
            pltpu.VMEM((n_cols, 3) + chunk, jnp.float32),
            pltpu.VMEM((3,) + chunk, jnp.float32),
            pltpu.VMEM((2,) + chunk, jnp.float32),
            pltpu.SemaphoreType.DMA((3 + 3 * n_cols,)),
            pltpu.SemaphoreType.DMA((slots,)),
            pltpu.SemaphoreType.DMA((3 * n_cols + 3,)),
            pltpu.SemaphoreType.DMA((3 * n_cols + 4,)),
        ],
        cost_estimate=pl.CostEstimate(
            flops=n_tiles * 2 * B * B * M * 3,
            bytes_accessed=slots * chunk[0] * B * 4,
            transcendentals=n_tiles * 2 * B,
        ),
        compiler_params=pltpu.CompilerParams(collective_id=0, has_side_effects=True),
    )(tiles, piece)


def on_device(series, tile_list):
    piece = series.shape[0]
    col_count = lax.axis_size("cols")
    n_rows = lax.axis_size("rows")
    result = fused_call(tile_list, series.reshape(SPILL, B), n_rows, col_count)
    return jnp.maximum(result, jnp.float32(-1.0)).reshape(piece)


def solution(mesh):
    in_specs = (P(("rows", "cols")), P(None, "rows"))
    out_specs = P(("rows", "cols"))
    return jax.shard_map(
        on_device, mesh=mesh, in_specs=in_specs, out_specs=out_specs, check_vma=False
    )
```

```python
import math

import jax
import jax.numpy as jnp
from jax import lax
from jax.experimental import pallas as pl
from jax.experimental.pallas import tpu as pltpu
from jax.sharding import PartitionSpec as P

M = 256
B = 512
BPR = 128
EXCL = 64
SPILL = 8
SEG = B + M
MESH = pl.DeviceIdType.MESH


def passed_along(block, axis, distance):
    devices = range(lax.axis_size(axis))
    route = [(i - distance, i) for i in devices if i - distance in devices]
    return lax.ppermute(block, axis, route)


def windows(held, b):
    seg = jnp.concatenate([held[pl.ds(b, 1), :], held[pl.ds(b + 1, 1), :][:, :M]], axis=1)
    parts = []
    for m in range(B // 128):
        lo = 3 * 128 - 128 * m
        sub = jnp.broadcast_to(seg[:, lo:lo + 3 * 128], (128, 3 * 128))
        parts.append(pltpu.roll(sub, 1, 1, stride=1, stride_axis=0)[:, 128:])
    w = jnp.concatenate(parts, axis=0)
    centre = w - jnp.mean(w, axis=1, keepdims=True)
    spread = jnp.mean(centre * centre, axis=1, keepdims=True)
    factor = lax.rsqrt(spread + 1e-05) / math.sqrt(M)
    return centre * factor


def split_dot(a, b):
    a_hi = a.astype(jnp.bfloat16)
    b_hi = b.astype(jnp.bfloat16)
    a_lo = (a - a_hi.astype(jnp.float32)).astype(jnp.bfloat16)
    b_lo = (b - b_hi.astype(jnp.float32)).astype(jnp.bfloat16)
    dims = (((1,), (1,)), ((), ()))

    def dot(x, y):
        return lax.dot_general(x, y, dims, preferred_element_type=jnp.float32)

    return dot(a_hi, b_hi) + (dot(a_hi, b_lo) + dot(a_lo, b_hi))


def greet_partners(n_rows, n_cols):
    g = lax.axis_index("rows")
    c = lax.axis_index("cols")
    barrier = pltpu.get_barrier_semaphore()
    half = (c // 2) % 2
    for p in range(n_cols):
        @pl.when(p != c)
        def _():
            pl.semaphore_signal(barrier, 1, device_id=(g, p), device_id_type=MESH)

    has_next = g + 1 < n_rows

    @pl.when(has_next)
    def _():
        pl.semaphore_signal(barrier, 1, device_id=(g + 1, 0), device_id_type=MESH)

    down = jnp.logical_and(c == 0, g > 0)

    @pl.when(down)
    def _():
        for p in range(n_cols):
            pl.semaphore_signal(barrier, 1, device_id=(g - 1, p), device_id_type=MESH)

    collector = jnp.logical_or(c == 0, c == 2)
    up = jnp.logical_and(collector, has_next)
    count = (n_cols - 1) + has_next.astype(jnp.int32) + n_cols * down.astype(jnp.int32)
    pl.semaphore_wait(barrier, count)
    return g, c, half, collector, up, down


def half_peers(n_cols, c, half):
    return [
        (p, jnp.logical_and(p != c, (p // 2) % 2 == half)) for p in range(n_cols)
    ]


def fused_kernel(n_rows, n_cols, n_tiles, tiles_ref, piece_ref, out_ref,
                 held, res, spill_out, spills, g_send, g_recv, r_send, r_recv, s_send, s_recv):
    spills[...] = jnp.full(spills.shape, -1.0, jnp.float32)
    g, c, half, collector, up, down = greet_partners(n_rows, n_cols)
    mate = c ^ 2
    head = n_cols
    rows = SPILL
    peers = half_peers(n_cols, c, half)

    def slab(ref, k):
        if isinstance(k, int):
            return ref.at[pl.ds(k * rows, rows)]
        return ref.at[pl.ds(pl.multiple_of(k * rows, rows), rows)]

    def remote(src, slot, sem, device):
        return pltpu.make_async_remote_copy(
            src_ref=src,
            dst_ref=slab(held, slot),
            send_sem=g_send.at[sem],
            recv_sem=g_recv.at[slot],
            device_id=device,
            device_id_type=MESH,
        )

    to_mate = remote(piece_ref, c, 0, (g, mate))
    to_mate.start()

    @pl.when(down)
    def _():
        remote(piece_ref, head, 1, (g - 1, 0)).start()
        remote(piece_ref, head, 2, (g - 1, 2)).start()

    @pl.when(g + 1 == n_rows)
    def _():
        held[pl.ds(head * rows, rows), :] = jnp.zeros(piece_ref.shape, jnp.float32)

    remote(piece_ref, mate, 0, (g, mate)).wait_recv()

    @pl.when(up)
    def _():
        remote(piece_ref, head, 1, (g + 1, 0)).wait_recv()

    for p, live in peers:
        @pl.when(live)
        def _():
            remote(piece_ref, c, 3 + 3 * p, (g, p)).start()
            remote(slab(held, mate), mate, 4 + 3 * p, (g, p)).start()

        @pl.when(jnp.logical_and(live, up))
        def _():
            remote(slab(held, head), head, 5 + 3 * p, (g, p)).start()

    held[pl.ds(pl.multiple_of(c * rows, rows), rows), :] = piece_ref[...]

    for p, live in peers:
        @pl.when(live)
        def _():
            remote(piece_ref, p, 3 + 3 * p, (g, p)).wait_recv()
            remote(piece_ref, p ^ 2, 3 + 3 * p, (g, p)).wait_recv()

    @pl.when(jnp.logical_and(jnp.logical_not(collector), g + 1 < n_rows))
    def _():
        remote(piece_ref, head, 1, (g, 0)).wait_recv()

    def result_copy(p, sender, t):
        return pltpu.make_async_remote_copy(
            src_ref=res.at[sender, t],
            dst_ref=res.at[sender, t],
            send_sem=r_send.at[p],
            recv_sem=r_recv.at[sender],
            device_id=(g, p),
            device_id_type=MESH,
        )

    def all_results(p, sender):
        return pltpu.make_async_remote_copy(
            src_ref=res.at[sender],
            dst_ref=res.at[sender],
            send_sem=r_send.at[p],
            recv_sem=r_recv.at[sender],
            device_id=(g, p),
            device_id_type=MESH,
        )

    r_i = lax.broadcasted_iota(jnp.int32, (B, B), 0)
    r_j = lax.broadcasted_iota(jnp.int32, (B, B), 1)
    flip = r_i + r_j == B - 1

    def body(t, carry):
        col = c + n_cols * t
        i = jnp.clip(tiles_ref[0, col] - g * BPR, 0, BPR - 1)
        d = jnp.clip(tiles_ref[1, col], 0, SPILL - 1)
        j = i + d
        zl = windows(held, i)
        zr = windows(held, j)
        corr = split_dot(zl, zr)
        corr = jnp.where(d * B + r_i - r_j >= EXCL, corr, jnp.float32(-1.0))
        row_c = jnp.max(corr, axis=1, keepdims=True)
        row_max = jnp.sum(jnp.where(flip, row_c, 0.0), axis=0, keepdims=True)
        col_r = jnp.max(corr, axis=0, keepdims=True)
        col_c = jnp.sum(jnp.where(flip, col_r, 0.0), axis=1, keepdims=True)
        col_max = jnp.sum(jnp.where(r_i == r_j, col_c, 0.0), axis=0, keepdims=True)
        sub = lax.broadcasted_iota(jnp.int32, (8, 128), 0)
        slab_v = jnp.full((8, 128), -1.0, jnp.float32)
        for v in range(B // 128):
            slab_v = jnp.where(sub == v, row_max[:, v * 128:(v + 1) * 128], slab_v)
            slab_v = jnp.where(sub == 4 + v, col_max[:, v * 128:(v + 1) * 128], slab_v)
        res[c, t] = slab_v
        for p in range(n_cols):
            @pl.when(p != c)
            def _():
                result_copy(p, c, t).start()
        return carry

    lax.fori_loop(0, n_tiles, body, 0)

    has_next = g + 1 < n_rows
    sub = lax.broadcasted_iota(jnp.int32, (8, 128), 0)
    top = sub < 4

    def gather_blocks(senders, base, acc):
        for sender, t in senders:
            col = sender + n_cols * t
            i = jnp.clip(tiles_ref[0, col] - g * BPR, 0, BPR - 1) - base
            j = i + jnp.clip(tiles_ref[1, col], 0, SPILL - 1)
            slab_v = res[sender, t]
            flipped = pltpu.roll(slab_v, 4, 0)
            for m in range(len(acc)):
                even, odd = 2 * m, 2 * m + 1
                take = jnp.logical_or(jnp.logical_and(top, i == even), jnp.logical_and(jnp.logical_not(top), j == odd))
                take_f = jnp.logical_or(jnp.logical_and(jnp.logical_not(top), i == odd), jnp.logical_and(top, j == even))
                acc[m] = jnp.maximum(acc[m], jnp.maximum(
                    jnp.where(take, slab_v, jnp.float32(-1.0)),
                    jnp.where(take_f, flipped, jnp.float32(-1.0))))
        return acc

    quads = SPILL // 2
    spill_acc = gather_blocks([(c, t) for t in range(n_tiles)], BPR,
                              [jnp.full((8, 128), -1.0, jnp.float32) for _ in range(quads)])
    for m in range(quads):
        spill_out[pl.ds(8 * m, 8), :] = spill_acc[m]

    def spill_up():
        return pltpu.make_async_remote_copy(
            src_ref=spill_out,
            dst_ref=spills.at[c],
            send_sem=s_send.at[0],
            recv_sem=s_recv.at[0],
            device_id=(g + 1, 0),
            device_id_type=MESH,
        )

    @pl.when(has_next)
    def _():
        spill_up().start()

    for p in range(n_cols):
        @pl.when(p != c)
        def _():
            all_results(p, p).wait_recv()

    @pl.when(down)
    def _():
        pltpu.make_async_remote_copy(
            src_ref=spills,
            dst_ref=spills,
            send_sem=s_send.at[0],
            recv_sem=s_recv.at[0],
            device_id=(g - 1, 0),
            device_id_type=MESH,
        ).wait_recv()

    base = c * SPILL
    acc = [jnp.full((8, 128), -1.0, jnp.float32) for _ in range(quads)]
    for sender in range(n_cols):
        acc = gather_blocks([(sender, t) for t in range(n_tiles)], base, acc)
    spilled = jnp.max(spills[...], axis=0)
    for m in range(quads):
        out_ref[pl.ds(8 * m, 8), :] = jnp.maximum(acc[m], spilled[8 * m:8 * m + 8])

    to_mate.wait_send()

    @pl.when(down)
    def _():
        remote(piece_ref, head, 1, (g - 1, 0)).wait_send()
        remote(piece_ref, head, 2, (g - 1, 2)).wait_send()

    for p, live in peers:
        @pl.when(live)
        def _():
            remote(piece_ref, c, 3 + 3 * p, (g, p)).wait_send()
            remote(piece_ref, c, 4 + 3 * p, (g, p)).wait_send()

        @pl.when(jnp.logical_and(live, up))
        def _():
            remote(piece_ref, c, 5 + 3 * p, (g, p)).wait_send()

    for p in range(n_cols):
        @pl.when(p != c)
        def _():
            all_results(p, c).wait_send()

    @pl.when(has_next)
    def _():
        spill_up().wait_send()


def fused_call(tiles, piece, n_rows, n_cols):
    n_tiles = tiles.shape[1] // n_cols
    slots = n_cols + 1
    chunk = piece.shape
    return pl.pallas_call(
        lambda *refs: fused_kernel(n_rows, n_cols, n_tiles, *refs),
        out_shape=jax.ShapeDtypeStruct((chunk[0] * chunk[1] // 128, 128), jnp.float32),
        in_specs=[
            pl.BlockSpec(memory_space=pltpu.SMEM),
            pl.BlockSpec(memory_space=pltpu.VMEM),
        ],
        out_specs=pl.BlockSpec(memory_space=pltpu.VMEM),
        scratch_shapes=[
            pltpu.VMEM((slots * chunk[0], B), jnp.float32),
            pltpu.VMEM((n_cols, n_tiles, 8, 128), jnp.float32),
            pltpu.VMEM((chunk[0] * chunk[1] // 128, 128), jnp.float32),
            pltpu.VMEM((n_cols, chunk[0] * chunk[1] // 128, 128), jnp.float32),
            pltpu.SemaphoreType.DMA((3 + 3 * n_cols,)),
            pltpu.SemaphoreType.DMA((slots,)),
            pltpu.SemaphoreType.DMA((n_cols,)),
            pltpu.SemaphoreType.DMA((n_cols,)),
            pltpu.SemaphoreType.DMA((1,)),
            pltpu.SemaphoreType.DMA((1,)),
        ],
        cost_estimate=pl.CostEstimate(
            flops=n_tiles * 2 * B * B * M * 3,
            bytes_accessed=slots * chunk[0] * B * 4,
            transcendentals=n_tiles * 2 * B,
        ),
        compiler_params=pltpu.CompilerParams(collective_id=0, has_side_effects=True),
    )(tiles, piece)


def on_device(series, tile_list):
    piece = series.shape[0]
    col_count = lax.axis_size("cols")
    n_rows = lax.axis_size("rows")
    result = fused_call(tile_list, series.reshape(SPILL, B), n_rows, col_count)
    return jnp.maximum(result, jnp.float32(-1.0)).reshape(piece)


def solution(mesh):
    in_specs = (P(("rows", "cols")), P(None, "rows"))
    out_specs = P(("rows", "cols"))
    return jax.shard_map(
        on_device, mesh=mesh, in_specs=in_specs, out_specs=out_specs, check_vma=False
    )
```

```python
import math

import jax
import jax.numpy as jnp
from jax import lax
from jax.experimental import pallas as pl
from jax.experimental.pallas import tpu as pltpu
from jax.sharding import PartitionSpec as P

M = 256
B = 512
BPR = 128
EXCL = 64
SPILL = 8
SEG = B + M
MESH = pl.DeviceIdType.MESH


def passed_along(block, axis, distance):
    devices = range(lax.axis_size(axis))
    route = [(i - distance, i) for i in devices if i - distance in devices]
    return lax.ppermute(block, axis, route)


def windows(held, b):
    per = B // 128
    seg = jnp.concatenate([held[pl.ds(b * per + v, 1), :] for v in range(SEG // 128)], axis=1)
    parts = []
    for m in range(B // 128):
        lo = 3 * 128 - 128 * m
        sub = jnp.broadcast_to(seg[:, lo:lo + 3 * 128], (128, 3 * 128))
        parts.append(pltpu.roll(sub, 1, 1, stride=1, stride_axis=0)[:, 128:])
    w = jnp.concatenate(parts, axis=0)
    centre = w - jnp.mean(w, axis=1, keepdims=True)
    spread = jnp.mean(centre * centre, axis=1, keepdims=True)
    factor = lax.rsqrt(spread + 1e-05) / math.sqrt(M)
    return centre * factor


def split_dot(a, b):
    a_hi = a.astype(jnp.bfloat16)
    b_hi = b.astype(jnp.bfloat16)
    a_lo = (a - a_hi.astype(jnp.float32)).astype(jnp.bfloat16)
    b_lo = (b - b_hi.astype(jnp.float32)).astype(jnp.bfloat16)
    dims = (((1,), (1,)), ((), ()))

    def dot(x, y):
        return lax.dot_general(x, y, dims, preferred_element_type=jnp.float32)

    return dot(a_hi, b_hi) + (dot(a_hi, b_lo) + dot(a_lo, b_hi))


def greet_partners(n_rows, n_cols):
    g = lax.axis_index("rows")
    c = lax.axis_index("cols")
    barrier = pltpu.get_barrier_semaphore()
    half = (c // 2) % 2
    for p in range(n_cols):
        @pl.when(p != c)
        def _():
            pl.semaphore_signal(barrier, 1, device_id=(g, p), device_id_type=MESH)

    has_next = g + 1 < n_rows

    @pl.when(has_next)
    def _():
        pl.semaphore_signal(barrier, 1, device_id=(g + 1, 0), device_id_type=MESH)

    down = jnp.logical_and(c == 0, g > 0)

    @pl.when(down)
    def _():
        for p in range(n_cols):
            pl.semaphore_signal(barrier, 1, device_id=(g - 1, p), device_id_type=MESH)

    collector = jnp.logical_or(c == 0, c == 2)
    up = jnp.logical_and(collector, has_next)
    count = (n_cols - 1) + has_next.astype(jnp.int32) + n_cols * down.astype(jnp.int32)
    pl.semaphore_wait(barrier, count)
    return g, c, half, collector, up, down


def half_peers(n_cols, c, half):
    return [
        (p, jnp.logical_and(p != c, (p // 2) % 2 == half)) for p in range(n_cols)
    ]


def fused_kernel(n_rows, n_cols, n_tiles, tiles_ref, piece_ref, out_ref,
                 held, res, spill_out, spills, g_send, g_recv, r_send, r_recv, s_send, s_recv):
    spills[...] = jnp.full(spills.shape, -1.0, jnp.float32)
    g, c, half, collector, up, down = greet_partners(n_rows, n_cols)
    mate = c ^ 2
    head = n_cols
    rows = SPILL * B // 128
    peers = half_peers(n_cols, c, half)

    def slab(ref, k):
        if isinstance(k, int):
            return ref.at[pl.ds(k * rows, rows)]
        return ref.at[pl.ds(pl.multiple_of(k * rows, rows), rows)]

    def remote(src, slot, sem, device):
        return pltpu.make_async_remote_copy(
            src_ref=src,
            dst_ref=slab(held, slot),
            send_sem=g_send.at[sem],
            recv_sem=g_recv.at[slot],
            device_id=device,
            device_id_type=MESH,
        )

    to_mate = remote(piece_ref, c, 0, (g, mate))
    to_mate.start()

    @pl.when(down)
    def _():
        remote(piece_ref, head, 1, (g - 1, 0)).start()
        remote(piece_ref, head, 2, (g - 1, 2)).start()

    @pl.when(g + 1 == n_rows)
    def _():
        held[pl.ds(head * rows, rows), :] = jnp.zeros(piece_ref.shape, jnp.float32)

    remote(piece_ref, mate, 0, (g, mate)).wait_recv()

    @pl.when(up)
    def _():
        remote(piece_ref, head, 1, (g + 1, 0)).wait_recv()

    for p, live in peers:
        @pl.when(live)
        def _():
            remote(piece_ref, c, 3 + 3 * p, (g, p)).start()
            remote(slab(held, mate), mate, 4 + 3 * p, (g, p)).start()

        @pl.when(jnp.logical_and(live, up))
        def _():
            remote(slab(held, head), head, 5 + 3 * p, (g, p)).start()

    held[pl.ds(pl.multiple_of(c * rows, rows), rows), :] = piece_ref[...]

    for p, live in peers:
        @pl.when(live)
        def _():
            remote(piece_ref, p, 3 + 3 * p, (g, p)).wait_recv()
            remote(piece_ref, p ^ 2, 3 + 3 * p, (g, p)).wait_recv()

    @pl.when(jnp.logical_and(jnp.logical_not(collector), g + 1 < n_rows))
    def _():
        remote(piece_ref, head, 1, (g, 0)).wait_recv()

    def result_copy(p, sender, t):
        return pltpu.make_async_remote_copy(
            src_ref=res.at[sender, t],
            dst_ref=res.at[sender, t],
            send_sem=r_send.at[p],
            recv_sem=r_recv.at[sender],
            device_id=(g, p),
            device_id_type=MESH,
        )

    def all_results(p, sender):
        return pltpu.make_async_remote_copy(
            src_ref=res.at[sender],
            dst_ref=res.at[sender],
            send_sem=r_send.at[p],
            recv_sem=r_recv.at[sender],
            device_id=(g, p),
            device_id_type=MESH,
        )

    r_i = lax.broadcasted_iota(jnp.int32, (B, B), 0)
    r_j = lax.broadcasted_iota(jnp.int32, (B, B), 1)
    flip = r_i + r_j == B - 1

    def body(t, carry):
        col = c + n_cols * t
        i = jnp.clip(tiles_ref[0, col] - g * BPR, 0, BPR - 1)
        d = jnp.clip(tiles_ref[1, col], 0, SPILL - 1)
        j = i + d
        zl = windows(held, i)
        zr = windows(held, j)
        corr = split_dot(zl, zr)
        corr = jnp.where(d * B + r_i - r_j >= EXCL, corr, jnp.float32(-1.0))
        row_c = jnp.max(corr, axis=1, keepdims=True)
        row_max = jnp.sum(jnp.where(flip, row_c, 0.0), axis=0, keepdims=True)
        col_r = jnp.max(corr, axis=0, keepdims=True)
        col_c = jnp.sum(jnp.where(flip, col_r, 0.0), axis=1, keepdims=True)
        col_max = jnp.sum(jnp.where(r_i == r_j, col_c, 0.0), axis=0, keepdims=True)
        sub = lax.broadcasted_iota(jnp.int32, (8, 128), 0)
        slab_v = jnp.full((8, 128), -1.0, jnp.float32)
        for v in range(B // 128):
            slab_v = jnp.where(sub == v, row_max[:, v * 128:(v + 1) * 128], slab_v)
            slab_v = jnp.where(sub == 4 + v, col_max[:, v * 128:(v + 1) * 128], slab_v)
        res[c, t] = slab_v
        for p in range(n_cols):
            @pl.when(p != c)
            def _():
                result_copy(p, c, t).start()
        return carry

    lax.fori_loop(0, n_tiles, body, 0)

    has_next = g + 1 < n_rows
    sub = lax.broadcasted_iota(jnp.int32, (8, 128), 0)
    top = sub < 4

    def gather_blocks(senders, base, acc):
        for sender, t in senders:
            col = sender + n_cols * t
            i = jnp.clip(tiles_ref[0, col] - g * BPR, 0, BPR - 1) - base
            j = i + jnp.clip(tiles_ref[1, col], 0, SPILL - 1)
            slab_v = res[sender, t]
            flipped = pltpu.roll(slab_v, 4, 0)
            for m in range(len(acc)):
                even, odd = 2 * m, 2 * m + 1
                take = jnp.logical_or(jnp.logical_and(top, i == even), jnp.logical_and(jnp.logical_not(top), j == odd))
                take_f = jnp.logical_or(jnp.logical_and(jnp.logical_not(top), i == odd), jnp.logical_and(top, j == even))
                acc[m] = jnp.maximum(acc[m], jnp.maximum(
                    jnp.where(take, slab_v, jnp.float32(-1.0)),
                    jnp.where(take_f, flipped, jnp.float32(-1.0))))
        return acc

    quads = SPILL // 2
    spill_acc = gather_blocks([(c, t) for t in range(n_tiles)], BPR,
                              [jnp.full((8, 128), -1.0, jnp.float32) for _ in range(quads)])
    for m in range(quads):
        spill_out[pl.ds(8 * m, 8), :] = spill_acc[m]

    def spill_up():
        return pltpu.make_async_remote_copy(
            src_ref=spill_out,
            dst_ref=spills.at[c],
            send_sem=s_send.at[0],
            recv_sem=s_recv.at[0],
            device_id=(g + 1, 0),
            device_id_type=MESH,
        )

    @pl.when(has_next)
    def _():
        spill_up().start()

    for p in range(n_cols):
        @pl.when(p != c)
        def _():
            all_results(p, p).wait_recv()

    @pl.when(down)
    def _():
        pltpu.make_async_remote_copy(
            src_ref=spills,
            dst_ref=spills,
            send_sem=s_send.at[0],
            recv_sem=s_recv.at[0],
            device_id=(g - 1, 0),
            device_id_type=MESH,
        ).wait_recv()

    base = c * SPILL
    acc = [jnp.full((8, 128), -1.0, jnp.float32) for _ in range(quads)]
    for sender in range(n_cols):
        acc = gather_blocks([(sender, t) for t in range(n_tiles)], base, acc)
    spilled = jnp.max(spills[...], axis=0)
    for m in range(quads):
        out_ref[pl.ds(8 * m, 8), :] = jnp.maximum(acc[m], spilled[8 * m:8 * m + 8])

    to_mate.wait_send()

    @pl.when(down)
    def _():
        remote(piece_ref, head, 1, (g - 1, 0)).wait_send()
        remote(piece_ref, head, 2, (g - 1, 2)).wait_send()

    for p, live in peers:
        @pl.when(live)
        def _():
            remote(piece_ref, c, 3 + 3 * p, (g, p)).wait_send()
            remote(piece_ref, c, 4 + 3 * p, (g, p)).wait_send()

        @pl.when(jnp.logical_and(live, up))
        def _():
            remote(piece_ref, c, 5 + 3 * p, (g, p)).wait_send()

    for p in range(n_cols):
        @pl.when(p != c)
        def _():
            all_results(p, c).wait_send()

    @pl.when(has_next)
    def _():
        spill_up().wait_send()


def fused_call(tiles, piece, n_rows, n_cols):
    n_tiles = tiles.shape[1] // n_cols
    slots = n_cols + 1
    chunk = piece.shape
    return pl.pallas_call(
        lambda *refs: fused_kernel(n_rows, n_cols, n_tiles, *refs),
        out_shape=jax.ShapeDtypeStruct(chunk, jnp.float32),
        in_specs=[
            pl.BlockSpec(memory_space=pltpu.SMEM),
            pl.BlockSpec(memory_space=pltpu.VMEM),
        ],
        out_specs=pl.BlockSpec(memory_space=pltpu.VMEM),
        scratch_shapes=[
            pltpu.VMEM((slots * chunk[0], 128), jnp.float32),
            pltpu.VMEM((n_cols, n_tiles, 8, 128), jnp.float32),
            pltpu.VMEM(chunk, jnp.float32),
            pltpu.VMEM((n_cols,) + chunk, jnp.float32),
            pltpu.SemaphoreType.DMA((3 + 3 * n_cols,)),
            pltpu.SemaphoreType.DMA((slots,)),
            pltpu.SemaphoreType.DMA((n_cols,)),
            pltpu.SemaphoreType.DMA((n_cols,)),
            pltpu.SemaphoreType.DMA((1,)),
            pltpu.SemaphoreType.DMA((1,)),
        ],
        cost_estimate=pl.CostEstimate(
            flops=n_tiles * 2 * B * B * M * 3,
            bytes_accessed=slots * chunk[0] * 128 * 4,
            transcendentals=n_tiles * 2 * B,
        ),
        compiler_params=pltpu.CompilerParams(collective_id=0, has_side_effects=True),
    )(tiles, piece)


def on_device(series, tile_list):
    piece = series.shape[0]
    col_count = lax.axis_size("cols")
    n_rows = lax.axis_size("rows")
    result = fused_call(tile_list, series.reshape(piece // 128, 128), n_rows, col_count)
    return jnp.maximum(result, jnp.float32(-1.0)).reshape(piece)


def solution(mesh):
    in_specs = (P(("rows", "cols")), P(None, "rows"))
    out_specs = P(("rows", "cols"))
    return jax.shard_map(
        on_device, mesh=mesh, in_specs=in_specs, out_specs=out_specs, check_vma=False
    )
```

```python
import math

import jax
import jax.numpy as jnp
from jax import lax
from jax.experimental import pallas as pl
from jax.experimental.pallas import tpu as pltpu
from jax.sharding import PartitionSpec as P

M = 256
B = 512
BPR = 128
EXCL = 64
SPILL = 8
SEG = B + M
MESH = pl.DeviceIdType.MESH


def passed_along(block, axis, distance):
    devices = range(lax.axis_size(axis))
    route = [(i - distance, i) for i in devices if i - distance in devices]
    return lax.ppermute(block, axis, route)


def windows(held, b):
    per = B // 128
    seg = jnp.concatenate([held[pl.ds(b * per + v, 1), :] for v in range(SEG // 128)], axis=1)
    parts = []
    for m in range(B // 128):
        lo = 3 * 128 - 128 * m
        sub = jnp.broadcast_to(seg[:, lo:lo + 3 * 128], (128, 3 * 128))
        parts.append(pltpu.roll(sub, 1, 1, stride=1, stride_axis=0)[:, 128:])
    w = jnp.concatenate(parts, axis=0)
    centre = w - jnp.mean(w, axis=1, keepdims=True)
    spread = jnp.mean(centre * centre, axis=1, keepdims=True)
    factor = lax.rsqrt(spread + 1e-05) / math.sqrt(M)
    return centre * factor


def split_dot(a, b):
    a_hi = a.astype(jnp.bfloat16)
    b_hi = b.astype(jnp.bfloat16)
    a_lo = (a - a_hi.astype(jnp.float32)).astype(jnp.bfloat16)
    b_lo = (b - b_hi.astype(jnp.float32)).astype(jnp.bfloat16)
    dims = (((1,), (1,)), ((), ()))

    def dot(x, y):
        return lax.dot_general(x, y, dims, preferred_element_type=jnp.float32)

    return dot(a_hi, b_hi) + (dot(a_hi, b_lo) + dot(a_lo, b_hi))


def greet_partners(n_rows, n_cols):
    g = lax.axis_index("rows")
    c = lax.axis_index("cols")
    barrier = pltpu.get_barrier_semaphore()
    half = (c // 2) % 2
    for p in range(n_cols):
        @pl.when(p != c)
        def _():
            pl.semaphore_signal(barrier, 1, device_id=(g, p), device_id_type=MESH)

    has_next = g + 1 < n_rows

    @pl.when(has_next)
    def _():
        pl.semaphore_signal(barrier, 1, device_id=(g + 1, 0), device_id_type=MESH)

    down = jnp.logical_and(c == 0, g > 0)

    @pl.when(down)
    def _():
        for p in range(n_cols):
            pl.semaphore_signal(barrier, 1, device_id=(g - 1, p), device_id_type=MESH)

    collector = jnp.logical_or(c == 0, c == 2)
    up = jnp.logical_and(collector, has_next)
    count = (n_cols - 1) + has_next.astype(jnp.int32) + n_cols * down.astype(jnp.int32)
    pl.semaphore_wait(barrier, count)
    return g, c, half, collector, up, down


def half_peers(n_cols, c, half):
    return [
        (p, jnp.logical_and(p != c, (p // 2) % 2 == half)) for p in range(n_cols)
    ]


def fused_kernel(n_rows, n_cols, n_tiles, tiles_ref, piece_ref, out_ref,
                 held, res, spill_out, spills, g_send, g_recv, r_send, r_recv, s_send, s_recv):
    spills[...] = jnp.full(spills.shape, -1.0, jnp.float32)
    g, c, half, collector, up, down = greet_partners(n_rows, n_cols)
    mate = c ^ 2
    head = n_cols
    rows = SPILL * B // 128
    peers = half_peers(n_cols, c, half)

    def slab(ref, k):
        if isinstance(k, int):
            return ref.at[pl.ds(k * rows, rows)]
        return ref.at[pl.ds(pl.multiple_of(k * rows, rows), rows)]

    def remote(src, slot, sem, device):
        return pltpu.make_async_remote_copy(
            src_ref=src,
            dst_ref=slab(held, slot),
            send_sem=g_send.at[sem],
            recv_sem=g_recv.at[slot],
            device_id=device,
            device_id_type=MESH,
        )

    to_mate = remote(piece_ref, c, 0, (g, mate))
    to_mate.start()

    @pl.when(down)
    def _():
        remote(piece_ref, head, 1, (g - 1, 0)).start()
        remote(piece_ref, head, 2, (g - 1, 2)).start()

    @pl.when(g + 1 == n_rows)
    def _():
        held[pl.ds(head * rows, rows), :] = jnp.zeros(piece_ref.shape, jnp.float32)

    remote(piece_ref, mate, 0, (g, mate)).wait_recv()

    @pl.when(up)
    def _():
        remote(piece_ref, head, 1, (g + 1, 0)).wait_recv()

    for p, live in peers:
        @pl.when(live)
        def _():
            remote(piece_ref, c, 3 + 3 * p, (g, p)).start()
            remote(slab(held, mate), mate, 4 + 3 * p, (g, p)).start()

        @pl.when(jnp.logical_and(live, up))
        def _():
            remote(slab(held, head), head, 5 + 3 * p, (g, p)).start()

    held[pl.ds(pl.multiple_of(c * rows, rows), rows), :] = piece_ref[...]

    for p, live in peers:
        @pl.when(live)
        def _():
            remote(piece_ref, p, 3 + 3 * p, (g, p)).wait_recv()
            remote(piece_ref, p ^ 2, 3 + 3 * p, (g, p)).wait_recv()

    @pl.when(jnp.logical_and(jnp.logical_not(collector), g + 1 < n_rows))
    def _():
        remote(piece_ref, head, 1, (g, 0)).wait_recv()

    def result_copy(p, sender, t):
        return pltpu.make_async_remote_copy(
            src_ref=res.at[sender, t],
            dst_ref=res.at[sender, t],
            send_sem=r_send.at[p],
            recv_sem=r_recv.at[sender],
            device_id=(g, p),
            device_id_type=MESH,
        )

    def all_results(p, sender):
        return pltpu.make_async_remote_copy(
            src_ref=res.at[sender],
            dst_ref=res.at[sender],
            send_sem=r_send.at[p],
            recv_sem=r_recv.at[sender],
            device_id=(g, p),
            device_id_type=MESH,
        )

    r_i = lax.broadcasted_iota(jnp.int32, (B, B), 0)
    r_j = lax.broadcasted_iota(jnp.int32, (B, B), 1)
    flip = r_i + r_j == B - 1

    def body(t, carry):
        col = c + n_cols * t
        i = jnp.clip(tiles_ref[0, col] - g * BPR, 0, BPR - 1)
        d = jnp.clip(tiles_ref[1, col], 0, SPILL - 1)
        j = i + d
        zl = windows(held, i)
        zr = windows(held, j)
        corr = split_dot(zl, zr)
        corr = jnp.where(d * B + r_i - r_j >= EXCL, corr, jnp.float32(-1.0))
        row_c = jnp.max(corr, axis=1, keepdims=True)
        row_max = jnp.sum(jnp.where(flip, row_c, 0.0), axis=0, keepdims=True)
        col_r = jnp.max(corr, axis=0, keepdims=True)
        col_c = jnp.sum(jnp.where(flip, col_r, 0.0), axis=1, keepdims=True)
        col_max = jnp.sum(jnp.where(r_i == r_j, col_c, 0.0), axis=0, keepdims=True)
        sub = lax.broadcasted_iota(jnp.int32, (8, 128), 0)
        slab_v = jnp.full((8, 128), -1.0, jnp.float32)
        for v in range(B // 128):
            slab_v = jnp.where(sub == v, row_max[:, v * 128:(v + 1) * 128], slab_v)
            slab_v = jnp.where(sub == 4 + v, col_max[:, v * 128:(v + 1) * 128], slab_v)
        res[c, t] = slab_v
        for p in range(n_cols):
            @pl.when(p != c)
            def _():
                result_copy(p, c, t).start()
        return carry

    lax.fori_loop(0, n_tiles, body, 0)

    has_next = g + 1 < n_rows
    sub = lax.broadcasted_iota(jnp.int32, (8, 128), 0)
    top = sub < 4

    def gather_blocks(senders, base, acc):
        for sender, t in senders:
            col = sender + n_cols * t
            i = jnp.clip(tiles_ref[0, col] - g * BPR, 0, BPR - 1) - base
            j = i + jnp.clip(tiles_ref[1, col], 0, SPILL - 1)
            slab_v = res[sender, t]
            flipped = pltpu.roll(slab_v, 4, 0)
            for m in range(len(acc)):
                even, odd = 2 * m, 2 * m + 1
                take = jnp.logical_or(jnp.logical_and(top, i == even), jnp.logical_and(jnp.logical_not(top), j == odd))
                take_f = jnp.logical_or(jnp.logical_and(jnp.logical_not(top), i == odd), jnp.logical_and(top, j == even))
                acc[m] = jnp.maximum(acc[m], jnp.maximum(
                    jnp.where(take, slab_v, jnp.float32(-1.0)),
                    jnp.where(take_f, flipped, jnp.float32(-1.0))))
        return acc

    quads = SPILL // 2
    spill_acc = gather_blocks([(c, t) for t in range(n_tiles)], BPR,
                              [jnp.full((8, 128), -1.0, jnp.float32) for _ in range(quads)])
    for m in range(quads):
        spill_out[pl.ds(8 * m, 8), :] = spill_acc[m]

    def spill_up():
        return pltpu.make_async_remote_copy(
            src_ref=spill_out,
            dst_ref=spills.at[c],
            send_sem=s_send.at[0],
            recv_sem=s_recv.at[0],
            device_id=(g + 1, 0),
            device_id_type=MESH,
        )

    @pl.when(has_next)
    def _():
        spill_up().start()


    base = c * SPILL
    acc = [jnp.full((8, 128), -1.0, jnp.float32) for _ in range(quads)]
    for sender in range(n_cols):
        @pl.when(sender != c)
        def _():
            all_results(sender, sender).wait_recv()

        acc = gather_blocks([(sender, t) for t in range(n_tiles)], base, acc)

    @pl.when(down)
    def _():
        pltpu.make_async_remote_copy(
            src_ref=spills,
            dst_ref=spills,
            send_sem=s_send.at[0],
            recv_sem=s_recv.at[0],
            device_id=(g - 1, 0),
            device_id_type=MESH,
        ).wait_recv()

    spilled = jnp.max(spills[...], axis=0)
    for m in range(quads):
        out_ref[pl.ds(8 * m, 8), :] = jnp.maximum(acc[m], spilled[8 * m:8 * m + 8])

    to_mate.wait_send()

    @pl.when(down)
    def _():
        remote(piece_ref, head, 1, (g - 1, 0)).wait_send()
        remote(piece_ref, head, 2, (g - 1, 2)).wait_send()

    for p, live in peers:
        @pl.when(live)
        def _():
            remote(piece_ref, c, 3 + 3 * p, (g, p)).wait_send()
            remote(piece_ref, c, 4 + 3 * p, (g, p)).wait_send()

        @pl.when(jnp.logical_and(live, up))
        def _():
            remote(piece_ref, c, 5 + 3 * p, (g, p)).wait_send()

    for p in range(n_cols):
        @pl.when(p != c)
        def _():
            all_results(p, c).wait_send()

    @pl.when(has_next)
    def _():
        spill_up().wait_send()


def fused_call(tiles, piece, n_rows, n_cols):
    n_tiles = tiles.shape[1] // n_cols
    slots = n_cols + 1
    chunk = piece.shape
    return pl.pallas_call(
        lambda *refs: fused_kernel(n_rows, n_cols, n_tiles, *refs),
        out_shape=jax.ShapeDtypeStruct(chunk, jnp.float32),
        in_specs=[
            pl.BlockSpec(memory_space=pltpu.SMEM),
            pl.BlockSpec(memory_space=pltpu.VMEM),
        ],
        out_specs=pl.BlockSpec(memory_space=pltpu.VMEM),
        scratch_shapes=[
            pltpu.VMEM((slots * chunk[0], 128), jnp.float32),
            pltpu.VMEM((n_cols, n_tiles, 8, 128), jnp.float32),
            pltpu.VMEM(chunk, jnp.float32),
            pltpu.VMEM((n_cols,) + chunk, jnp.float32),
            pltpu.SemaphoreType.DMA((3 + 3 * n_cols,)),
            pltpu.SemaphoreType.DMA((slots,)),
            pltpu.SemaphoreType.DMA((n_cols,)),
            pltpu.SemaphoreType.DMA((n_cols,)),
            pltpu.SemaphoreType.DMA((1,)),
            pltpu.SemaphoreType.DMA((1,)),
        ],
        cost_estimate=pl.CostEstimate(
            flops=n_tiles * 2 * B * B * M * 3,
            bytes_accessed=slots * chunk[0] * 128 * 4,
            transcendentals=n_tiles * 2 * B,
        ),
        compiler_params=pltpu.CompilerParams(collective_id=0, has_side_effects=True),
    )(tiles, piece)


def on_device(series, tile_list):
    piece = series.shape[0]
    col_count = lax.axis_size("cols")
    n_rows = lax.axis_size("rows")
    result = fused_call(tile_list, series.reshape(piece // 128, 128), n_rows, col_count)
    return jnp.maximum(result, jnp.float32(-1.0)).reshape(piece)


def solution(mesh):
    in_specs = (P(("rows", "cols")), P(None, "rows"))
    out_specs = P(("rows", "cols"))
    return jax.shard_map(
        on_device, mesh=mesh, in_specs=in_specs, out_specs=out_specs, check_vma=False
    )
```

```python
import math

import jax
import jax.numpy as jnp
from jax import lax
from jax.experimental import pallas as pl
from jax.experimental.pallas import tpu as pltpu
from jax.sharding import PartitionSpec as P

M = 256
B = 512
BPR = 128
EXCL = 64
SPILL = 8
SEG = B + M
MESH = pl.DeviceIdType.MESH


def passed_along(block, axis, distance):
    devices = range(lax.axis_size(axis))
    route = [(i - distance, i) for i in devices if i - distance in devices]
    return lax.ppermute(block, axis, route)


def windows(held, b):
    per = B // 128
    seg = jnp.concatenate([held[pl.ds(b * per + v, 1), :] for v in range(SEG // 128)], axis=1)
    parts = []
    for m in range(B // 128):
        lo = 3 * 128 - 128 * m
        sub = jnp.broadcast_to(seg[:, lo:lo + 3 * 128], (128, 3 * 128))
        parts.append(pltpu.roll(sub, 1, 1, stride=1, stride_axis=0)[:, 128:])
    w = jnp.concatenate(parts, axis=0)
    centre = w - jnp.mean(w, axis=1, keepdims=True)
    spread = jnp.mean(centre * centre, axis=1, keepdims=True)
    factor = lax.rsqrt(spread + 1e-05) / math.sqrt(M)
    return centre * factor


def split_dot(a, b):
    a_hi = a.astype(jnp.bfloat16)
    b_hi = b.astype(jnp.bfloat16)
    a_lo = (a - a_hi.astype(jnp.float32)).astype(jnp.bfloat16)
    b_lo = (b - b_hi.astype(jnp.float32)).astype(jnp.bfloat16)
    dims = (((1,), (1,)), ((), ()))

    def dot(x, y):
        return lax.dot_general(x, y, dims, preferred_element_type=jnp.float32)

    return dot(a_hi, b_hi) + (dot(a_hi, b_lo) + dot(a_lo, b_hi))


def reverse_lanes(x, mirror):
    hi = x.astype(jnp.bfloat16)
    rest = x - hi.astype(jnp.float32)
    mid = rest.astype(jnp.bfloat16)
    lo = (rest - mid.astype(jnp.float32)).astype(jnp.bfloat16)

    def dot(part):
        return jnp.dot(part, mirror, preferred_element_type=jnp.float32)

    return (dot(hi) + dot(mid)) + dot(lo)


def greet_partners(n_rows, n_cols):
    g = lax.axis_index("rows")
    c = lax.axis_index("cols")
    barrier = pltpu.get_barrier_semaphore()
    half = (c // 2) % 2
    for p in range(n_cols):
        @pl.when(p != c)
        def _():
            pl.semaphore_signal(barrier, 1, device_id=(g, p), device_id_type=MESH)

    has_next = g + 1 < n_rows

    @pl.when(has_next)
    def _():
        pl.semaphore_signal(barrier, 1, device_id=(g + 1, 0), device_id_type=MESH)

    down = jnp.logical_and(c == 0, g > 0)

    @pl.when(down)
    def _():
        for p in range(n_cols):
            pl.semaphore_signal(barrier, 1, device_id=(g - 1, p), device_id_type=MESH)

    collector = jnp.logical_or(c == 0, c == 2)
    up = jnp.logical_and(collector, has_next)
    count = (n_cols - 1) + has_next.astype(jnp.int32) + n_cols * down.astype(jnp.int32)
    pl.semaphore_wait(barrier, count)
    return g, c, half, collector, up, down


def half_peers(n_cols, c, half):
    return [
        (p, jnp.logical_and(p != c, (p // 2) % 2 == half)) for p in range(n_cols)
    ]


def fused_kernel(n_rows, n_cols, n_tiles, tiles_ref, piece_ref, out_ref,
                 held, res, spill_out, spills, g_send, g_recv, r_send, r_recv, s_send, s_recv):
    spills[...] = jnp.full(spills.shape, -1.0, jnp.float32)
    g, c, half, collector, up, down = greet_partners(n_rows, n_cols)
    mate = c ^ 2
    head = n_cols
    rows = SPILL * B // 128
    peers = half_peers(n_cols, c, half)

    def slab(ref, k):
        if isinstance(k, int):
            return ref.at[pl.ds(k * rows, rows)]
        return ref.at[pl.ds(pl.multiple_of(k * rows, rows), rows)]

    def remote(src, slot, sem, device):
        return pltpu.make_async_remote_copy(
            src_ref=src,
            dst_ref=slab(held, slot),
            send_sem=g_send.at[sem],
            recv_sem=g_recv.at[slot],
            device_id=device,
            device_id_type=MESH,
        )

    to_mate = remote(piece_ref, c, 0, (g, mate))
    to_mate.start()

    @pl.when(down)
    def _():
        remote(piece_ref, head, 1, (g - 1, 0)).start()
        remote(piece_ref, head, 2, (g - 1, 2)).start()

    @pl.when(g + 1 == n_rows)
    def _():
        held[pl.ds(head * rows, rows), :] = jnp.zeros(piece_ref.shape, jnp.float32)

    remote(piece_ref, mate, 0, (g, mate)).wait_recv()

    @pl.when(up)
    def _():
        remote(piece_ref, head, 1, (g + 1, 0)).wait_recv()

    for p, live in peers:
        @pl.when(live)
        def _():
            remote(piece_ref, c, 3 + 3 * p, (g, p)).start()
            remote(slab(held, mate), mate, 4 + 3 * p, (g, p)).start()

        @pl.when(jnp.logical_and(live, up))
        def _():
            remote(slab(held, head), head, 5 + 3 * p, (g, p)).start()

    held[pl.ds(pl.multiple_of(c * rows, rows), rows), :] = piece_ref[...]

    for p, live in peers:
        @pl.when(live)
        def _():
            remote(piece_ref, p, 3 + 3 * p, (g, p)).wait_recv()
            remote(piece_ref, p ^ 2, 3 + 3 * p, (g, p)).wait_recv()

    @pl.when(jnp.logical_and(jnp.logical_not(collector), g + 1 < n_rows))
    def _():
        remote(piece_ref, head, 1, (g, 0)).wait_recv()

    def result_copy(p, sender, t):
        return pltpu.make_async_remote_copy(
            src_ref=res.at[sender, t],
            dst_ref=res.at[sender, t],
            send_sem=r_send.at[p],
            recv_sem=r_recv.at[sender],
            device_id=(g, p),
            device_id_type=MESH,
        )

    def all_results(p, sender):
        return pltpu.make_async_remote_copy(
            src_ref=res.at[sender],
            dst_ref=res.at[sender],
            send_sem=r_send.at[p],
            recv_sem=r_recv.at[sender],
            device_id=(g, p),
            device_id_type=MESH,
        )

    r_i = lax.broadcasted_iota(jnp.int32, (B, B), 0)
    r_j = lax.broadcasted_iota(jnp.int32, (B, B), 1)
    flip = r_i + r_j == B - 1
    m_i = lax.broadcasted_iota(jnp.int32, (128, 128), 0)
    m_j = lax.broadcasted_iota(jnp.int32, (128, 128), 1)
    mirror = jnp.where(m_i + m_j == 127, 1.0, 0.0).astype(jnp.bfloat16)

    def body(t, carry):
        col = c + n_cols * t
        i = jnp.clip(tiles_ref[0, col] - g * BPR, 0, BPR - 1)
        d = jnp.clip(tiles_ref[1, col], 0, SPILL - 1)
        j = i + d
        zl = windows(held, i)
        zr = windows(held, j)
        corr = split_dot(zl, zr)
        corr = jnp.where(d * B + r_i - r_j >= EXCL, corr, jnp.float32(-1.0))
        row_c = jnp.max(corr, axis=1, keepdims=True)
        row_max = jnp.sum(jnp.where(flip, row_c, 0.0), axis=0, keepdims=True)
        col_r = jnp.max(corr, axis=0, keepdims=True)
        sub = lax.broadcasted_iota(jnp.int32, (8, 128), 0)
        slab_v = jnp.full((8, 128), -1.0, jnp.float32)
        nb = B // 128
        for v in range(nb):
            slab_v = jnp.where(sub == v, row_max[:, v * 128:(v + 1) * 128], slab_v)
            slab_v = jnp.where(sub == nb + v, col_r[:, (nb - 1 - v) * 128:(nb - v) * 128], slab_v)
        slab_v = jnp.where(sub < nb, slab_v, reverse_lanes(slab_v, mirror))
        res[c, t] = slab_v
        for p in range(n_cols):
            @pl.when(p != c)
            def _():
                result_copy(p, c, t).start()
        return carry

    lax.fori_loop(0, n_tiles, body, 0)

    has_next = g + 1 < n_rows
    sub = lax.broadcasted_iota(jnp.int32, (8, 128), 0)
    top = sub < 4

    def gather_blocks(senders, base, acc):
        for sender, t in senders:
            col = sender + n_cols * t
            i = jnp.clip(tiles_ref[0, col] - g * BPR, 0, BPR - 1) - base
            j = i + jnp.clip(tiles_ref[1, col], 0, SPILL - 1)
            slab_v = res[sender, t]
            flipped = pltpu.roll(slab_v, 4, 0)
            for m in range(len(acc)):
                even, odd = 2 * m, 2 * m + 1
                take = jnp.logical_or(jnp.logical_and(top, i == even), jnp.logical_and(jnp.logical_not(top), j == odd))
                take_f = jnp.logical_or(jnp.logical_and(jnp.logical_not(top), i == odd), jnp.logical_and(top, j == even))
                acc[m] = jnp.maximum(acc[m], jnp.maximum(
                    jnp.where(take, slab_v, jnp.float32(-1.0)),
                    jnp.where(take_f, flipped, jnp.float32(-1.0))))
        return acc

    quads = SPILL // 2
    spill_acc = gather_blocks([(c, t) for t in range(n_tiles)], BPR,
                              [jnp.full((8, 128), -1.0, jnp.float32) for _ in range(quads)])
    for m in range(quads):
        spill_out[pl.ds(8 * m, 8), :] = spill_acc[m]

    def spill_up():
        return pltpu.make_async_remote_copy(
            src_ref=spill_out,
            dst_ref=spills.at[c],
            send_sem=s_send.at[0],
            recv_sem=s_recv.at[0],
            device_id=(g + 1, 0),
            device_id_type=MESH,
        )

    @pl.when(has_next)
    def _():
        spill_up().start()


    base = c * SPILL
    acc = [jnp.full((8, 128), -1.0, jnp.float32) for _ in range(quads)]
    for sender in range(n_cols):
        @pl.when(sender != c)
        def _():
            all_results(sender, sender).wait_recv()

        acc = gather_blocks([(sender, t) for t in range(n_tiles)], base, acc)

    @pl.when(down)
    def _():
        pltpu.make_async_remote_copy(
            src_ref=spills,
            dst_ref=spills,
            send_sem=s_send.at[0],
            recv_sem=s_recv.at[0],
            device_id=(g - 1, 0),
            device_id_type=MESH,
        ).wait_recv()

    spilled = jnp.max(spills[...], axis=0)
    for m in range(quads):
        out_ref[pl.ds(8 * m, 8), :] = jnp.maximum(acc[m], spilled[8 * m:8 * m + 8])

    to_mate.wait_send()

    @pl.when(down)
    def _():
        remote(piece_ref, head, 1, (g - 1, 0)).wait_send()
        remote(piece_ref, head, 2, (g - 1, 2)).wait_send()

    for p, live in peers:
        @pl.when(live)
        def _():
            remote(piece_ref, c, 3 + 3 * p, (g, p)).wait_send()
            remote(piece_ref, c, 4 + 3 * p, (g, p)).wait_send()

        @pl.when(jnp.logical_and(live, up))
        def _():
            remote(piece_ref, c, 5 + 3 * p, (g, p)).wait_send()

    for p in range(n_cols):
        @pl.when(p != c)
        def _():
            all_results(p, c).wait_send()

    @pl.when(has_next)
    def _():
        spill_up().wait_send()


def fused_call(tiles, piece, n_rows, n_cols):
    n_tiles = tiles.shape[1] // n_cols
    slots = n_cols + 1
    chunk = piece.shape
    return pl.pallas_call(
        lambda *refs: fused_kernel(n_rows, n_cols, n_tiles, *refs),
        out_shape=jax.ShapeDtypeStruct(chunk, jnp.float32),
        in_specs=[
            pl.BlockSpec(memory_space=pltpu.SMEM),
            pl.BlockSpec(memory_space=pltpu.VMEM),
        ],
        out_specs=pl.BlockSpec(memory_space=pltpu.VMEM),
        scratch_shapes=[
            pltpu.VMEM((slots * chunk[0], 128), jnp.float32),
            pltpu.VMEM((n_cols, n_tiles, 8, 128), jnp.float32),
            pltpu.VMEM(chunk, jnp.float32),
            pltpu.VMEM((n_cols,) + chunk, jnp.float32),
            pltpu.SemaphoreType.DMA((3 + 3 * n_cols,)),
            pltpu.SemaphoreType.DMA((slots,)),
            pltpu.SemaphoreType.DMA((n_cols,)),
            pltpu.SemaphoreType.DMA((n_cols,)),
            pltpu.SemaphoreType.DMA((1,)),
            pltpu.SemaphoreType.DMA((1,)),
        ],
        cost_estimate=pl.CostEstimate(
            flops=n_tiles * 2 * B * B * M * 3,
            bytes_accessed=slots * chunk[0] * 128 * 4,
            transcendentals=n_tiles * 2 * B,
        ),
        compiler_params=pltpu.CompilerParams(collective_id=0, has_side_effects=True),
    )(tiles, piece)


def on_device(series, tile_list):
    piece = series.shape[0]
    col_count = lax.axis_size("cols")
    n_rows = lax.axis_size("rows")
    result = fused_call(tile_list, series.reshape(piece // 128, 128), n_rows, col_count)
    return jnp.maximum(result, jnp.float32(-1.0)).reshape(piece)


def solution(mesh):
    in_specs = (P(("rows", "cols")), P(None, "rows"))
    out_specs = P(("rows", "cols"))
    return jax.shard_map(
        on_device, mesh=mesh, in_specs=in_specs, out_specs=out_specs, check_vma=False
    )
```

```python
import math

import jax
import jax.numpy as jnp
from jax import lax
from jax.experimental import pallas as pl
from jax.experimental.pallas import tpu as pltpu
from jax.sharding import PartitionSpec as P

M = 256
B = 512
BPR = 128
EXCL = 64
SPILL = 8
SEG = B + M
MESH = pl.DeviceIdType.MESH


def passed_along(block, axis, distance):
    devices = range(lax.axis_size(axis))
    route = [(i - distance, i) for i in devices if i - distance in devices]
    return lax.ppermute(block, axis, route)


def windows(held, b):
    per = B // 128
    seg = jnp.concatenate([held[pl.ds(b * per + v, 1), :] for v in range(SEG // 128)], axis=1)
    parts = []
    for m in range(B // 128):
        lo = 3 * 128 - 128 * m
        sub = jnp.broadcast_to(seg[:, lo:lo + 3 * 128], (128, 3 * 128))
        parts.append(pltpu.roll(sub, 1, 1, stride=1, stride_axis=0)[:, 128:])
    w = jnp.concatenate(parts, axis=0)
    centre = w - jnp.mean(w, axis=1, keepdims=True)
    spread = jnp.mean(centre * centre, axis=1, keepdims=True)
    factor = lax.rsqrt(spread + 1e-05) / math.sqrt(M)
    return centre * factor


def split_dot(a, b):
    a_hi = a.astype(jnp.bfloat16)
    b_hi = b.astype(jnp.bfloat16)
    a_lo = (a - a_hi.astype(jnp.float32)).astype(jnp.bfloat16)
    b_lo = (b - b_hi.astype(jnp.float32)).astype(jnp.bfloat16)
    dims = (((1,), (1,)), ((), ()))

    def dot(x, y):
        return lax.dot_general(x, y, dims, preferred_element_type=jnp.float32)

    return dot(a_hi, b_hi) + (dot(a_hi, b_lo) + dot(a_lo, b_hi))


def reverse_lanes(x, mirror):
    hi = x.astype(jnp.bfloat16)
    rest = x - hi.astype(jnp.float32)
    mid = rest.astype(jnp.bfloat16)
    lo = (rest - mid.astype(jnp.float32)).astype(jnp.bfloat16)

    def dot(part):
        return jnp.dot(part, mirror, preferred_element_type=jnp.float32)

    return (dot(hi) + dot(mid)) + dot(lo)


def greet_partners(n_rows, n_cols):
    g = lax.axis_index("rows")
    c = lax.axis_index("cols")
    barrier = pltpu.get_barrier_semaphore()
    half = (c // 2) % 2
    for p in range(n_cols):
        @pl.when(p != c)
        def _():
            pl.semaphore_signal(barrier, 1, device_id=(g, p), device_id_type=MESH)

    has_next = g + 1 < n_rows

    @pl.when(has_next)
    def _():
        pl.semaphore_signal(barrier, 1, device_id=(g + 1, 0), device_id_type=MESH)

    down = jnp.logical_and(c == 0, g > 0)

    @pl.when(down)
    def _():
        for p in range(n_cols):
            pl.semaphore_signal(barrier, 1, device_id=(g - 1, p), device_id_type=MESH)

    collector = jnp.logical_or(c == 0, c == 2)
    up = jnp.logical_and(collector, has_next)
    count = (n_cols - 1) + has_next.astype(jnp.int32) + n_cols * down.astype(jnp.int32)
    pl.semaphore_wait(barrier, count)
    return g, c, half, collector, up, down


def half_peers(n_cols, c, half):
    return [
        (p, jnp.logical_and(p != c, (p // 2) % 2 == half)) for p in range(n_cols)
    ]


def fused_kernel(n_rows, n_cols, n_tiles, tiles_ref, piece_ref, out_ref,
                 held, res, spill_out, spills, diff_ref, flip_ref,
                 g_send, g_recv, r_send, r_recv, s_send, s_recv):
    spills[...] = jnp.full(spills.shape, -1.0, jnp.float32)
    r_i = lax.broadcasted_iota(jnp.int32, (B, B), 0)
    r_j = lax.broadcasted_iota(jnp.int32, (B, B), 1)
    diff_ref[...] = r_i - r_j
    flip_ref[...] = jnp.where(r_i + r_j == B - 1, 1.0, 0.0)
    g, c, half, collector, up, down = greet_partners(n_rows, n_cols)
    mate = c ^ 2
    head = n_cols
    rows = SPILL * B // 128
    peers = half_peers(n_cols, c, half)

    def slab(ref, k):
        if isinstance(k, int):
            return ref.at[pl.ds(k * rows, rows)]
        return ref.at[pl.ds(pl.multiple_of(k * rows, rows), rows)]

    def remote(src, slot, sem, device):
        return pltpu.make_async_remote_copy(
            src_ref=src,
            dst_ref=slab(held, slot),
            send_sem=g_send.at[sem],
            recv_sem=g_recv.at[slot],
            device_id=device,
            device_id_type=MESH,
        )

    to_mate = remote(piece_ref, c, 0, (g, mate))
    to_mate.start()

    @pl.when(down)
    def _():
        remote(piece_ref, head, 1, (g - 1, 0)).start()
        remote(piece_ref, head, 2, (g - 1, 2)).start()

    @pl.when(g + 1 == n_rows)
    def _():
        held[pl.ds(head * rows, rows), :] = jnp.zeros(piece_ref.shape, jnp.float32)

    remote(piece_ref, mate, 0, (g, mate)).wait_recv()

    @pl.when(up)
    def _():
        remote(piece_ref, head, 1, (g + 1, 0)).wait_recv()

    for p, live in peers:
        @pl.when(live)
        def _():
            remote(piece_ref, c, 3 + 3 * p, (g, p)).start()
            remote(slab(held, mate), mate, 4 + 3 * p, (g, p)).start()

        @pl.when(jnp.logical_and(live, up))
        def _():
            remote(slab(held, head), head, 5 + 3 * p, (g, p)).start()

    held[pl.ds(pl.multiple_of(c * rows, rows), rows), :] = piece_ref[...]

    for p, live in peers:
        @pl.when(live)
        def _():
            remote(piece_ref, p, 3 + 3 * p, (g, p)).wait_recv()
            remote(piece_ref, p ^ 2, 3 + 3 * p, (g, p)).wait_recv()

    @pl.when(jnp.logical_and(jnp.logical_not(collector), g + 1 < n_rows))
    def _():
        remote(piece_ref, head, 1, (g, 0)).wait_recv()

    def result_copy(p, sender, t):
        return pltpu.make_async_remote_copy(
            src_ref=res.at[sender, t],
            dst_ref=res.at[sender, t],
            send_sem=r_send.at[p],
            recv_sem=r_recv.at[sender],
            device_id=(g, p),
            device_id_type=MESH,
        )

    def all_results(p, sender):
        return pltpu.make_async_remote_copy(
            src_ref=res.at[sender],
            dst_ref=res.at[sender],
            send_sem=r_send.at[p],
            recv_sem=r_recv.at[sender],
            device_id=(g, p),
            device_id_type=MESH,
        )

    m_i = lax.broadcasted_iota(jnp.int32, (128, 128), 0)
    m_j = lax.broadcasted_iota(jnp.int32, (128, 128), 1)
    mirror = jnp.where(m_i + m_j == 127, 1.0, 0.0).astype(jnp.bfloat16)

    def body(t, carry):
        col = c + n_cols * t
        i = jnp.clip(tiles_ref[0, col] - g * BPR, 0, BPR - 1)
        d = jnp.clip(tiles_ref[1, col], 0, SPILL - 1)
        j = i + d
        zl = windows(held, i)
        zr = windows(held, j)
        corr = split_dot(zl, zr)
        corr = jnp.where(diff_ref[...] >= EXCL - d * B, corr, jnp.float32(-1.0))
        row_c = jnp.max(corr, axis=1, keepdims=True)
        row_max = jnp.sum(row_c * flip_ref[...], axis=0, keepdims=True)
        col_r = jnp.max(corr, axis=0, keepdims=True)
        sub = lax.broadcasted_iota(jnp.int32, (8, 128), 0)
        slab_v = jnp.full((8, 128), -1.0, jnp.float32)
        nb = B // 128
        for v in range(nb):
            slab_v = jnp.where(sub == v, row_max[:, v * 128:(v + 1) * 128], slab_v)
            slab_v = jnp.where(sub == nb + v, col_r[:, (nb - 1 - v) * 128:(nb - v) * 128], slab_v)
        slab_v = jnp.where(sub < nb, slab_v, reverse_lanes(slab_v, mirror))
        res[c, t] = slab_v
        for p in range(n_cols):
            @pl.when(p != c)
            def _():
                result_copy(p, c, t).start()
        return carry

    lax.fori_loop(0, n_tiles, body, 0)

    has_next = g + 1 < n_rows
    sub = lax.broadcasted_iota(jnp.int32, (8, 128), 0)
    top = sub < 4

    def gather_blocks(senders, base, acc):
        for sender, t in senders:
            col = sender + n_cols * t
            i = jnp.clip(tiles_ref[0, col] - g * BPR, 0, BPR - 1) - base
            j = i + jnp.clip(tiles_ref[1, col], 0, SPILL - 1)
            slab_v = res[sender, t]
            flipped = pltpu.roll(slab_v, 4, 0)
            for m in range(len(acc)):
                even, odd = 2 * m, 2 * m + 1
                take = jnp.logical_or(jnp.logical_and(top, i == even), jnp.logical_and(jnp.logical_not(top), j == odd))
                take_f = jnp.logical_or(jnp.logical_and(jnp.logical_not(top), i == odd), jnp.logical_and(top, j == even))
                acc[m] = jnp.maximum(acc[m], jnp.maximum(
                    jnp.where(take, slab_v, jnp.float32(-1.0)),
                    jnp.where(take_f, flipped, jnp.float32(-1.0))))
        return acc

    quads = SPILL // 2
    spill_acc = gather_blocks([(c, t) for t in range(n_tiles)], BPR,
                              [jnp.full((8, 128), -1.0, jnp.float32) for _ in range(quads)])
    for m in range(quads):
        spill_out[pl.ds(8 * m, 8), :] = spill_acc[m]

    def spill_up():
        return pltpu.make_async_remote_copy(
            src_ref=spill_out,
            dst_ref=spills.at[c],
            send_sem=s_send.at[0],
            recv_sem=s_recv.at[0],
            device_id=(g + 1, 0),
            device_id_type=MESH,
        )

    @pl.when(has_next)
    def _():
        spill_up().start()


    base = c * SPILL
    acc = [jnp.full((8, 128), -1.0, jnp.float32) for _ in range(quads)]
    for sender in range(n_cols):
        @pl.when(sender != c)
        def _():
            all_results(sender, sender).wait_recv()

        acc = gather_blocks([(sender, t) for t in range(n_tiles)], base, acc)

    @pl.when(down)
    def _():
        pltpu.make_async_remote_copy(
            src_ref=spills,
            dst_ref=spills,
            send_sem=s_send.at[0],
            recv_sem=s_recv.at[0],
            device_id=(g - 1, 0),
            device_id_type=MESH,
        ).wait_recv()

    spilled = jnp.max(spills[...], axis=0)
    for m in range(quads):
        out_ref[pl.ds(8 * m, 8), :] = jnp.maximum(acc[m], spilled[8 * m:8 * m + 8])

    to_mate.wait_send()

    @pl.when(down)
    def _():
        remote(piece_ref, head, 1, (g - 1, 0)).wait_send()
        remote(piece_ref, head, 2, (g - 1, 2)).wait_send()

    for p, live in peers:
        @pl.when(live)
        def _():
            remote(piece_ref, c, 3 + 3 * p, (g, p)).wait_send()
            remote(piece_ref, c, 4 + 3 * p, (g, p)).wait_send()

        @pl.when(jnp.logical_and(live, up))
        def _():
            remote(piece_ref, c, 5 + 3 * p, (g, p)).wait_send()

    for p in range(n_cols):
        @pl.when(p != c)
        def _():
            all_results(p, c).wait_send()

    @pl.when(has_next)
    def _():
        spill_up().wait_send()


def fused_call(tiles, piece, n_rows, n_cols):
    n_tiles = tiles.shape[1] // n_cols
    slots = n_cols + 1
    chunk = piece.shape
    return pl.pallas_call(
        lambda *refs: fused_kernel(n_rows, n_cols, n_tiles, *refs),
        out_shape=jax.ShapeDtypeStruct(chunk, jnp.float32),
        in_specs=[
            pl.BlockSpec(memory_space=pltpu.SMEM),
            pl.BlockSpec(memory_space=pltpu.VMEM),
        ],
        out_specs=pl.BlockSpec(memory_space=pltpu.VMEM),
        scratch_shapes=[
            pltpu.VMEM((slots * chunk[0], 128), jnp.float32),
            pltpu.VMEM((n_cols, n_tiles, 8, 128), jnp.float32),
            pltpu.VMEM(chunk, jnp.float32),
            pltpu.VMEM((n_cols,) + chunk, jnp.float32),
            pltpu.VMEM((B, B), jnp.int32),
            pltpu.VMEM((B, B), jnp.float32),
            pltpu.SemaphoreType.DMA((3 + 3 * n_cols,)),
            pltpu.SemaphoreType.DMA((slots,)),
            pltpu.SemaphoreType.DMA((n_cols,)),
            pltpu.SemaphoreType.DMA((n_cols,)),
            pltpu.SemaphoreType.DMA((1,)),
            pltpu.SemaphoreType.DMA((1,)),
        ],
        cost_estimate=pl.CostEstimate(
            flops=n_tiles * 2 * B * B * M * 3,
            bytes_accessed=slots * chunk[0] * 128 * 4,
            transcendentals=n_tiles * 2 * B,
        ),
        compiler_params=pltpu.CompilerParams(collective_id=0, has_side_effects=True),
    )(tiles, piece)


def on_device(series, tile_list):
    piece = series.shape[0]
    col_count = lax.axis_size("cols")
    n_rows = lax.axis_size("rows")
    result = fused_call(tile_list, series.reshape(piece // 128, 128), n_rows, col_count)
    return jnp.maximum(result, jnp.float32(-1.0)).reshape(piece)


def solution(mesh):
    in_specs = (P(("rows", "cols")), P(None, "rows"))
    out_specs = P(("rows", "cols"))
    return jax.shard_map(
        on_device, mesh=mesh, in_specs=in_specs, out_specs=out_specs, check_vma=False
    )
```

```python
import math

import jax
import jax.numpy as jnp
from jax import lax
from jax.experimental import pallas as pl
from jax.experimental.pallas import tpu as pltpu
from jax.sharding import PartitionSpec as P

M = 256
B = 512
BPR = 128
EXCL = 64
SPILL = 8
SEG = B + M
MESH = pl.DeviceIdType.MESH


def passed_along(block, axis, distance):
    devices = range(lax.axis_size(axis))
    route = [(i - distance, i) for i in devices if i - distance in devices]
    return lax.ppermute(block, axis, route)


def windows(held, b):
    per = B // 128
    seg = jnp.concatenate([held[pl.ds(b * per + v, 1), :] for v in range(SEG // 128)], axis=1)
    parts = []
    for m in range(B // 128):
        lo = 3 * 128 - 128 * m
        sub = jnp.broadcast_to(seg[:, lo:lo + 3 * 128], (128, 3 * 128))
        parts.append(pltpu.roll(sub, 1, 1, stride=1, stride_axis=0)[:, 128:])
    w = jnp.concatenate(parts, axis=0)
    centre = w - jnp.mean(w, axis=1, keepdims=True)
    spread = jnp.mean(centre * centre, axis=1, keepdims=True)
    factor = lax.rsqrt(spread + 1e-05) / math.sqrt(M)
    return centre * factor


def split_dot(a, b):
    a_hi = a.astype(jnp.bfloat16)
    b_hi = b.astype(jnp.bfloat16)
    a_lo = (a - a_hi.astype(jnp.float32)).astype(jnp.bfloat16)
    b_lo = (b - b_hi.astype(jnp.float32)).astype(jnp.bfloat16)
    dims = (((1,), (1,)), ((), ()))

    def dot(x, y):
        return lax.dot_general(x, y, dims, preferred_element_type=jnp.float32)

    return dot(a_hi, b_hi) + (dot(a_hi, b_lo) + dot(a_lo, b_hi))


def reverse_lanes(x, mirror):
    hi = x.astype(jnp.bfloat16)
    rest = x - hi.astype(jnp.float32)
    mid = rest.astype(jnp.bfloat16)
    lo = (rest - mid.astype(jnp.float32)).astype(jnp.bfloat16)

    def dot(part):
        return jnp.dot(part, mirror, preferred_element_type=jnp.float32)

    return (dot(hi) + dot(mid)) + dot(lo)


def greet_partners(n_rows, n_cols):
    g = lax.axis_index("rows")
    c = lax.axis_index("cols")
    barrier = pltpu.get_barrier_semaphore()
    half = (c // 2) % 2
    for p in range(n_cols):
        @pl.when(p != c)
        def _():
            pl.semaphore_signal(barrier, 1, device_id=(g, p), device_id_type=MESH)

    has_next = g + 1 < n_rows

    @pl.when(has_next)
    def _():
        pl.semaphore_signal(barrier, 1, device_id=(g + 1, 0), device_id_type=MESH)

    down = jnp.logical_and(c == 0, g > 0)

    @pl.when(down)
    def _():
        for p in range(n_cols):
            pl.semaphore_signal(barrier, 1, device_id=(g - 1, p), device_id_type=MESH)

    collector = jnp.logical_or(c == 0, c == 2)
    up = jnp.logical_and(collector, has_next)
    count = (n_cols - 1) + has_next.astype(jnp.int32) + n_cols * down.astype(jnp.int32)
    pl.semaphore_wait(barrier, count)
    return g, c, half, collector, up, down


def half_peers(n_cols, c, half):
    return [
        (p, jnp.logical_and(p != c, (p // 2) % 2 == half)) for p in range(n_cols)
    ]


def fused_kernel(n_rows, n_cols, n_tiles, tiles_ref, piece_ref, out_ref,
                 held, res, spill_out, spills, diff_ref, flip_ref,
                 g_send, g_recv, r_send, r_recv, s_send, s_recv):
    spills[...] = jnp.full(spills.shape, -1.0, jnp.float32)
    r_i = lax.broadcasted_iota(jnp.int32, (B, B), 0)
    r_j = lax.broadcasted_iota(jnp.int32, (B, B), 1)
    diff_ref[...] = r_i - r_j
    flip_ref[...] = jnp.where(r_i + r_j == B - 1, 1.0, 0.0)
    g, c, half, collector, up, down = greet_partners(n_rows, n_cols)
    mate = c ^ 2
    head = n_cols
    rows = SPILL * B // 128
    peers = half_peers(n_cols, c, half)

    def slab(ref, k):
        if isinstance(k, int):
            return ref.at[pl.ds(k * rows, rows)]
        return ref.at[pl.ds(pl.multiple_of(k * rows, rows), rows)]

    def remote(src, slot, sem, device):
        return pltpu.make_async_remote_copy(
            src_ref=src,
            dst_ref=slab(held, slot),
            send_sem=g_send.at[sem],
            recv_sem=g_recv.at[slot],
            device_id=device,
            device_id_type=MESH,
        )

    to_mate = remote(piece_ref, c, 0, (g, mate))
    to_mate.start()

    for p, live in peers:
        @pl.when(live)
        def _():
            remote(piece_ref, c, 3 + 3 * p, (g, p)).start()

    @pl.when(down)
    def _():
        remote(piece_ref, head, 1, (g - 1, 0)).start()
        remote(piece_ref, head, 2, (g - 1, 2)).start()

    @pl.when(g + 1 == n_rows)
    def _():
        held[pl.ds(head * rows, rows), :] = jnp.zeros(piece_ref.shape, jnp.float32)

    remote(piece_ref, mate, 0, (g, mate)).wait_recv()

    @pl.when(up)
    def _():
        remote(piece_ref, head, 1, (g + 1, 0)).wait_recv()

    for p, live in peers:
        @pl.when(live)
        def _():
            remote(slab(held, mate), mate, 4 + 3 * p, (g, p)).start()

        @pl.when(jnp.logical_and(live, up))
        def _():
            remote(slab(held, head), head, 5 + 3 * p, (g, p)).start()

    held[pl.ds(pl.multiple_of(c * rows, rows), rows), :] = piece_ref[...]

    for p, live in peers:
        @pl.when(live)
        def _():
            remote(piece_ref, p, 3 + 3 * p, (g, p)).wait_recv()
            remote(piece_ref, p ^ 2, 3 + 3 * p, (g, p)).wait_recv()

    @pl.when(jnp.logical_and(jnp.logical_not(collector), g + 1 < n_rows))
    def _():
        remote(piece_ref, head, 1, (g, 0)).wait_recv()

    def result_copy(p, sender, t):
        return pltpu.make_async_remote_copy(
            src_ref=res.at[sender, t],
            dst_ref=res.at[sender, t],
            send_sem=r_send.at[p],
            recv_sem=r_recv.at[sender],
            device_id=(g, p),
            device_id_type=MESH,
        )

    def all_results(p, sender):
        return pltpu.make_async_remote_copy(
            src_ref=res.at[sender],
            dst_ref=res.at[sender],
            send_sem=r_send.at[p],
            recv_sem=r_recv.at[sender],
            device_id=(g, p),
            device_id_type=MESH,
        )

    m_i = lax.broadcasted_iota(jnp.int32, (128, 128), 0)
    m_j = lax.broadcasted_iota(jnp.int32, (128, 128), 1)
    mirror = jnp.where(m_i + m_j == 127, 1.0, 0.0).astype(jnp.bfloat16)

    def body(t, carry):
        col = c + n_cols * t
        i = jnp.clip(tiles_ref[0, col] - g * BPR, 0, BPR - 1)
        d = jnp.clip(tiles_ref[1, col], 0, SPILL - 1)
        j = i + d
        zl = windows(held, i)
        zr = windows(held, j)
        corr = split_dot(zl, zr)
        corr = jnp.where(diff_ref[...] >= EXCL - d * B, corr, jnp.float32(-1.0))
        row_c = jnp.max(corr, axis=1, keepdims=True)
        row_max = jnp.sum(row_c * flip_ref[...], axis=0, keepdims=True)
        col_r = jnp.max(corr, axis=0, keepdims=True)
        sub = lax.broadcasted_iota(jnp.int32, (8, 128), 0)
        slab_v = jnp.full((8, 128), -1.0, jnp.float32)
        nb = B // 128
        for v in range(nb):
            slab_v = jnp.where(sub == v, row_max[:, v * 128:(v + 1) * 128], slab_v)
            slab_v = jnp.where(sub == nb + v, col_r[:, (nb - 1 - v) * 128:(nb - v) * 128], slab_v)
        slab_v = jnp.where(sub < nb, slab_v, reverse_lanes(slab_v, mirror))
        res[c, t] = slab_v
        for p in range(n_cols):
            @pl.when(p != c)
            def _():
                result_copy(p, c, t).start()
        return carry

    lax.fori_loop(0, n_tiles, body, 0, unroll=True)

    has_next = g + 1 < n_rows
    sub = lax.broadcasted_iota(jnp.int32, (8, 128), 0)
    top = sub < 4

    def gather_blocks(senders, base, acc):
        for sender, t in senders:
            col = sender + n_cols * t
            i = jnp.clip(tiles_ref[0, col] - g * BPR, 0, BPR - 1) - base
            j = i + jnp.clip(tiles_ref[1, col], 0, SPILL - 1)
            slab_v = res[sender, t]
            flipped = pltpu.roll(slab_v, 4, 0)
            for m in range(len(acc)):
                even, odd = 2 * m, 2 * m + 1
                take = jnp.logical_or(jnp.logical_and(top, i == even), jnp.logical_and(jnp.logical_not(top), j == odd))
                take_f = jnp.logical_or(jnp.logical_and(jnp.logical_not(top), i == odd), jnp.logical_and(top, j == even))
                acc[m] = jnp.maximum(acc[m], jnp.maximum(
                    jnp.where(take, slab_v, jnp.float32(-1.0)),
                    jnp.where(take_f, flipped, jnp.float32(-1.0))))
        return acc

    quads = SPILL // 2
    spill_acc = gather_blocks([(c, t) for t in range(n_tiles)], BPR,
                              [jnp.full((8, 128), -1.0, jnp.float32) for _ in range(quads)])
    for m in range(quads):
        spill_out[pl.ds(8 * m, 8), :] = spill_acc[m]

    def spill_up():
        return pltpu.make_async_remote_copy(
            src_ref=spill_out,
            dst_ref=spills.at[c],
            send_sem=s_send.at[0],
            recv_sem=s_recv.at[0],
            device_id=(g + 1, 0),
            device_id_type=MESH,
        )

    @pl.when(has_next)
    def _():
        spill_up().start()


    base = c * SPILL
    acc = [jnp.full((8, 128), -1.0, jnp.float32) for _ in range(quads)]
    for sender in range(n_cols):
        @pl.when(sender != c)
        def _():
            all_results(sender, sender).wait_recv()

        acc = gather_blocks([(sender, t) for t in range(n_tiles)], base, acc)

    @pl.when(down)
    def _():
        pltpu.make_async_remote_copy(
            src_ref=spills,
            dst_ref=spills,
            send_sem=s_send.at[0],
            recv_sem=s_recv.at[0],
            device_id=(g - 1, 0),
            device_id_type=MESH,
        ).wait_recv()

    spilled = jnp.max(spills[...], axis=0)
    for m in range(quads):
        out_ref[pl.ds(8 * m, 8), :] = jnp.maximum(acc[m], spilled[8 * m:8 * m + 8])

    to_mate.wait_send()

    @pl.when(down)
    def _():
        remote(piece_ref, head, 1, (g - 1, 0)).wait_send()
        remote(piece_ref, head, 2, (g - 1, 2)).wait_send()

    for p, live in peers:
        @pl.when(live)
        def _():
            remote(piece_ref, c, 3 + 3 * p, (g, p)).wait_send()
            remote(piece_ref, c, 4 + 3 * p, (g, p)).wait_send()

        @pl.when(jnp.logical_and(live, up))
        def _():
            remote(piece_ref, c, 5 + 3 * p, (g, p)).wait_send()

    for p in range(n_cols):
        @pl.when(p != c)
        def _():
            all_results(p, c).wait_send()

    @pl.when(has_next)
    def _():
        spill_up().wait_send()


def fused_call(tiles, piece, n_rows, n_cols):
    n_tiles = tiles.shape[1] // n_cols
    slots = n_cols + 1
    chunk = piece.shape
    return pl.pallas_call(
        lambda *refs: fused_kernel(n_rows, n_cols, n_tiles, *refs),
        out_shape=jax.ShapeDtypeStruct(chunk, jnp.float32),
        in_specs=[
            pl.BlockSpec(memory_space=pltpu.SMEM),
            pl.BlockSpec(memory_space=pltpu.VMEM),
        ],
        out_specs=pl.BlockSpec(memory_space=pltpu.VMEM),
        scratch_shapes=[
            pltpu.VMEM((slots * chunk[0], 128), jnp.float32),
            pltpu.VMEM((n_cols, n_tiles, 8, 128), jnp.float32),
            pltpu.VMEM(chunk, jnp.float32),
            pltpu.VMEM((n_cols,) + chunk, jnp.float32),
            pltpu.VMEM((B, B), jnp.int32),
            pltpu.VMEM((B, B), jnp.float32),
            pltpu.SemaphoreType.DMA((3 + 3 * n_cols,)),
            pltpu.SemaphoreType.DMA((slots,)),
            pltpu.SemaphoreType.DMA((n_cols,)),
            pltpu.SemaphoreType.DMA((n_cols,)),
            pltpu.SemaphoreType.DMA((1,)),
            pltpu.SemaphoreType.DMA((1,)),
        ],
        cost_estimate=pl.CostEstimate(
            flops=n_tiles * 2 * B * B * M * 3,
            bytes_accessed=slots * chunk[0] * 128 * 4,
            transcendentals=n_tiles * 2 * B,
        ),
        compiler_params=pltpu.CompilerParams(collective_id=0, has_side_effects=True),
    )(tiles, piece)


def on_device(series, tile_list):
    piece = series.shape[0]
    col_count = lax.axis_size("cols")
    n_rows = lax.axis_size("rows")
    result = fused_call(tile_list, series.reshape(piece // 128, 128), n_rows, col_count)
    return jnp.maximum(result, jnp.float32(-1.0)).reshape(piece)


def solution(mesh):
    in_specs = (P(("rows", "cols")), P(None, "rows"))
    out_specs = P(("rows", "cols"))
    return jax.shard_map(
        on_device, mesh=mesh, in_specs=in_specs, out_specs=out_specs, check_vma=False
    )
```

```python
import math

import jax
import jax.numpy as jnp
from jax import lax
from jax.experimental import pallas as pl
from jax.experimental.pallas import tpu as pltpu
from jax.sharding import PartitionSpec as P

M = 256
B = 512
BPR = 128
EXCL = 64
SPILL = 8
SEG = B + M
MESH = pl.DeviceIdType.MESH


def passed_along(block, axis, distance):
    devices = range(lax.axis_size(axis))
    route = [(i - distance, i) for i in devices if i - distance in devices]
    return lax.ppermute(block, axis, route)


def windows(held, b):
    per = B // 128
    seg = jnp.concatenate([held[pl.ds(b * per + v, 1), :] for v in range(SEG // 128)], axis=1)
    parts = []
    for m in range(B // 128):
        lo = 3 * 128 - 128 * m
        sub = jnp.broadcast_to(seg[:, lo:lo + 3 * 128], (128, 3 * 128))
        parts.append(pltpu.roll(sub, 1, 1, stride=1, stride_axis=0)[:, 128:])
    w = jnp.concatenate(parts, axis=0)
    centre = w - jnp.mean(w, axis=1, keepdims=True)
    spread = jnp.mean(centre * centre, axis=1, keepdims=True)
    factor = lax.rsqrt(spread + 1e-05) / math.sqrt(M)
    return centre * factor


def split_dot(a, b):
    a_hi = a.astype(jnp.bfloat16)
    b_hi = b.astype(jnp.bfloat16)
    a_lo = (a - a_hi.astype(jnp.float32)).astype(jnp.bfloat16)
    b_lo = (b - b_hi.astype(jnp.float32)).astype(jnp.bfloat16)
    dims = (((1,), (1,)), ((), ()))

    def dot(x, y):
        return lax.dot_general(x, y, dims, preferred_element_type=jnp.float32)

    return dot(a_hi, b_hi) + (dot(a_hi, b_lo) + dot(a_lo, b_hi))


def reverse_lanes(x, mirror):
    hi = x.astype(jnp.bfloat16)
    rest = x - hi.astype(jnp.float32)
    mid = rest.astype(jnp.bfloat16)
    lo = (rest - mid.astype(jnp.float32)).astype(jnp.bfloat16)

    def dot(part):
        return jnp.dot(part, mirror, preferred_element_type=jnp.float32)

    return (dot(hi) + dot(mid)) + dot(lo)


def greet_partners(n_rows, n_cols, before_wait):
    g = lax.axis_index("rows")
    c = lax.axis_index("cols")
    barrier = pltpu.get_barrier_semaphore()
    half = (c // 2) % 2
    for p in range(n_cols):
        @pl.when(p != c)
        def _():
            pl.semaphore_signal(barrier, 1, device_id=(g, p), device_id_type=MESH)

    has_next = g + 1 < n_rows

    @pl.when(has_next)
    def _():
        pl.semaphore_signal(barrier, 1, device_id=(g + 1, 0), device_id_type=MESH)

    down = jnp.logical_and(c == 0, g > 0)

    @pl.when(down)
    def _():
        for p in range(n_cols):
            pl.semaphore_signal(barrier, 1, device_id=(g - 1, p), device_id_type=MESH)

    collector = jnp.logical_or(c == 0, c == 2)
    up = jnp.logical_and(collector, has_next)
    count = (n_cols - 1) + has_next.astype(jnp.int32) + n_cols * down.astype(jnp.int32)
    before_wait()
    pl.semaphore_wait(barrier, count)
    return g, c, half, collector, up, down


def half_peers(n_cols, c, half):
    return [
        (p, jnp.logical_and(p != c, (p // 2) % 2 == half)) for p in range(n_cols)
    ]


def fused_kernel(n_rows, n_cols, n_tiles, tiles_ref, piece_ref, out_ref,
                 held, res, spill_out, spills, diff_ref, flip_ref,
                 g_send, g_recv, r_send, r_recv, s_send, s_recv):
    spills[...] = jnp.full(spills.shape, -1.0, jnp.float32)

    def tables():
        r_i = lax.broadcasted_iota(jnp.int32, (B, B), 0)
        r_j = lax.broadcasted_iota(jnp.int32, (B, B), 1)
        diff_ref[...] = r_i - r_j
        flip_ref[...] = jnp.where(r_i + r_j == B - 1, 1.0, 0.0)

    g, c, half, collector, up, down = greet_partners(n_rows, n_cols, tables)
    mate = c ^ 2
    head = n_cols
    rows = SPILL * B // 128
    peers = half_peers(n_cols, c, half)

    def slab(ref, k):
        if isinstance(k, int):
            return ref.at[pl.ds(k * rows, rows)]
        return ref.at[pl.ds(pl.multiple_of(k * rows, rows), rows)]

    def remote(src, slot, sem, device):
        return pltpu.make_async_remote_copy(
            src_ref=src,
            dst_ref=slab(held, slot),
            send_sem=g_send.at[sem],
            recv_sem=g_recv.at[slot],
            device_id=device,
            device_id_type=MESH,
        )

    to_mate = remote(piece_ref, c, 0, (g, mate))
    to_mate.start()

    for p, live in peers:
        @pl.when(live)
        def _():
            remote(piece_ref, c, 3 + 3 * p, (g, p)).start()

    @pl.when(down)
    def _():
        remote(piece_ref, head, 1, (g - 1, 0)).start()
        remote(piece_ref, head, 2, (g - 1, 2)).start()

    @pl.when(g + 1 == n_rows)
    def _():
        held[pl.ds(head * rows, rows), :] = jnp.zeros(piece_ref.shape, jnp.float32)

    remote(piece_ref, mate, 0, (g, mate)).wait_recv()

    @pl.when(up)
    def _():
        remote(piece_ref, head, 1, (g + 1, 0)).wait_recv()

    for p, live in peers:
        @pl.when(live)
        def _():
            remote(slab(held, mate), mate, 4 + 3 * p, (g, p)).start()

        @pl.when(jnp.logical_and(live, up))
        def _():
            remote(slab(held, head), head, 5 + 3 * p, (g, p)).start()

    held[pl.ds(pl.multiple_of(c * rows, rows), rows), :] = piece_ref[...]

    for p, live in peers:
        @pl.when(live)
        def _():
            remote(piece_ref, p, 3 + 3 * p, (g, p)).wait_recv()
            remote(piece_ref, p ^ 2, 3 + 3 * p, (g, p)).wait_recv()

    @pl.when(jnp.logical_and(jnp.logical_not(collector), g + 1 < n_rows))
    def _():
        remote(piece_ref, head, 1, (g, 0)).wait_recv()

    def result_copy(p, sender, t):
        return pltpu.make_async_remote_copy(
            src_ref=res.at[sender, t],
            dst_ref=res.at[sender, t],
            send_sem=r_send.at[p],
            recv_sem=r_recv.at[sender],
            device_id=(g, p),
            device_id_type=MESH,
        )

    def all_results(p, sender):
        return pltpu.make_async_remote_copy(
            src_ref=res.at[sender],
            dst_ref=res.at[sender],
            send_sem=r_send.at[p],
            recv_sem=r_recv.at[sender],
            device_id=(g, p),
            device_id_type=MESH,
        )

    m_i = lax.broadcasted_iota(jnp.int32, (128, 128), 0)
    m_j = lax.broadcasted_iota(jnp.int32, (128, 128), 1)
    mirror = jnp.where(m_i + m_j == 127, 1.0, 0.0).astype(jnp.bfloat16)

    def body(t, carry):
        col = c + n_cols * t
        i = jnp.clip(tiles_ref[0, col] - g * BPR, 0, BPR - 1)
        d = jnp.clip(tiles_ref[1, col], 0, SPILL - 1)
        j = i + d
        zl = windows(held, i)
        zr = windows(held, j)
        corr = split_dot(zl, zr)
        corr = jnp.where(diff_ref[...] >= EXCL - d * B, corr, jnp.float32(-1.0))
        row_c = jnp.max(corr, axis=1, keepdims=True)
        row_max = jnp.sum(row_c * flip_ref[...], axis=0, keepdims=True)
        col_r = jnp.max(corr, axis=0, keepdims=True)
        sub = lax.broadcasted_iota(jnp.int32, (8, 128), 0)
        slab_v = jnp.full((8, 128), -1.0, jnp.float32)
        nb = B // 128
        for v in range(nb):
            slab_v = jnp.where(sub == v, row_max[:, v * 128:(v + 1) * 128], slab_v)
            slab_v = jnp.where(sub == nb + v, col_r[:, (nb - 1 - v) * 128:(nb - v) * 128], slab_v)
        slab_v = jnp.where(sub < nb, slab_v, reverse_lanes(slab_v, mirror))
        res[c, t] = slab_v
        for p in range(n_cols):
            @pl.when(p != c)
            def _():
                result_copy(p, c, t).start()
        return carry

    lax.fori_loop(0, n_tiles, body, 0, unroll=True)

    has_next = g + 1 < n_rows
    sub = lax.broadcasted_iota(jnp.int32, (8, 128), 0)
    top = sub < 4

    def gather_blocks(senders, base, acc):
        for sender, t in senders:
            col = sender + n_cols * t
            i = jnp.clip(tiles_ref[0, col] - g * BPR, 0, BPR - 1) - base
            j = i + jnp.clip(tiles_ref[1, col], 0, SPILL - 1)
            slab_v = res[sender, t]
            flipped = pltpu.roll(slab_v, 4, 0)
            for m in range(len(acc)):
                even, odd = 2 * m, 2 * m + 1
                take = jnp.logical_or(jnp.logical_and(top, i == even), jnp.logical_and(jnp.logical_not(top), j == odd))
                take_f = jnp.logical_or(jnp.logical_and(jnp.logical_not(top), i == odd), jnp.logical_and(top, j == even))
                acc[m] = jnp.maximum(acc[m], jnp.maximum(
                    jnp.where(take, slab_v, jnp.float32(-1.0)),
                    jnp.where(take_f, flipped, jnp.float32(-1.0))))
        return acc

    quads = SPILL // 2
    spill_acc = gather_blocks([(c, t) for t in range(n_tiles)], BPR,
                              [jnp.full((8, 128), -1.0, jnp.float32) for _ in range(quads)])
    for m in range(quads):
        spill_out[pl.ds(8 * m, 8), :] = spill_acc[m]

    def spill_up():
        return pltpu.make_async_remote_copy(
            src_ref=spill_out,
            dst_ref=spills.at[c],
            send_sem=s_send.at[0],
            recv_sem=s_recv.at[0],
            device_id=(g + 1, 0),
            device_id_type=MESH,
        )

    @pl.when(has_next)
    def _():
        spill_up().start()


    base = c * SPILL
    acc = [jnp.full((8, 128), -1.0, jnp.float32) for _ in range(quads)]
    for sender in range(n_cols):
        @pl.when(sender != c)
        def _():
            all_results(sender, sender).wait_recv()

        acc = gather_blocks([(sender, t) for t in range(n_tiles)], base, acc)

    @pl.when(down)
    def _():
        pltpu.make_async_remote_copy(
            src_ref=spills,
            dst_ref=spills,
            send_sem=s_send.at[0],
            recv_sem=s_recv.at[0],
            device_id=(g - 1, 0),
            device_id_type=MESH,
        ).wait_recv()

    spilled = jnp.max(spills[...], axis=0)
    for m in range(quads):
        out_ref[pl.ds(8 * m, 8), :] = jnp.maximum(acc[m], spilled[8 * m:8 * m + 8])

    to_mate.wait_send()

    @pl.when(down)
    def _():
        remote(piece_ref, head, 1, (g - 1, 0)).wait_send()
        remote(piece_ref, head, 2, (g - 1, 2)).wait_send()

    for p, live in peers:
        @pl.when(live)
        def _():
            remote(piece_ref, c, 3 + 3 * p, (g, p)).wait_send()
            remote(piece_ref, c, 4 + 3 * p, (g, p)).wait_send()

        @pl.when(jnp.logical_and(live, up))
        def _():
            remote(piece_ref, c, 5 + 3 * p, (g, p)).wait_send()

    for p in range(n_cols):
        @pl.when(p != c)
        def _():
            all_results(p, c).wait_send()

    @pl.when(has_next)
    def _():
        spill_up().wait_send()


def fused_call(tiles, piece, n_rows, n_cols):
    n_tiles = tiles.shape[1] // n_cols
    slots = n_cols + 1
    chunk = piece.shape
    return pl.pallas_call(
        lambda *refs: fused_kernel(n_rows, n_cols, n_tiles, *refs),
        out_shape=jax.ShapeDtypeStruct(chunk, jnp.float32),
        in_specs=[
            pl.BlockSpec(memory_space=pltpu.SMEM),
            pl.BlockSpec(memory_space=pltpu.VMEM),
        ],
        out_specs=pl.BlockSpec(memory_space=pltpu.VMEM),
        scratch_shapes=[
            pltpu.VMEM((slots * chunk[0], 128), jnp.float32),
            pltpu.VMEM((n_cols, n_tiles, 8, 128), jnp.float32),
            pltpu.VMEM(chunk, jnp.float32),
            pltpu.VMEM((n_cols,) + chunk, jnp.float32),
            pltpu.VMEM((B, B), jnp.int32),
            pltpu.VMEM((B, B), jnp.float32),
            pltpu.SemaphoreType.DMA((3 + 3 * n_cols,)),
            pltpu.SemaphoreType.DMA((slots,)),
            pltpu.SemaphoreType.DMA((n_cols,)),
            pltpu.SemaphoreType.DMA((n_cols,)),
            pltpu.SemaphoreType.DMA((1,)),
            pltpu.SemaphoreType.DMA((1,)),
        ],
        cost_estimate=pl.CostEstimate(
            flops=n_tiles * 2 * B * B * M * 3,
            bytes_accessed=slots * chunk[0] * 128 * 4,
            transcendentals=n_tiles * 2 * B,
        ),
        compiler_params=pltpu.CompilerParams(collective_id=0, has_side_effects=True),
    )(tiles, piece)


def on_device(series, tile_list):
    piece = series.shape[0]
    col_count = lax.axis_size("cols")
    n_rows = lax.axis_size("rows")
    result = fused_call(tile_list, series.reshape(piece // 128, 128), n_rows, col_count)
    return jnp.maximum(result, jnp.float32(-1.0)).reshape(piece)


def solution(mesh):
    in_specs = (P(("rows", "cols")), P(None, "rows"))
    out_specs = P(("rows", "cols"))
    return jax.shard_map(
        on_device, mesh=mesh, in_specs=in_specs, out_specs=out_specs, check_vma=False
    )
```

```python
import math

import jax
import jax.numpy as jnp
from jax import lax
from jax.experimental import pallas as pl
from jax.experimental.pallas import tpu as pltpu
from jax.sharding import PartitionSpec as P

M = 256
B = 512
BPR = 128
EXCL = 64
SPILL = 8
SEG = B + M
MESH = pl.DeviceIdType.MESH


def passed_along(block, axis, distance):
    devices = range(lax.axis_size(axis))
    route = [(i - distance, i) for i in devices if i - distance in devices]
    return lax.ppermute(block, axis, route)


def windows(held, b):
    per = B // 128
    seg = jnp.concatenate([held[pl.ds(b * per + v, 1), :] for v in range(SEG // 128)], axis=1)
    parts = []
    for m in range(B // 128):
        lo = 3 * 128 - 128 * m
        sub = jnp.broadcast_to(seg[:, lo:lo + 3 * 128], (128, 3 * 128))
        parts.append(pltpu.roll(sub, 1, 1, stride=1, stride_axis=0)[:, 128:])
    w = jnp.concatenate(parts, axis=0)
    centre = w - jnp.mean(w, axis=1, keepdims=True)
    spread = jnp.mean(centre * centre, axis=1, keepdims=True)
    factor = lax.rsqrt(spread + 1e-05) / math.sqrt(M)
    return centre * factor


def split_dot(a, b):
    a_hi = a.astype(jnp.bfloat16)
    b_hi = b.astype(jnp.bfloat16)
    a_lo = (a - a_hi.astype(jnp.float32)).astype(jnp.bfloat16)
    b_lo = (b - b_hi.astype(jnp.float32)).astype(jnp.bfloat16)
    dims = (((1,), (1,)), ((), ()))

    def dot(x, y):
        return lax.dot_general(x, y, dims, preferred_element_type=jnp.float32)

    lhs = jnp.concatenate([a_hi, a_hi, a_lo], axis=1)
    rhs = jnp.concatenate([b_hi, b_lo, b_hi], axis=1)
    return dot(lhs, rhs)


def reverse_lanes(x, mirror):
    hi = x.astype(jnp.bfloat16)
    rest = x - hi.astype(jnp.float32)
    mid = rest.astype(jnp.bfloat16)
    lo = (rest - mid.astype(jnp.float32)).astype(jnp.bfloat16)

    def dot(part):
        return jnp.dot(part, mirror, preferred_element_type=jnp.float32)

    return (dot(hi) + dot(mid)) + dot(lo)


def greet_partners(n_rows, n_cols, before_wait):
    g = lax.axis_index("rows")
    c = lax.axis_index("cols")
    barrier = pltpu.get_barrier_semaphore()
    half = (c // 2) % 2
    for p in range(n_cols):
        @pl.when(p != c)
        def _():
            pl.semaphore_signal(barrier, 1, device_id=(g, p), device_id_type=MESH)

    has_next = g + 1 < n_rows

    @pl.when(has_next)
    def _():
        pl.semaphore_signal(barrier, 1, device_id=(g + 1, 0), device_id_type=MESH)

    down = jnp.logical_and(c == 0, g > 0)

    @pl.when(down)
    def _():
        for p in range(n_cols):
            pl.semaphore_signal(barrier, 1, device_id=(g - 1, p), device_id_type=MESH)

    collector = jnp.logical_or(c == 0, c == 2)
    up = jnp.logical_and(collector, has_next)
    count = (n_cols - 1) + has_next.astype(jnp.int32) + n_cols * down.astype(jnp.int32)
    before_wait()
    pl.semaphore_wait(barrier, count)
    return g, c, half, collector, up, down


def half_peers(n_cols, c, half):
    return [
        (p, jnp.logical_and(p != c, (p // 2) % 2 == half)) for p in range(n_cols)
    ]


def fused_kernel(n_rows, n_cols, n_tiles, tiles_ref, piece_ref, out_ref,
                 held, res, spill_out, spills, diff_ref, flip_ref,
                 g_send, g_recv, r_send, r_recv, s_send, s_recv):
    spills[...] = jnp.full(spills.shape, -1.0, jnp.float32)

    def tables():
        r_i = lax.broadcasted_iota(jnp.int32, (B, B), 0)
        r_j = lax.broadcasted_iota(jnp.int32, (B, B), 1)
        diff_ref[...] = r_i - r_j
        flip_ref[...] = jnp.where(r_i + r_j == B - 1, 1.0, 0.0)

    g, c, half, collector, up, down = greet_partners(n_rows, n_cols, tables)
    mate = c ^ 2
    head = n_cols
    rows = SPILL * B // 128
    peers = half_peers(n_cols, c, half)

    def slab(ref, k):
        if isinstance(k, int):
            return ref.at[pl.ds(k * rows, rows)]
        return ref.at[pl.ds(pl.multiple_of(k * rows, rows), rows)]

    def remote(src, slot, sem, device):
        return pltpu.make_async_remote_copy(
            src_ref=src,
            dst_ref=slab(held, slot),
            send_sem=g_send.at[sem],
            recv_sem=g_recv.at[slot],
            device_id=device,
            device_id_type=MESH,
        )

    to_mate = remote(piece_ref, c, 0, (g, mate))
    to_mate.start()

    for p, live in peers:
        @pl.when(live)
        def _():
            remote(piece_ref, c, 3 + 3 * p, (g, p)).start()

    @pl.when(down)
    def _():
        remote(piece_ref, head, 1, (g - 1, 0)).start()
        remote(piece_ref, head, 2, (g - 1, 2)).start()

    @pl.when(g + 1 == n_rows)
    def _():
        held[pl.ds(head * rows, rows), :] = jnp.zeros(piece_ref.shape, jnp.float32)

    remote(piece_ref, mate, 0, (g, mate)).wait_recv()

    @pl.when(up)
    def _():
        remote(piece_ref, head, 1, (g + 1, 0)).wait_recv()

    for p, live in peers:
        @pl.when(live)
        def _():
            remote(slab(held, mate), mate, 4 + 3 * p, (g, p)).start()

        @pl.when(jnp.logical_and(live, up))
        def _():
            remote(slab(held, head), head, 5 + 3 * p, (g, p)).start()

    held[pl.ds(pl.multiple_of(c * rows, rows), rows), :] = piece_ref[...]

    for p, live in peers:
        @pl.when(live)
        def _():
            remote(piece_ref, p, 3 + 3 * p, (g, p)).wait_recv()
            remote(piece_ref, p ^ 2, 3 + 3 * p, (g, p)).wait_recv()

    @pl.when(jnp.logical_and(jnp.logical_not(collector), g + 1 < n_rows))
    def _():
        remote(piece_ref, head, 1, (g, 0)).wait_recv()

    def result_copy(p, sender, t):
        return pltpu.make_async_remote_copy(
            src_ref=res.at[sender, t],
            dst_ref=res.at[sender, t],
            send_sem=r_send.at[p],
            recv_sem=r_recv.at[sender],
            device_id=(g, p),
            device_id_type=MESH,
        )

    def all_results(p, sender):
        return pltpu.make_async_remote_copy(
            src_ref=res.at[sender],
            dst_ref=res.at[sender],
            send_sem=r_send.at[p],
            recv_sem=r_recv.at[sender],
            device_id=(g, p),
            device_id_type=MESH,
        )

    m_i = lax.broadcasted_iota(jnp.int32, (128, 128), 0)
    m_j = lax.broadcasted_iota(jnp.int32, (128, 128), 1)
    mirror = jnp.where(m_i + m_j == 127, 1.0, 0.0).astype(jnp.bfloat16)

    def body(t, carry):
        col = c + n_cols * t
        i = jnp.clip(tiles_ref[0, col] - g * BPR, 0, BPR - 1)
        d = jnp.clip(tiles_ref[1, col], 0, SPILL - 1)
        j = i + d
        zl = windows(held, i)
        zr = windows(held, j)
        corr = split_dot(zl, zr)
        corr = jnp.where(diff_ref[...] >= EXCL - d * B, corr, jnp.float32(-1.0))
        row_c = jnp.max(corr, axis=1, keepdims=True)
        row_max = jnp.sum(row_c * flip_ref[...], axis=0, keepdims=True)
        col_r = jnp.max(corr, axis=0, keepdims=True)
        sub = lax.broadcasted_iota(jnp.int32, (8, 128), 0)
        slab_v = jnp.full((8, 128), -1.0, jnp.float32)
        nb = B // 128
        for v in range(nb):
            slab_v = jnp.where(sub == v, row_max[:, v * 128:(v + 1) * 128], slab_v)
            slab_v = jnp.where(sub == nb + v, col_r[:, (nb - 1 - v) * 128:(nb - v) * 128], slab_v)
        slab_v = jnp.where(sub < nb, slab_v, reverse_lanes(slab_v, mirror))
        res[c, t] = slab_v
        for p in range(n_cols):
            @pl.when(p != c)
            def _():
                result_copy(p, c, t).start()
        return carry

    lax.fori_loop(0, n_tiles, body, 0, unroll=True)

    has_next = g + 1 < n_rows
    sub = lax.broadcasted_iota(jnp.int32, (8, 128), 0)
    top = sub < 4

    def gather_blocks(senders, base, acc):
        for sender, t in senders:
            col = sender + n_cols * t
            i = jnp.clip(tiles_ref[0, col] - g * BPR, 0, BPR - 1) - base
            j = i + jnp.clip(tiles_ref[1, col], 0, SPILL - 1)
            slab_v = res[sender, t]
            flipped = pltpu.roll(slab_v, 4, 0)
            for m in range(len(acc)):
                even, odd = 2 * m, 2 * m + 1
                take = jnp.logical_or(jnp.logical_and(top, i == even), jnp.logical_and(jnp.logical_not(top), j == odd))
                take_f = jnp.logical_or(jnp.logical_and(jnp.logical_not(top), i == odd), jnp.logical_and(top, j == even))
                acc[m] = jnp.maximum(acc[m], jnp.maximum(
                    jnp.where(take, slab_v, jnp.float32(-1.0)),
                    jnp.where(take_f, flipped, jnp.float32(-1.0))))
        return acc

    quads = SPILL // 2
    spill_acc = gather_blocks([(c, t) for t in range(n_tiles)], BPR,
                              [jnp.full((8, 128), -1.0, jnp.float32) for _ in range(quads)])
    for m in range(quads):
        spill_out[pl.ds(8 * m, 8), :] = spill_acc[m]

    def spill_up():
        return pltpu.make_async_remote_copy(
            src_ref=spill_out,
            dst_ref=spills.at[c],
            send_sem=s_send.at[0],
            recv_sem=s_recv.at[0],
            device_id=(g + 1, 0),
            device_id_type=MESH,
        )

    @pl.when(has_next)
    def _():
        spill_up().start()


    base = c * SPILL
    acc = [jnp.full((8, 128), -1.0, jnp.float32) for _ in range(quads)]
    for sender in range(n_cols):
        @pl.when(sender != c)
        def _():
            all_results(sender, sender).wait_recv()

        acc = gather_blocks([(sender, t) for t in range(n_tiles)], base, acc)

    @pl.when(down)
    def _():
        pltpu.make_async_remote_copy(
            src_ref=spills,
            dst_ref=spills,
            send_sem=s_send.at[0],
            recv_sem=s_recv.at[0],
            device_id=(g - 1, 0),
            device_id_type=MESH,
        ).wait_recv()

    spilled = jnp.max(spills[...], axis=0)
    for m in range(quads):
        out_ref[pl.ds(8 * m, 8), :] = jnp.maximum(acc[m], spilled[8 * m:8 * m + 8])

    to_mate.wait_send()

    @pl.when(down)
    def _():
        remote(piece_ref, head, 1, (g - 1, 0)).wait_send()
        remote(piece_ref, head, 2, (g - 1, 2)).wait_send()

    for p, live in peers:
        @pl.when(live)
        def _():
            remote(piece_ref, c, 3 + 3 * p, (g, p)).wait_send()
            remote(piece_ref, c, 4 + 3 * p, (g, p)).wait_send()

        @pl.when(jnp.logical_and(live, up))
        def _():
            remote(piece_ref, c, 5 + 3 * p, (g, p)).wait_send()

    for p in range(n_cols):
        @pl.when(p != c)
        def _():
            all_results(p, c).wait_send()

    @pl.when(has_next)
    def _():
        spill_up().wait_send()


def fused_call(tiles, piece, n_rows, n_cols):
    n_tiles = tiles.shape[1] // n_cols
    slots = n_cols + 1
    chunk = piece.shape
    return pl.pallas_call(
        lambda *refs: fused_kernel(n_rows, n_cols, n_tiles, *refs),
        out_shape=jax.ShapeDtypeStruct(chunk, jnp.float32),
        in_specs=[
            pl.BlockSpec(memory_space=pltpu.SMEM),
            pl.BlockSpec(memory_space=pltpu.VMEM),
        ],
        out_specs=pl.BlockSpec(memory_space=pltpu.VMEM),
        scratch_shapes=[
            pltpu.VMEM((slots * chunk[0], 128), jnp.float32),
            pltpu.VMEM((n_cols, n_tiles, 8, 128), jnp.float32),
            pltpu.VMEM(chunk, jnp.float32),
            pltpu.VMEM((n_cols,) + chunk, jnp.float32),
            pltpu.VMEM((B, B), jnp.int32),
            pltpu.VMEM((B, B), jnp.float32),
            pltpu.SemaphoreType.DMA((3 + 3 * n_cols,)),
            pltpu.SemaphoreType.DMA((slots,)),
            pltpu.SemaphoreType.DMA((n_cols,)),
            pltpu.SemaphoreType.DMA((n_cols,)),
            pltpu.SemaphoreType.DMA((1,)),
            pltpu.SemaphoreType.DMA((1,)),
        ],
        cost_estimate=pl.CostEstimate(
            flops=n_tiles * 2 * B * B * M * 3,
            bytes_accessed=slots * chunk[0] * 128 * 4,
            transcendentals=n_tiles * 2 * B,
        ),
        compiler_params=pltpu.CompilerParams(collective_id=0, has_side_effects=True),
    )(tiles, piece)


def on_device(series, tile_list):
    piece = series.shape[0]
    col_count = lax.axis_size("cols")
    n_rows = lax.axis_size("rows")
    result = fused_call(tile_list, series.reshape(piece // 128, 128), n_rows, col_count)
    return jnp.maximum(result, jnp.float32(-1.0)).reshape(piece)


def solution(mesh):
    in_specs = (P(("rows", "cols")), P(None, "rows"))
    out_specs = P(("rows", "cols"))
    return jax.shard_map(
        on_device, mesh=mesh, in_specs=in_specs, out_specs=out_specs, check_vma=False
    )
```

```python
import math

import jax
import jax.numpy as jnp
from jax import lax
from jax.experimental import pallas as pl
from jax.experimental.pallas import tpu as pltpu
from jax.sharding import PartitionSpec as P

M = 256
B = 512
BPR = 128
EXCL = 64
SPILL = 8
SEG = B + M
MESH = pl.DeviceIdType.MESH


def passed_along(block, axis, distance):
    devices = range(lax.axis_size(axis))
    route = [(i - distance, i) for i in devices if i - distance in devices]
    return lax.ppermute(block, axis, route)


def windows(held, b):
    per = B // 128
    seg = jnp.concatenate([held[pl.ds(b * per + v, 1), :] for v in range(SEG // 128)], axis=1)
    parts = []
    for m in range(B // 128):
        lo = 3 * 128 - 128 * m
        sub = jnp.broadcast_to(seg[:, lo:lo + 3 * 128], (128, 3 * 128))
        parts.append(pltpu.roll(sub, 1, 1, stride=1, stride_axis=0)[:, 128:])
    w = jnp.concatenate(parts, axis=0)
    centre = w - jnp.mean(w, axis=1, keepdims=True)
    spread = jnp.mean(centre * centre, axis=1, keepdims=True)
    factor = lax.rsqrt(spread + 1e-05) / math.sqrt(M)
    return centre * factor


def split_dot(a, b):
    a_hi = a.astype(jnp.bfloat16)
    b_hi = b.astype(jnp.bfloat16)
    a_lo = (a - a_hi.astype(jnp.float32)).astype(jnp.bfloat16)
    b_lo = (b - b_hi.astype(jnp.float32)).astype(jnp.bfloat16)
    dims = (((1,), (1,)), ((), ()))

    def dot(x, y):
        return lax.dot_general(x, y, dims, preferred_element_type=jnp.float32)

    return dot(a_hi, b_hi) + (dot(a_hi, b_lo) + dot(a_lo, b_hi))


def reverse_lanes(x, mirror):
    hi = x.astype(jnp.bfloat16)
    rest = x - hi.astype(jnp.float32)
    mid = rest.astype(jnp.bfloat16)
    lo = (rest - mid.astype(jnp.float32)).astype(jnp.bfloat16)

    def dot(part):
        return jnp.dot(part, mirror, preferred_element_type=jnp.float32)

    return (dot(hi) + dot(mid)) + dot(lo)


def greet_partners(n_rows, n_cols, before_wait):
    g = lax.axis_index("rows")
    c = lax.axis_index("cols")
    barrier = pltpu.get_barrier_semaphore()
    half = (c // 2) % 2
    for p in range(n_cols):
        @pl.when(p != c)
        def _():
            pl.semaphore_signal(barrier, 1, device_id=(g, p), device_id_type=MESH)

    has_next = g + 1 < n_rows

    @pl.when(has_next)
    def _():
        pl.semaphore_signal(barrier, 1, device_id=(g + 1, 0), device_id_type=MESH)

    down = jnp.logical_and(c == 0, g > 0)

    @pl.when(down)
    def _():
        for p in range(n_cols):
            pl.semaphore_signal(barrier, 1, device_id=(g - 1, p), device_id_type=MESH)

    collector = jnp.logical_or(c == 0, c == 2)
    up = jnp.logical_and(collector, has_next)
    count = (n_cols - 1) + has_next.astype(jnp.int32) + n_cols * down.astype(jnp.int32)
    before_wait()
    pl.semaphore_wait(barrier, count)
    return g, c, half, collector, up, down


def half_peers(n_cols, c, half):
    return [
        (p, jnp.logical_and(p != c, (p // 2) % 2 == half)) for p in range(n_cols)
    ]


def fused_kernel(n_rows, n_cols, n_tiles, tiles_ref, piece_ref, out_ref,
                 held, res, spill_out, spills, diff_ref, flip_ref,
                 g_send, g_recv, r_send, r_recv, s_send, s_recv):
    spills[...] = jnp.full(spills.shape, -1.0, jnp.float32)

    def tables():
        r_i = lax.broadcasted_iota(jnp.int32, (B, B), 0)
        r_j = lax.broadcasted_iota(jnp.int32, (B, B), 1)
        diff_ref[...] = r_i - r_j
        flip_ref[...] = jnp.where(r_i + r_j == B - 1, 1.0, 0.0)

    g, c, half, collector, up, down = greet_partners(n_rows, n_cols, tables)
    mate = c ^ 2
    head = n_cols
    rows = SPILL * B // 128
    peers = half_peers(n_cols, c, half)

    def slab(ref, k):
        if isinstance(k, int):
            return ref.at[pl.ds(k * rows, rows)]
        return ref.at[pl.ds(pl.multiple_of(k * rows, rows), rows)]

    def remote(src, slot, sem, device):
        return pltpu.make_async_remote_copy(
            src_ref=src,
            dst_ref=slab(held, slot),
            send_sem=g_send.at[sem],
            recv_sem=g_recv.at[slot],
            device_id=device,
            device_id_type=MESH,
        )

    to_mate = remote(piece_ref, c, 0, (g, mate))
    to_mate.start()

    for p, live in peers:
        @pl.when(live)
        def _():
            remote(piece_ref, c, 3 + 3 * p, (g, p)).start()

    @pl.when(down)
    def _():
        remote(piece_ref, head, 1, (g - 1, 0)).start()
        remote(piece_ref, head, 2, (g - 1, 2)).start()

    @pl.when(g + 1 == n_rows)
    def _():
        held[pl.ds(head * rows, rows), :] = jnp.zeros(piece_ref.shape, jnp.float32)

    remote(piece_ref, mate, 0, (g, mate)).wait_recv()

    for p, live in peers:
        @pl.when(live)
        def _():
            remote(slab(held, mate), mate, 4 + 3 * p, (g, p)).start()

    @pl.when(up)
    def _():
        remote(piece_ref, head, 1, (g + 1, 0)).wait_recv()

    for p, live in peers:
        @pl.when(jnp.logical_and(live, up))
        def _():
            remote(slab(held, head), head, 5 + 3 * p, (g, p)).start()

    held[pl.ds(pl.multiple_of(c * rows, rows), rows), :] = piece_ref[...]

    for p, live in peers:
        @pl.when(live)
        def _():
            remote(piece_ref, p, 3 + 3 * p, (g, p)).wait_recv()
            remote(piece_ref, p ^ 2, 3 + 3 * p, (g, p)).wait_recv()

    @pl.when(jnp.logical_and(jnp.logical_not(collector), g + 1 < n_rows))
    def _():
        remote(piece_ref, head, 1, (g, 0)).wait_recv()

    def result_copy(p, sender, t):
        return pltpu.make_async_remote_copy(
            src_ref=res.at[sender, t],
            dst_ref=res.at[sender, t],
            send_sem=r_send.at[p],
            recv_sem=r_recv.at[sender],
            device_id=(g, p),
            device_id_type=MESH,
        )

    def all_results(p, sender):
        return pltpu.make_async_remote_copy(
            src_ref=res.at[sender],
            dst_ref=res.at[sender],
            send_sem=r_send.at[p],
            recv_sem=r_recv.at[sender],
            device_id=(g, p),
            device_id_type=MESH,
        )

    m_i = lax.broadcasted_iota(jnp.int32, (128, 128), 0)
    m_j = lax.broadcasted_iota(jnp.int32, (128, 128), 1)
    mirror = jnp.where(m_i + m_j == 127, 1.0, 0.0).astype(jnp.bfloat16)

    def body(t, carry):
        col = c + n_cols * t
        i = jnp.clip(tiles_ref[0, col] - g * BPR, 0, BPR - 1)
        d = jnp.clip(tiles_ref[1, col], 0, SPILL - 1)
        j = i + d
        zl = windows(held, i)
        zr = windows(held, j)
        corr = split_dot(zl, zr)
        corr = jnp.where(diff_ref[...] >= EXCL - d * B, corr, jnp.float32(-1.0))
        row_c = jnp.max(corr, axis=1, keepdims=True)
        row_max = jnp.sum(row_c * flip_ref[...], axis=0, keepdims=True)
        col_r = jnp.max(corr, axis=0, keepdims=True)
        sub = lax.broadcasted_iota(jnp.int32, (8, 128), 0)
        slab_v = jnp.full((8, 128), -1.0, jnp.float32)
        nb = B // 128
        for v in range(nb):
            slab_v = jnp.where(sub == v, row_max[:, v * 128:(v + 1) * 128], slab_v)
            slab_v = jnp.where(sub == nb + v, col_r[:, (nb - 1 - v) * 128:(nb - v) * 128], slab_v)
        slab_v = jnp.where(sub < nb, slab_v, reverse_lanes(slab_v, mirror))
        res[c, t] = slab_v
        for p in range(n_cols):
            @pl.when(p != c)
            def _():
                result_copy(p, c, t).start()
        return carry

    lax.fori_loop(0, n_tiles, body, 0, unroll=True)

    has_next = g + 1 < n_rows
    sub = lax.broadcasted_iota(jnp.int32, (8, 128), 0)
    top = sub < 4

    def gather_blocks(senders, base, acc):
        for sender, t in senders:
            col = sender + n_cols * t
            i = jnp.clip(tiles_ref[0, col] - g * BPR, 0, BPR - 1) - base
            j = i + jnp.clip(tiles_ref[1, col], 0, SPILL - 1)
            slab_v = res[sender, t]
            flipped = pltpu.roll(slab_v, 4, 0)
            for m in range(len(acc)):
                even, odd = 2 * m, 2 * m + 1
                take = jnp.logical_or(jnp.logical_and(top, i == even), jnp.logical_and(jnp.logical_not(top), j == odd))
                take_f = jnp.logical_or(jnp.logical_and(jnp.logical_not(top), i == odd), jnp.logical_and(top, j == even))
                acc[m] = jnp.maximum(acc[m], jnp.maximum(
                    jnp.where(take, slab_v, jnp.float32(-1.0)),
                    jnp.where(take_f, flipped, jnp.float32(-1.0))))
        return acc

    quads = SPILL // 2
    spill_acc = gather_blocks([(c, t) for t in range(n_tiles)], BPR,
                              [jnp.full((8, 128), -1.0, jnp.float32) for _ in range(quads)])
    for m in range(quads):
        spill_out[pl.ds(8 * m, 8), :] = spill_acc[m]

    def spill_up():
        return pltpu.make_async_remote_copy(
            src_ref=spill_out,
            dst_ref=spills.at[c],
            send_sem=s_send.at[0],
            recv_sem=s_recv.at[0],
            device_id=(g + 1, 0),
            device_id_type=MESH,
        )

    @pl.when(has_next)
    def _():
        spill_up().start()


    base = c * SPILL
    acc = [jnp.full((8, 128), -1.0, jnp.float32) for _ in range(quads)]
    for sender in range(n_cols):
        @pl.when(sender != c)
        def _():
            all_results(sender, sender).wait_recv()

        acc = gather_blocks([(sender, t) for t in range(n_tiles)], base, acc)

    @pl.when(down)
    def _():
        pltpu.make_async_remote_copy(
            src_ref=spills,
            dst_ref=spills,
            send_sem=s_send.at[0],
            recv_sem=s_recv.at[0],
            device_id=(g - 1, 0),
            device_id_type=MESH,
        ).wait_recv()

    spilled = jnp.max(spills[...], axis=0)
    for m in range(quads):
        out_ref[pl.ds(8 * m, 8), :] = jnp.maximum(acc[m], spilled[8 * m:8 * m + 8])

    to_mate.wait_send()

    @pl.when(down)
    def _():
        remote(piece_ref, head, 1, (g - 1, 0)).wait_send()
        remote(piece_ref, head, 2, (g - 1, 2)).wait_send()

    for p, live in peers:
        @pl.when(live)
        def _():
            remote(piece_ref, c, 3 + 3 * p, (g, p)).wait_send()
            remote(piece_ref, c, 4 + 3 * p, (g, p)).wait_send()

        @pl.when(jnp.logical_and(live, up))
        def _():
            remote(piece_ref, c, 5 + 3 * p, (g, p)).wait_send()

    for p in range(n_cols):
        @pl.when(p != c)
        def _():
            all_results(p, c).wait_send()

    @pl.when(has_next)
    def _():
        spill_up().wait_send()


def fused_call(tiles, piece, n_rows, n_cols):
    n_tiles = tiles.shape[1] // n_cols
    slots = n_cols + 1
    chunk = piece.shape
    return pl.pallas_call(
        lambda *refs: fused_kernel(n_rows, n_cols, n_tiles, *refs),
        out_shape=jax.ShapeDtypeStruct(chunk, jnp.float32),
        in_specs=[
            pl.BlockSpec(memory_space=pltpu.SMEM),
            pl.BlockSpec(memory_space=pltpu.VMEM),
        ],
        out_specs=pl.BlockSpec(memory_space=pltpu.VMEM),
        scratch_shapes=[
            pltpu.VMEM((slots * chunk[0], 128), jnp.float32),
            pltpu.VMEM((n_cols, n_tiles, 8, 128), jnp.float32),
            pltpu.VMEM(chunk, jnp.float32),
            pltpu.VMEM((n_cols,) + chunk, jnp.float32),
            pltpu.VMEM((B, B), jnp.int32),
            pltpu.VMEM((B, B), jnp.float32),
            pltpu.SemaphoreType.DMA((3 + 3 * n_cols,)),
            pltpu.SemaphoreType.DMA((slots,)),
            pltpu.SemaphoreType.DMA((n_cols,)),
            pltpu.SemaphoreType.DMA((n_cols,)),
            pltpu.SemaphoreType.DMA((1,)),
            pltpu.SemaphoreType.DMA((1,)),
        ],
        cost_estimate=pl.CostEstimate(
            flops=n_tiles * 2 * B * B * M * 3,
            bytes_accessed=slots * chunk[0] * 128 * 4,
            transcendentals=n_tiles * 2 * B,
        ),
        compiler_params=pltpu.CompilerParams(collective_id=0, has_side_effects=True),
    )(tiles, piece)


def on_device(series, tile_list):
    piece = series.shape[0]
    col_count = lax.axis_size("cols")
    n_rows = lax.axis_size("rows")
    result = fused_call(tile_list, series.reshape(piece // 128, 128), n_rows, col_count)
    return jnp.maximum(result, jnp.float32(-1.0)).reshape(piece)


def solution(mesh):
    in_specs = (P(("rows", "cols")), P(None, "rows"))
    out_specs = P(("rows", "cols"))
    return jax.shard_map(
        on_device, mesh=mesh, in_specs=in_specs, out_specs=out_specs, check_vma=False
    )
```

```python
import math

import jax
import jax.numpy as jnp
from jax import lax
from jax.experimental import pallas as pl
from jax.experimental.pallas import tpu as pltpu
from jax.sharding import PartitionSpec as P

M = 256
B = 512
BPR = 128
EXCL = 64
SPILL = 8
SEG = B + M
MESH = pl.DeviceIdType.MESH


def passed_along(block, axis, distance):
    devices = range(lax.axis_size(axis))
    route = [(i - distance, i) for i in devices if i - distance in devices]
    return lax.ppermute(block, axis, route)


def windows(held, b):
    per = B // 128
    seg = jnp.concatenate([held[pl.ds(b * per + v, 1), :] for v in range(SEG // 128)], axis=1)
    parts = []
    for m in range(B // 128):
        lo = 3 * 128 - 128 * m
        sub = jnp.broadcast_to(seg[:, lo:lo + 3 * 128], (128, 3 * 128))
        parts.append(pltpu.roll(sub, 1, 1, stride=1, stride_axis=0)[:, 128:])
    w = jnp.concatenate(parts, axis=0)
    centre = w - jnp.mean(w, axis=1, keepdims=True)
    spread = jnp.mean(centre * centre, axis=1, keepdims=True)
    factor = lax.rsqrt(spread + 1e-05) / math.sqrt(M)
    return centre * factor


def split_dot(a, b):
    a_hi = a.astype(jnp.bfloat16)
    b_hi = b.astype(jnp.bfloat16)
    a_lo = (a - a_hi.astype(jnp.float32)).astype(jnp.bfloat16)
    b_lo = (b - b_hi.astype(jnp.float32)).astype(jnp.bfloat16)
    dims = (((1,), (1,)), ((), ()))

    def dot(x, y):
        return lax.dot_general(x, y, dims, preferred_element_type=jnp.float32)

    return dot(a_hi, b_hi) + (dot(a_hi, b_lo) + dot(a_lo, b_hi))


def reverse_lanes(x, mirror):
    hi = x.astype(jnp.bfloat16)
    rest = x - hi.astype(jnp.float32)
    mid = rest.astype(jnp.bfloat16)
    lo = (rest - mid.astype(jnp.float32)).astype(jnp.bfloat16)

    def dot(part):
        return jnp.dot(part, mirror, preferred_element_type=jnp.float32)

    return (dot(hi) + dot(mid)) + dot(lo)


def greet_partners(n_rows, n_cols, before_wait):
    g = lax.axis_index("rows")
    c = lax.axis_index("cols")
    barrier = pltpu.get_barrier_semaphore()
    half = (c // 2) % 2
    for p in range(n_cols):
        @pl.when(p != c)
        def _():
            pl.semaphore_signal(barrier, 1, device_id=(g, p), device_id_type=MESH)

    has_next = g + 1 < n_rows

    @pl.when(has_next)
    def _():
        pl.semaphore_signal(barrier, 1, device_id=(g + 1, 0), device_id_type=MESH)

    down = jnp.logical_and(c == 0, g > 0)

    @pl.when(down)
    def _():
        for p in range(n_cols):
            pl.semaphore_signal(barrier, 1, device_id=(g - 1, p), device_id_type=MESH)

    collector = jnp.logical_or(c == 0, c == 2)
    up = jnp.logical_and(collector, has_next)
    count = (n_cols - 1) + has_next.astype(jnp.int32) + n_cols * down.astype(jnp.int32)
    before_wait()
    pl.semaphore_wait(barrier, count)
    return g, c, half, collector, up, down


def half_peers(n_cols, c, half):
    return [
        (p, jnp.logical_and(p != c, (p // 2) % 2 == half)) for p in range(n_cols)
    ]


def fused_kernel(n_rows, n_cols, n_tiles, tiles_ref, piece_ref, out_ref,
                 held, res, spill_out, spills, diff_ref, flip_ref,
                 g_send, g_recv, r_send, r_recv, s_send, s_recv):
    spills[...] = jnp.full(spills.shape, -1.0, jnp.float32)

    def tables():
        r_i = lax.broadcasted_iota(jnp.int32, (B, B), 0)
        r_j = lax.broadcasted_iota(jnp.int32, (B, B), 1)
        diff_ref[...] = r_i - r_j
        flip_ref[...] = jnp.where(r_i + r_j == B - 1, 1.0, 0.0)

    g, c, half, collector, up, down = greet_partners(n_rows, n_cols, tables)
    mate = c ^ 2
    head = n_cols
    rows = SPILL * B // 128
    peers = half_peers(n_cols, c, half)

    def slab(ref, k):
        if isinstance(k, int):
            return ref.at[pl.ds(k * rows, rows)]
        return ref.at[pl.ds(pl.multiple_of(k * rows, rows), rows)]

    def remote(src, slot, sem, device):
        return pltpu.make_async_remote_copy(
            src_ref=src,
            dst_ref=slab(held, slot),
            send_sem=g_send.at[sem],
            recv_sem=g_recv.at[slot],
            device_id=device,
            device_id_type=MESH,
        )

    to_mate = remote(piece_ref, c, 0, (g, mate))
    to_mate.start()

    for p, live in peers:
        @pl.when(live)
        def _():
            remote(piece_ref, c, 3 + 3 * p, (g, p)).start()

    @pl.when(down)
    def _():
        remote(piece_ref, head, 1, (g - 1, 0)).start()
        remote(piece_ref, head, 2, (g - 1, 2)).start()

    @pl.when(g + 1 == n_rows)
    def _():
        held[pl.ds(head * rows, rows), :] = jnp.zeros(piece_ref.shape, jnp.float32)

    remote(piece_ref, mate, 0, (g, mate)).wait_recv()

    for p, live in peers:
        @pl.when(live)
        def _():
            remote(slab(held, mate), mate, 4 + 3 * p, (g, p)).start()

    @pl.when(up)
    def _():
        remote(piece_ref, head, 1, (g + 1, 0)).wait_recv()

    for p, live in peers:
        @pl.when(jnp.logical_and(live, up))
        def _():
            remote(slab(held, head), head, 5 + 3 * p, (g, p)).start()

    held[pl.ds(pl.multiple_of(c * rows, rows), rows), :] = piece_ref[...]

    for p, live in peers:
        @pl.when(live)
        def _():
            remote(piece_ref, p, 3 + 3 * p, (g, p)).wait_recv()
            remote(piece_ref, p ^ 2, 3 + 3 * p, (g, p)).wait_recv()

    @pl.when(jnp.logical_and(jnp.logical_not(collector), g + 1 < n_rows))
    def _():
        remote(piece_ref, head, 1, (g, 0)).wait_recv()

    def result_copy(p, sender, t):
        return pltpu.make_async_remote_copy(
            src_ref=res.at[sender, t],
            dst_ref=res.at[sender, t],
            send_sem=r_send.at[p],
            recv_sem=r_recv.at[sender],
            device_id=(g, p),
            device_id_type=MESH,
        )

    def all_results(p, sender):
        return pltpu.make_async_remote_copy(
            src_ref=res.at[sender],
            dst_ref=res.at[sender],
            send_sem=r_send.at[p],
            recv_sem=r_recv.at[sender],
            device_id=(g, p),
            device_id_type=MESH,
        )

    m_i = lax.broadcasted_iota(jnp.int32, (128, 128), 0)
    m_j = lax.broadcasted_iota(jnp.int32, (128, 128), 1)
    mirror = jnp.where(m_i + m_j == 127, 1.0, 0.0).astype(jnp.bfloat16)

    def body(t, carry):
        col = c + n_cols * t
        i = jnp.clip(tiles_ref[0, col] - g * BPR, 0, BPR - 1)
        d = jnp.clip(tiles_ref[1, col], 0, SPILL - 1)
        j = i + d
        zl = windows(held, i)
        zr = windows(held, j)
        corr = split_dot(zl, zr)
        corr = jnp.where(diff_ref[...] >= EXCL - d * B, corr, jnp.float32(-1.0))
        row_c = jnp.max(corr, axis=1, keepdims=True)
        row_max = jnp.sum(row_c * flip_ref[...], axis=0, keepdims=True)
        col_r = jnp.max(corr, axis=0, keepdims=True)
        sub = lax.broadcasted_iota(jnp.int32, (8, 128), 0)
        slab_v = jnp.full((8, 128), -1.0, jnp.float32)
        nb = B // 128
        for v in range(nb):
            slab_v = jnp.where(sub == v, row_max[:, v * 128:(v + 1) * 128], slab_v)
            slab_v = jnp.where(sub == nb + v, col_r[:, (nb - 1 - v) * 128:(nb - v) * 128], slab_v)
        slab_v = jnp.where(sub < nb, slab_v, reverse_lanes(slab_v, mirror))
        res[c, t] = slab_v
        for near in (False, True):
            for p in range(n_cols):
                same = ((p // 2) % 2 == half)
                @pl.when(jnp.logical_and(p != c, same == near))
                def _():
                    result_copy(p, c, t).start()
        return carry

    lax.fori_loop(0, n_tiles, body, 0, unroll=True)

    has_next = g + 1 < n_rows
    sub = lax.broadcasted_iota(jnp.int32, (8, 128), 0)
    top = sub < 4

    def gather_blocks(senders, base, acc):
        for sender, t in senders:
            col = sender + n_cols * t
            i = jnp.clip(tiles_ref[0, col] - g * BPR, 0, BPR - 1) - base
            j = i + jnp.clip(tiles_ref[1, col], 0, SPILL - 1)
            slab_v = res[sender, t]
            flipped = pltpu.roll(slab_v, 4, 0)
            for m in range(len(acc)):
                even, odd = 2 * m, 2 * m + 1
                take = jnp.logical_or(jnp.logical_and(top, i == even), jnp.logical_and(jnp.logical_not(top), j == odd))
                take_f = jnp.logical_or(jnp.logical_and(jnp.logical_not(top), i == odd), jnp.logical_and(top, j == even))
                acc[m] = jnp.maximum(acc[m], jnp.maximum(
                    jnp.where(take, slab_v, jnp.float32(-1.0)),
                    jnp.where(take_f, flipped, jnp.float32(-1.0))))
        return acc

    quads = SPILL // 2
    spill_acc = gather_blocks([(c, t) for t in range(n_tiles)], BPR,
                              [jnp.full((8, 128), -1.0, jnp.float32) for _ in range(quads)])
    for m in range(quads):
        spill_out[pl.ds(8 * m, 8), :] = spill_acc[m]

    def spill_up():
        return pltpu.make_async_remote_copy(
            src_ref=spill_out,
            dst_ref=spills.at[c],
            send_sem=s_send.at[0],
            recv_sem=s_recv.at[0],
            device_id=(g + 1, 0),
            device_id_type=MESH,
        )

    @pl.when(has_next)
    def _():
        spill_up().start()


    base = c * SPILL
    acc = [jnp.full((8, 128), -1.0, jnp.float32) for _ in range(quads)]
    for sender in range(n_cols):
        @pl.when(sender != c)
        def _():
            all_results(sender, sender).wait_recv()

        acc = gather_blocks([(sender, t) for t in range(n_tiles)], base, acc)

    @pl.when(down)
    def _():
        pltpu.make_async_remote_copy(
            src_ref=spills,
            dst_ref=spills,
            send_sem=s_send.at[0],
            recv_sem=s_recv.at[0],
            device_id=(g - 1, 0),
            device_id_type=MESH,
        ).wait_recv()

    spilled = jnp.max(spills[...], axis=0)
    for m in range(quads):
        out_ref[pl.ds(8 * m, 8), :] = jnp.maximum(acc[m], spilled[8 * m:8 * m + 8])

    to_mate.wait_send()

    @pl.when(down)
    def _():
        remote(piece_ref, head, 1, (g - 1, 0)).wait_send()
        remote(piece_ref, head, 2, (g - 1, 2)).wait_send()

    for p, live in peers:
        @pl.when(live)
        def _():
            remote(piece_ref, c, 3 + 3 * p, (g, p)).wait_send()
            remote(piece_ref, c, 4 + 3 * p, (g, p)).wait_send()

        @pl.when(jnp.logical_and(live, up))
        def _():
            remote(piece_ref, c, 5 + 3 * p, (g, p)).wait_send()

    for p in range(n_cols):
        @pl.when(p != c)
        def _():
            all_results(p, c).wait_send()

    @pl.when(has_next)
    def _():
        spill_up().wait_send()


def fused_call(tiles, piece, n_rows, n_cols):
    n_tiles = tiles.shape[1] // n_cols
    slots = n_cols + 1
    chunk = piece.shape
    return pl.pallas_call(
        lambda *refs: fused_kernel(n_rows, n_cols, n_tiles, *refs),
        out_shape=jax.ShapeDtypeStruct(chunk, jnp.float32),
        in_specs=[
            pl.BlockSpec(memory_space=pltpu.SMEM),
            pl.BlockSpec(memory_space=pltpu.VMEM),
        ],
        out_specs=pl.BlockSpec(memory_space=pltpu.VMEM),
        scratch_shapes=[
            pltpu.VMEM((slots * chunk[0], 128), jnp.float32),
            pltpu.VMEM((n_cols, n_tiles, 8, 128), jnp.float32),
            pltpu.VMEM(chunk, jnp.float32),
            pltpu.VMEM((n_cols,) + chunk, jnp.float32),
            pltpu.VMEM((B, B), jnp.int32),
            pltpu.VMEM((B, B), jnp.float32),
            pltpu.SemaphoreType.DMA((3 + 3 * n_cols,)),
            pltpu.SemaphoreType.DMA((slots,)),
            pltpu.SemaphoreType.DMA((n_cols,)),
            pltpu.SemaphoreType.DMA((n_cols,)),
            pltpu.SemaphoreType.DMA((1,)),
            pltpu.SemaphoreType.DMA((1,)),
        ],
        cost_estimate=pl.CostEstimate(
            flops=n_tiles * 2 * B * B * M * 3,
            bytes_accessed=slots * chunk[0] * 128 * 4,
            transcendentals=n_tiles * 2 * B,
        ),
        compiler_params=pltpu.CompilerParams(collective_id=0, has_side_effects=True),
    )(tiles, piece)


def on_device(series, tile_list):
    piece = series.shape[0]
    col_count = lax.axis_size("cols")
    n_rows = lax.axis_size("rows")
    result = fused_call(tile_list, series.reshape(piece // 128, 128), n_rows, col_count)
    return jnp.maximum(result, jnp.float32(-1.0)).reshape(piece)


def solution(mesh):
    in_specs = (P(("rows", "cols")), P(None, "rows"))
    out_specs = P(("rows", "cols"))
    return jax.shard_map(
        on_device, mesh=mesh, in_specs=in_specs, out_specs=out_specs, check_vma=False
    )
```

```python
import math

import jax
import jax.numpy as jnp
from jax import lax
from jax.experimental import pallas as pl
from jax.experimental.pallas import tpu as pltpu
from jax.sharding import PartitionSpec as P

M = 256
B = 512
BPR = 128
EXCL = 64
SPILL = 8
SEG = B + M
MESH = pl.DeviceIdType.MESH


def passed_along(block, axis, distance):
    devices = range(lax.axis_size(axis))
    route = [(i - distance, i) for i in devices if i - distance in devices]
    return lax.ppermute(block, axis, route)


def windows(held, b):
    per = B // 128
    seg = jnp.concatenate([held[pl.ds(b * per + v, 1), :] for v in range(SEG // 128)], axis=1)
    parts = []
    for m in range(B // 128):
        lo = 3 * 128 - 128 * m
        sub = jnp.broadcast_to(seg[:, lo:lo + 3 * 128], (128, 3 * 128))
        parts.append(pltpu.roll(sub, 1, 1, stride=1, stride_axis=0)[:, 128:])
    w = jnp.concatenate(parts, axis=0)
    centre = w - jnp.mean(w, axis=1, keepdims=True)
    spread = jnp.mean(centre * centre, axis=1, keepdims=True)
    factor = lax.rsqrt(spread + 1e-05) / math.sqrt(M)
    return centre * factor


def split_dot(a, b):
    a_hi = a.astype(jnp.bfloat16)
    b_hi = b.astype(jnp.bfloat16)
    a_lo = (a - a_hi.astype(jnp.float32)).astype(jnp.bfloat16)
    b_lo = (b - b_hi.astype(jnp.float32)).astype(jnp.bfloat16)
    dims = (((1,), (1,)), ((), ()))

    def dot(x, y):
        return lax.dot_general(x, y, dims, preferred_element_type=jnp.float32)

    return dot(a_hi, b_hi) + (dot(a_hi, b_lo) + dot(a_lo, b_hi))


def reverse_lanes(x, mirror):
    hi = x.astype(jnp.bfloat16)
    rest = x - hi.astype(jnp.float32)
    mid = rest.astype(jnp.bfloat16)
    lo = (rest - mid.astype(jnp.float32)).astype(jnp.bfloat16)

    def dot(part):
        return jnp.dot(part, mirror, preferred_element_type=jnp.float32)

    return (dot(hi) + dot(mid)) + dot(lo)


def greet_partners(n_rows, n_cols, before_wait):
    g = lax.axis_index("rows")
    c = lax.axis_index("cols")
    barrier = pltpu.get_barrier_semaphore()
    half = (c // 2) % 2
    for p in range(n_cols):
        @pl.when(p != c)
        def _():
            pl.semaphore_signal(barrier, 1, device_id=(g, p), device_id_type=MESH)

    has_next = g + 1 < n_rows

    @pl.when(has_next)
    def _():
        pl.semaphore_signal(barrier, 1, device_id=(g + 1, 0), device_id_type=MESH)

    down = jnp.logical_and(c == 0, g > 0)

    @pl.when(down)
    def _():
        for p in range(n_cols):
            pl.semaphore_signal(barrier, 1, device_id=(g - 1, p), device_id_type=MESH)

    collector = jnp.logical_or(c == 0, c == 2)
    up = jnp.logical_and(collector, has_next)
    count = (n_cols - 1) + has_next.astype(jnp.int32) + n_cols * down.astype(jnp.int32)
    before_wait()
    pl.semaphore_wait(barrier, count)
    return g, c, half, collector, up, down


def half_peers(n_cols, c, half):
    return [
        (p, jnp.logical_and(p != c, (p // 2) % 2 == half)) for p in range(n_cols)
    ]


def fused_kernel(n_rows, n_cols, n_tiles, tiles_ref, piece_ref, out_ref,
                 held, res, spill_out, spills, diff_ref, flip_ref,
                 g_send, g_recv, r_send, r_recv, s_send, s_recv):
    spills[...] = jnp.full(spills.shape, -1.0, jnp.float32)

    def tables():
        r_i = lax.broadcasted_iota(jnp.int32, (B, B), 0)
        r_j = lax.broadcasted_iota(jnp.int32, (B, B), 1)
        diff_ref[...] = r_i - r_j
        flip_ref[...] = jnp.where(r_i + r_j == B - 1, 1.0, 0.0)

    g, c, half, collector, up, down = greet_partners(n_rows, n_cols, tables)
    mate = c ^ 2
    head = n_cols
    rows = SPILL * B // 128
    peers = half_peers(n_cols, c, half)

    def slab(ref, k):
        if isinstance(k, int):
            return ref.at[pl.ds(k * rows, rows)]
        return ref.at[pl.ds(pl.multiple_of(k * rows, rows), rows)]

    def remote(src, slot, sem, device):
        return pltpu.make_async_remote_copy(
            src_ref=src,
            dst_ref=slab(held, slot),
            send_sem=g_send.at[sem],
            recv_sem=g_recv.at[slot],
            device_id=device,
            device_id_type=MESH,
        )

    @pl.when(down)
    def _():
        remote(piece_ref, head, 2, (g - 1, 2)).start()
        remote(piece_ref, head, 1, (g - 1, 0)).start()

    to_mate = remote(piece_ref, c, 0, (g, mate))
    to_mate.start()

    for p, live in peers:
        @pl.when(live)
        def _():
            remote(piece_ref, c, 3 + 3 * p, (g, p)).start()

    @pl.when(g + 1 == n_rows)
    def _():
        held[pl.ds(head * rows, rows), :] = jnp.zeros(piece_ref.shape, jnp.float32)

    remote(piece_ref, mate, 0, (g, mate)).wait_recv()

    for p, live in peers:
        @pl.when(live)
        def _():
            remote(slab(held, mate), mate, 4 + 3 * p, (g, p)).start()

    @pl.when(up)
    def _():
        remote(piece_ref, head, 1, (g + 1, 0)).wait_recv()

    for p, live in peers:
        @pl.when(jnp.logical_and(live, up))
        def _():
            remote(slab(held, head), head, 5 + 3 * p, (g, p)).start()

    held[pl.ds(pl.multiple_of(c * rows, rows), rows), :] = piece_ref[...]

    for p, live in peers:
        @pl.when(live)
        def _():
            remote(piece_ref, p, 3 + 3 * p, (g, p)).wait_recv()
            remote(piece_ref, p ^ 2, 3 + 3 * p, (g, p)).wait_recv()

    @pl.when(jnp.logical_and(jnp.logical_not(collector), g + 1 < n_rows))
    def _():
        remote(piece_ref, head, 1, (g, 0)).wait_recv()

    def result_copy(p, sender, t):
        return pltpu.make_async_remote_copy(
            src_ref=res.at[sender, t],
            dst_ref=res.at[sender, t],
            send_sem=r_send.at[p],
            recv_sem=r_recv.at[sender],
            device_id=(g, p),
            device_id_type=MESH,
        )

    def all_results(p, sender):
        return pltpu.make_async_remote_copy(
            src_ref=res.at[sender],
            dst_ref=res.at[sender],
            send_sem=r_send.at[p],
            recv_sem=r_recv.at[sender],
            device_id=(g, p),
            device_id_type=MESH,
        )

    m_i = lax.broadcasted_iota(jnp.int32, (128, 128), 0)
    m_j = lax.broadcasted_iota(jnp.int32, (128, 128), 1)
    mirror = jnp.where(m_i + m_j == 127, 1.0, 0.0).astype(jnp.bfloat16)

    def body(t, carry):
        col = c + n_cols * t
        i = jnp.clip(tiles_ref[0, col] - g * BPR, 0, BPR - 1)
        d = jnp.clip(tiles_ref[1, col], 0, SPILL - 1)
        j = i + d
        zl = windows(held, i)
        zr = windows(held, j)
        corr = split_dot(zl, zr)
        corr = jnp.where(diff_ref[...] >= EXCL - d * B, corr, jnp.float32(-1.0))
        row_c = jnp.max(corr, axis=1, keepdims=True)
        row_max = jnp.sum(row_c * flip_ref[...], axis=0, keepdims=True)
        col_r = jnp.max(corr, axis=0, keepdims=True)
        sub = lax.broadcasted_iota(jnp.int32, (8, 128), 0)
        slab_v = jnp.full((8, 128), -1.0, jnp.float32)
        nb = B // 128
        for v in range(nb):
            slab_v = jnp.where(sub == v, row_max[:, v * 128:(v + 1) * 128], slab_v)
            slab_v = jnp.where(sub == nb + v, col_r[:, (nb - 1 - v) * 128:(nb - v) * 128], slab_v)
        slab_v = jnp.where(sub < nb, slab_v, reverse_lanes(slab_v, mirror))
        res[c, t] = slab_v
        for near in (False, True):
            for p in range(n_cols):
                same = ((p // 2) % 2 == half)
                @pl.when(jnp.logical_and(p != c, same == near))
                def _():
                    result_copy(p, c, t).start()
        return carry

    lax.fori_loop(0, n_tiles, body, 0, unroll=True)

    has_next = g + 1 < n_rows
    sub = lax.broadcasted_iota(jnp.int32, (8, 128), 0)
    top = sub < 4

    def gather_blocks(senders, base, acc):
        for sender, t in senders:
            col = sender + n_cols * t
            i = jnp.clip(tiles_ref[0, col] - g * BPR, 0, BPR - 1) - base
            j = i + jnp.clip(tiles_ref[1, col], 0, SPILL - 1)
            slab_v = res[sender, t]
            flipped = pltpu.roll(slab_v, 4, 0)
            for m in range(len(acc)):
                even, odd = 2 * m, 2 * m + 1
                take = jnp.logical_or(jnp.logical_and(top, i == even), jnp.logical_and(jnp.logical_not(top), j == odd))
                take_f = jnp.logical_or(jnp.logical_and(jnp.logical_not(top), i == odd), jnp.logical_and(top, j == even))
                acc[m] = jnp.maximum(acc[m], jnp.maximum(
                    jnp.where(take, slab_v, jnp.float32(-1.0)),
                    jnp.where(take_f, flipped, jnp.float32(-1.0))))
        return acc

    quads = SPILL // 2
    spill_acc = gather_blocks([(c, t) for t in range(n_tiles)], BPR,
                              [jnp.full((8, 128), -1.0, jnp.float32) for _ in range(quads)])
    for m in range(quads):
        spill_out[pl.ds(8 * m, 8), :] = spill_acc[m]

    def spill_up():
        return pltpu.make_async_remote_copy(
            src_ref=spill_out,
            dst_ref=spills.at[c],
            send_sem=s_send.at[0],
            recv_sem=s_recv.at[0],
            device_id=(g + 1, 0),
            device_id_type=MESH,
        )

    @pl.when(has_next)
    def _():
        spill_up().start()


    base = c * SPILL
    acc = [jnp.full((8, 128), -1.0, jnp.float32) for _ in range(quads)]
    for sender in range(n_cols):
        @pl.when(sender != c)
        def _():
            all_results(sender, sender).wait_recv()

        acc = gather_blocks([(sender, t) for t in range(n_tiles)], base, acc)

    @pl.when(down)
    def _():
        pltpu.make_async_remote_copy(
            src_ref=spills,
            dst_ref=spills,
            send_sem=s_send.at[0],
            recv_sem=s_recv.at[0],
            device_id=(g - 1, 0),
            device_id_type=MESH,
        ).wait_recv()

    spilled = jnp.max(spills[...], axis=0)
    for m in range(quads):
        out_ref[pl.ds(8 * m, 8), :] = jnp.maximum(acc[m], spilled[8 * m:8 * m + 8])

    to_mate.wait_send()

    @pl.when(down)
    def _():
        remote(piece_ref, head, 1, (g - 1, 0)).wait_send()
        remote(piece_ref, head, 2, (g - 1, 2)).wait_send()

    for p, live in peers:
        @pl.when(live)
        def _():
            remote(piece_ref, c, 3 + 3 * p, (g, p)).wait_send()
            remote(piece_ref, c, 4 + 3 * p, (g, p)).wait_send()

        @pl.when(jnp.logical_and(live, up))
        def _():
            remote(piece_ref, c, 5 + 3 * p, (g, p)).wait_send()

    for p in range(n_cols):
        @pl.when(p != c)
        def _():
            all_results(p, c).wait_send()

    @pl.when(has_next)
    def _():
        spill_up().wait_send()


def fused_call(tiles, piece, n_rows, n_cols):
    n_tiles = tiles.shape[1] // n_cols
    slots = n_cols + 1
    chunk = piece.shape
    return pl.pallas_call(
        lambda *refs: fused_kernel(n_rows, n_cols, n_tiles, *refs),
        out_shape=jax.ShapeDtypeStruct(chunk, jnp.float32),
        in_specs=[
            pl.BlockSpec(memory_space=pltpu.SMEM),
            pl.BlockSpec(memory_space=pltpu.VMEM),
        ],
        out_specs=pl.BlockSpec(memory_space=pltpu.VMEM),
        scratch_shapes=[
            pltpu.VMEM((slots * chunk[0], 128), jnp.float32),
            pltpu.VMEM((n_cols, n_tiles, 8, 128), jnp.float32),
            pltpu.VMEM(chunk, jnp.float32),
            pltpu.VMEM((n_cols,) + chunk, jnp.float32),
            pltpu.VMEM((B, B), jnp.int32),
            pltpu.VMEM((B, B), jnp.float32),
            pltpu.SemaphoreType.DMA((3 + 3 * n_cols,)),
            pltpu.SemaphoreType.DMA((slots,)),
            pltpu.SemaphoreType.DMA((n_cols,)),
            pltpu.SemaphoreType.DMA((n_cols,)),
            pltpu.SemaphoreType.DMA((1,)),
            pltpu.SemaphoreType.DMA((1,)),
        ],
        cost_estimate=pl.CostEstimate(
            flops=n_tiles * 2 * B * B * M * 3,
            bytes_accessed=slots * chunk[0] * 128 * 4,
            transcendentals=n_tiles * 2 * B,
        ),
        compiler_params=pltpu.CompilerParams(collective_id=0, has_side_effects=True),
    )(tiles, piece)


def on_device(series, tile_list):
    piece = series.shape[0]
    col_count = lax.axis_size("cols")
    n_rows = lax.axis_size("rows")
    result = fused_call(tile_list, series.reshape(piece // 128, 128), n_rows, col_count)
    return jnp.maximum(result, jnp.float32(-1.0)).reshape(piece)


def solution(mesh):
    in_specs = (P(("rows", "cols")), P(None, "rows"))
    out_specs = P(("rows", "cols"))
    return jax.shard_map(
        on_device, mesh=mesh, in_specs=in_specs, out_specs=out_specs, check_vma=False
    )
```

```python
import math

import jax
import jax.numpy as jnp
from jax import lax
from jax.experimental import pallas as pl
from jax.experimental.pallas import tpu as pltpu
from jax.sharding import PartitionSpec as P

M = 256
B = 512
BPR = 128
EXCL = 64
SPILL = 8
SEG = B + M
MESH = pl.DeviceIdType.MESH


def passed_along(block, axis, distance):
    devices = range(lax.axis_size(axis))
    route = [(i - distance, i) for i in devices if i - distance in devices]
    return lax.ppermute(block, axis, route)


def windows(held, b):
    per = B // 128
    seg = jnp.concatenate([held[pl.ds(b * per + v, 1), :] for v in range(SEG // 128)], axis=1)
    parts = []
    for m in range(B // 128):
        lo = 3 * 128 - 128 * m
        sub = jnp.broadcast_to(seg[:, lo:lo + 3 * 128], (128, 3 * 128))
        parts.append(pltpu.roll(sub, 1, 1, stride=1, stride_axis=0)[:, 128:])
    w = jnp.concatenate(parts, axis=0)
    centre = w - jnp.mean(w, axis=1, keepdims=True)
    spread = jnp.mean(centre * centre, axis=1, keepdims=True)
    factor = lax.rsqrt(spread + 1e-05) / math.sqrt(M)
    return centre * factor


def split_dot(a, b):
    a_hi = a.astype(jnp.bfloat16)
    b_hi = b.astype(jnp.bfloat16)
    a_lo = (a - a_hi.astype(jnp.float32)).astype(jnp.bfloat16)
    b_lo = (b - b_hi.astype(jnp.float32)).astype(jnp.bfloat16)
    dims = (((1,), (1,)), ((), ()))

    def dot(x, y):
        return lax.dot_general(x, y, dims, preferred_element_type=jnp.float32)

    return dot(a_hi, b_hi) + (dot(a_hi, b_lo) + dot(a_lo, b_hi))


def reverse_lanes(x, mirror):
    hi = x.astype(jnp.bfloat16)
    rest = x - hi.astype(jnp.float32)
    mid = rest.astype(jnp.bfloat16)
    lo = (rest - mid.astype(jnp.float32)).astype(jnp.bfloat16)

    def dot(part):
        return jnp.dot(part, mirror, preferred_element_type=jnp.float32)

    return (dot(hi) + dot(mid)) + dot(lo)


def greet_partners(n_rows, n_cols, before_wait):
    g = lax.axis_index("rows")
    c = lax.axis_index("cols")
    barrier = pltpu.get_barrier_semaphore()
    half = (c // 2) % 2
    for p in range(n_cols):
        @pl.when(p != c)
        def _():
            pl.semaphore_signal(barrier, 1, device_id=(g, p), device_id_type=MESH)

    has_next = g + 1 < n_rows

    @pl.when(has_next)
    def _():
        pl.semaphore_signal(barrier, 1, device_id=(g + 1, 0), device_id_type=MESH)

    down = jnp.logical_and(c == 0, g > 0)

    @pl.when(down)
    def _():
        for p in range(n_cols):
            pl.semaphore_signal(barrier, 1, device_id=(g - 1, p), device_id_type=MESH)

    collector = jnp.logical_or(c == 0, c == 2)
    up = jnp.logical_and(collector, has_next)
    count = (n_cols - 1) + has_next.astype(jnp.int32) + n_cols * down.astype(jnp.int32)
    before_wait()
    pl.semaphore_wait(barrier, count)
    return g, c, half, collector, up, down


def half_peers(n_cols, c, half):
    return [
        (p, jnp.logical_and(p != c, (p // 2) % 2 == half)) for p in range(n_cols)
    ]


def fused_kernel(n_rows, n_cols, n_tiles, tiles_ref, piece_ref, out_ref,
                 held, res, spill_out, spills, diff_ref, flip_ref,
                 g_send, g_recv, r_send, r_recv, s_send, s_recv):
    spills[...] = jnp.full(spills.shape, -1.0, jnp.float32)

    def tables():
        r_i = lax.broadcasted_iota(jnp.int32, (B, B), 0)
        r_j = lax.broadcasted_iota(jnp.int32, (B, B), 1)
        diff_ref[...] = r_i - r_j
        flip_ref[...] = jnp.where(r_i + r_j == B - 1, 1.0, 0.0)

    g, c, half, collector, up, down = greet_partners(n_rows, n_cols, tables)
    mate = c ^ 2
    head = n_cols
    rows = SPILL * B // 128
    peers = half_peers(n_cols, c, half)

    def slab(ref, k):
        if isinstance(k, int):
            return ref.at[pl.ds(k * rows, rows)]
        return ref.at[pl.ds(pl.multiple_of(k * rows, rows), rows)]

    def remote(src, slot, sem, device):
        return pltpu.make_async_remote_copy(
            src_ref=src,
            dst_ref=slab(held, slot),
            send_sem=g_send.at[sem],
            recv_sem=g_recv.at[slot],
            device_id=device,
            device_id_type=MESH,
        )

    @pl.when(down)
    def _():
        remote(piece_ref, head, 2, (g - 1, 2)).start()
        remote(piece_ref, head, 1, (g - 1, 0)).start()

    to_mate = remote(piece_ref, c, 0, (g, mate))
    to_mate.start()

    for p, live in peers:
        @pl.when(live)
        def _():
            remote(piece_ref, c, 3 + 3 * p, (g, p)).start()

    @pl.when(g + 1 == n_rows)
    def _():
        held[pl.ds(head * rows, rows), :] = jnp.zeros(piece_ref.shape, jnp.float32)

    remote(piece_ref, mate, 0, (g, mate)).wait_recv()

    for p, live in peers:
        @pl.when(live)
        def _():
            remote(slab(held, mate), mate, 4 + 3 * p, (g, p)).start()

    @pl.when(up)
    def _():
        remote(piece_ref, head, 1, (g + 1, 0)).wait_recv()

    for p, live in peers:
        @pl.when(jnp.logical_and(live, up))
        def _():
            remote(slab(held, head), head, 5 + 3 * p, (g, p)).start()

    held[pl.ds(pl.multiple_of(c * rows, rows), rows), :] = piece_ref[...]

    for p, live in peers:
        @pl.when(live)
        def _():
            remote(piece_ref, p, 3 + 3 * p, (g, p)).wait_recv()
            remote(piece_ref, p ^ 2, 3 + 3 * p, (g, p)).wait_recv()

    @pl.when(jnp.logical_and(jnp.logical_not(collector), g + 1 < n_rows))
    def _():
        remote(piece_ref, head, 1, (g, 0)).wait_recv()

    def result_copy(p, sender, t):
        return pltpu.make_async_remote_copy(
            src_ref=res.at[sender, t],
            dst_ref=res.at[sender, t],
            send_sem=r_send.at[p],
            recv_sem=r_recv.at[sender],
            device_id=(g, p),
            device_id_type=MESH,
        )

    def all_results(p, sender):
        return pltpu.make_async_remote_copy(
            src_ref=res.at[sender],
            dst_ref=res.at[sender],
            send_sem=r_send.at[p],
            recv_sem=r_recv.at[sender],
            device_id=(g, p),
            device_id_type=MESH,
        )

    m_i = lax.broadcasted_iota(jnp.int32, (128, 128), 0)
    m_j = lax.broadcasted_iota(jnp.int32, (128, 128), 1)
    mirror = jnp.where(m_i + m_j == 127, 1.0, 0.0).astype(jnp.bfloat16)

    def body(t, carry):
        col = c + n_cols * t
        i = jnp.clip(tiles_ref[0, col] - g * BPR, 0, BPR - 1)
        d = jnp.clip(tiles_ref[1, col], 0, SPILL - 1)
        j = i + d
        zl = windows(held, i)
        zr = windows(held, j)
        corr = split_dot(zl, zr)
        corr = jnp.where(diff_ref[...] >= EXCL - d * B, corr, jnp.float32(-1.0))
        row_c = jnp.max(corr, axis=1, keepdims=True)
        row_max = jnp.sum(row_c * flip_ref[...], axis=0, keepdims=True)
        col_r = jnp.max(corr, axis=0, keepdims=True)
        sub = lax.broadcasted_iota(jnp.int32, (8, 128), 0)
        slab_v = jnp.full((8, 128), -1.0, jnp.float32)
        nb = B // 128
        for v in range(nb):
            slab_v = jnp.where(sub == v, row_max[:, v * 128:(v + 1) * 128], slab_v)
            slab_v = jnp.where(sub == nb + v, col_r[:, (nb - 1 - v) * 128:(nb - v) * 128], slab_v)
        slab_v = jnp.where(sub < nb, slab_v, reverse_lanes(slab_v, mirror))
        res[c, t] = slab_v
        for near in (False, True):
            for p in range(n_cols):
                same = ((p // 2) % 2 == half)
                @pl.when(jnp.logical_and(p != c, same == near))
                def _():
                    result_copy(p, c, t).start()
        return carry

    lax.fori_loop(0, n_tiles, body, 0, unroll=True)

    has_next = g + 1 < n_rows
    sub = lax.broadcasted_iota(jnp.int32, (8, 128), 0)
    top = sub < 4

    def gather_blocks(senders, base, acc):
        for sender, t in senders:
            col = sender + n_cols * t
            i = jnp.clip(tiles_ref[0, col] - g * BPR, 0, BPR - 1) - base
            j = i + jnp.clip(tiles_ref[1, col], 0, SPILL - 1)
            slab_v = res[sender, t]
            flipped = pltpu.roll(slab_v, 4, 0)
            for m in range(len(acc)):
                even, odd = 2 * m, 2 * m + 1
                take = jnp.logical_or(jnp.logical_and(top, i == even), jnp.logical_and(jnp.logical_not(top), j == odd))
                take_f = jnp.logical_or(jnp.logical_and(jnp.logical_not(top), i == odd), jnp.logical_and(top, j == even))
                acc[m] = jnp.maximum(acc[m], jnp.maximum(
                    jnp.where(take, slab_v, jnp.float32(-1.0)),
                    jnp.where(take_f, flipped, jnp.float32(-1.0))))
        return acc

    quads = SPILL // 2
    spill_acc = gather_blocks([(c, t) for t in range(n_tiles)], BPR,
                              [jnp.full((8, 128), -1.0, jnp.float32) for _ in range(quads)])
    for m in range(quads):
        spill_out[pl.ds(8 * m, 8), :] = spill_acc[m]

    def spill_up():
        return pltpu.make_async_remote_copy(
            src_ref=spill_out,
            dst_ref=spills.at[c],
            send_sem=s_send.at[0],
            recv_sem=s_recv.at[0],
            device_id=(g + 1, 0),
            device_id_type=MESH,
        )

    @pl.when(has_next)
    def _():
        spill_up().start()


    base = c * SPILL
    acc = [jnp.full((8, 128), -1.0, jnp.float32) for _ in range(quads)]
    for side in (half, 1 - half):
        for k in range(n_cols // 2):
            sender = 4 * (k // 2) + 2 * side + (k % 2)

            @pl.when(sender != c)
            def _():
                all_results(sender, sender).wait_recv()

            acc = gather_blocks([(sender, t) for t in range(n_tiles)], base, acc)

    @pl.when(down)
    def _():
        pltpu.make_async_remote_copy(
            src_ref=spills,
            dst_ref=spills,
            send_sem=s_send.at[0],
            recv_sem=s_recv.at[0],
            device_id=(g - 1, 0),
            device_id_type=MESH,
        ).wait_recv()

    spilled = jnp.max(spills[...], axis=0)
    for m in range(quads):
        out_ref[pl.ds(8 * m, 8), :] = jnp.maximum(acc[m], spilled[8 * m:8 * m + 8])

    to_mate.wait_send()

    @pl.when(down)
    def _():
        remote(piece_ref, head, 1, (g - 1, 0)).wait_send()
        remote(piece_ref, head, 2, (g - 1, 2)).wait_send()

    for p, live in peers:
        @pl.when(live)
        def _():
            remote(piece_ref, c, 3 + 3 * p, (g, p)).wait_send()
            remote(piece_ref, c, 4 + 3 * p, (g, p)).wait_send()

        @pl.when(jnp.logical_and(live, up))
        def _():
            remote(piece_ref, c, 5 + 3 * p, (g, p)).wait_send()

    for p in range(n_cols):
        @pl.when(p != c)
        def _():
            all_results(p, c).wait_send()

    @pl.when(has_next)
    def _():
        spill_up().wait_send()


def fused_call(tiles, piece, n_rows, n_cols):
    n_tiles = tiles.shape[1] // n_cols
    slots = n_cols + 1
    chunk = piece.shape
    return pl.pallas_call(
        lambda *refs: fused_kernel(n_rows, n_cols, n_tiles, *refs),
        out_shape=jax.ShapeDtypeStruct(chunk, jnp.float32),
        in_specs=[
            pl.BlockSpec(memory_space=pltpu.SMEM),
            pl.BlockSpec(memory_space=pltpu.VMEM),
        ],
        out_specs=pl.BlockSpec(memory_space=pltpu.VMEM),
        scratch_shapes=[
            pltpu.VMEM((slots * chunk[0], 128), jnp.float32),
            pltpu.VMEM((n_cols, n_tiles, 8, 128), jnp.float32),
            pltpu.VMEM(chunk, jnp.float32),
            pltpu.VMEM((n_cols,) + chunk, jnp.float32),
            pltpu.VMEM((B, B), jnp.int32),
            pltpu.VMEM((B, B), jnp.float32),
            pltpu.SemaphoreType.DMA((3 + 3 * n_cols,)),
            pltpu.SemaphoreType.DMA((slots,)),
            pltpu.SemaphoreType.DMA((n_cols,)),
            pltpu.SemaphoreType.DMA((n_cols,)),
            pltpu.SemaphoreType.DMA((1,)),
            pltpu.SemaphoreType.DMA((1,)),
        ],
        cost_estimate=pl.CostEstimate(
            flops=n_tiles * 2 * B * B * M * 3,
            bytes_accessed=slots * chunk[0] * 128 * 4,
            transcendentals=n_tiles * 2 * B,
        ),
        compiler_params=pltpu.CompilerParams(collective_id=0, has_side_effects=True),
    )(tiles, piece)


def on_device(series, tile_list):
    piece = series.shape[0]
    col_count = lax.axis_size("cols")
    n_rows = lax.axis_size("rows")
    result = fused_call(tile_list, series.reshape(piece // 128, 128), n_rows, col_count)
    return jnp.maximum(result, jnp.float32(-1.0)).reshape(piece)


def solution(mesh):
    in_specs = (P(("rows", "cols")), P(None, "rows"))
    out_specs = P(("rows", "cols"))
    return jax.shard_map(
        on_device, mesh=mesh, in_specs=in_specs, out_specs=out_specs, check_vma=False
    )
```
